128 devices in a mesh: dp: 8 (over z, y_lo), seq: 16 (over x, y_hi, core).
Axes of the slice: x: 4, y: 4 (y_hi: 2, y_lo: 2; y = y_hi * 2 + y_lo), z: 4, core: 2. Of those that a mesh axis runs over, the one named last changes fastest.
Arguments:
- tokens: bfloat16 [8, 12288, 1024], P('dp', 'seq'), may hold values from -6 to 6
- image_tokens: bfloat16 [8, 2048, 768], P('dp', 'seq'), may hold values from -51 to 51
- norm_gain: float32 [1024], replicated, may hold values from 0.1 to 1.9
- w_query: bfloat16 [1024, 1024], replicated, may hold values from -0.1875 to 0.1875
- w_key: bfloat16 [768, 1024], replicated, may hold values from -0.21875 to 0.21875
- w_value: bfloat16 [768, 1024], replicated, may hold values from -0.21875 to 0.21875
- w_out: bfloat16 [1024, 1024], replicated, may hold values from -0.1875 to 0.1875
- w_plane: bfloat16 [1024, 80], replicated, may hold values from -0.1875 to 0.1875
- dec_w1: bfloat16 [64, 80], replicated, may hold values from -0.625 to 0.625
- dec_b1: float32 [64], replicated, may hold values from -3 to 3
- dec_w2: bfloat16 [64, 64], replicated, may hold values from -0.75 to 0.75
- dec_b2: float32 [64], replicated, may hold values from -3 to 3
- dec_w3: bfloat16 [4, 64], replicated, may hold values from -0.75 to 0.75
- dec_b3: float32 [4], replicated, may hold values from -3 to 3
- corner_idx: int32 [8, 12, 65536], P('dp', None, 'seq'), may hold values from 0 to 12287, as said below
- corner_wts: bfloat16 [8, 12, 65536], P('dp', None, 'seq'), may hold values from 0 to 1, as said below
- target_color: float32 [8, 3, 512], P('dp', None, 'seq'), may hold values from 0 to 1
Outputs:
- colors: float32 [8, 3, 512], P('dp', None, 'seq')
- token_grad: bfloat16 [8, 12288, 1024], P('dp', 'seq')
- plane_weight_grad: float32 [1024, 80], replicated
The draws below stay inside these ranges and needn't reach their ends.
Inputs may be any that keep to these rules, and one draw needn't show every extreme that they name: `corner_idx`: each entry names a triplane token of the scene; for each sample and plane the four entries are the corners of one grid cell of that plane, and consecutive samples of a ray walk through neighbouring cells. `corner_wts`: for each sample and plane the four weights are the bilinear weights of one point in that cell.
All inputs are finite; a program needn't handle non-finite values.
Results may differ from the reference program's by a relative error of at most 0.017.
Values may be sent and summed in bfloat16 or wider, within the bound.
A program may use at most 128 MiB of HBM per device.

```python
import math
import jax
import jax.numpy as jnp
from jax import lax

D = 1024
HEADS = 16
C = 768
GRID = 64
CP = 80
HID = 64
STEPS = 128
SCENES = 8
TOK = 12288
NIMG = 2048
RAYS = 512


def sample_table(key):
    subkeys = jax.random.split(jax.random.fold_in(key, 11), 3)
    anchor = jax.random.randint(subkeys[0], (SCENES, RAYS, 1, 3), 0, GRID - 1)
    heading = jax.random.randint(subkeys[1], (SCENES, RAYS, 1, 3), -2, 3)
    step_ids = jnp.arange(STEPS, dtype=jnp.int32)[None, None, :, None]
    cell_ids = jnp.clip(anchor + step_ids * heading // 4, 0, GRID - 2)
    fraction = jax.random.uniform(subkeys[2], (SCENES, RAYS, STEPS, 3), jnp.float32)
    plane_axes = ((0, 1), (0, 2), (1, 2))
    index_list = []
    weight_list = []
    for plane_id in range(3):
        first_axis, second_axis = plane_axes[plane_id]
        for shift_b in (0, 1):
            for shift_a in (0, 1):
                flat_id = plane_id * GRID * GRID + (cell_ids[..., second_axis] + shift_b) * GRID + cell_ids[..., first_axis] + shift_a
                weight_a = fraction[..., first_axis] if shift_a else 1.0 - fraction[..., first_axis]
                weight_b = fraction[..., second_axis] if shift_b else 1.0 - fraction[..., second_axis]
                index_list.append(flat_id.reshape(SCENES, RAYS * STEPS))
                weight_list.append((weight_a * weight_b).reshape(SCENES, RAYS * STEPS))
    return (jnp.stack(index_list, axis=1).astype(jnp.int32), jnp.stack(weight_list, axis=1))


def draw_corner_idx(key, part):
    return sample_table(key)[0]


def draw_corner_wts(key, part):
    return sample_table(key)[1].astype(jnp.bfloat16)


def draw_image_tokens(key, part):
    subkeys = jax.random.split(jax.random.fold_in(key, 5), 1)
    base = jnp.clip(jax.random.normal(subkeys[0], (SCENES, NIMG, C), jnp.float32), -6.0, 6.0)
    return base.astype(jnp.bfloat16)


def steps_of(rng, extent, pieces, low, largest):
    loudness, own = 1.0, jax.random.fold_in(rng, 6)
    for dim, blocks in pieces:
        draws = jnp.exp(jax.random.uniform(jax.random.fold_in(own, dim), (blocks,), jnp.float32, low / len(pieces), largest / len(pieces)))
        loudness = loudness * jnp.repeat(draws, extent[dim] // blocks).reshape([-1 if axis == dim else 1 for axis in range(len(extent))])
    return loudness


def bell_draw(stream_key, shape, width, most, shards=(), kind=jnp.bfloat16):
    drawn = jax.random.normal(stream_key, shape, jnp.float32) * width
    if len(shards) > 0:
        drawn = steps_of(stream_key, shape, shards, -0.22, 0.18) * drawn
    return jnp.clip(drawn, min=-most, max=most).astype(kind)


def setup_inputs(seed: int = 0) -> dict:
    streams_of = jax.random.split(jax.random.key(seed), 18)
    tokens = bell_draw(streams_of[0], (SCENES, TOK, D), 1.0, 6.0, ((0, 8), (1, 16)))
    image_tokens = draw_image_tokens(jax.random.fold_in(streams_of[17], 71), 0)
    norm_gain = jnp.clip(1.0 + 0.18 * jax.random.normal(streams_of[2], (D,), jnp.float32), 0.1, 1.9)
    w_query = bell_draw(streams_of[3], (D, D), D ** -0.5, 0.1875)
    w_key = bell_draw(streams_of[4], (C, D), C ** -0.5, 0.21875)
    w_value = bell_draw(streams_of[5], (C, D), C ** -0.5, 0.21875)
    w_out = bell_draw(streams_of[6], (D, D), D ** -0.5, 0.1875)
    w_plane = bell_draw(streams_of[7], (D, CP), D ** -0.5, 0.1875)
    dec_w1 = bell_draw(streams_of[8], (HID, CP), CP ** -0.5, 0.625)
    dec_b1 = bell_draw(streams_of[9], (HID,), 0.5, 3.0, (), jnp.float32)
    dec_w2 = bell_draw(streams_of[10], (HID, HID), HID ** -0.5, 0.75)
    dec_b2 = bell_draw(streams_of[11], (HID,), 0.5, 3.0, (), jnp.float32)
    dec_w3 = bell_draw(streams_of[12], (4, HID), HID ** -0.5, 0.75)
    dec_b3 = bell_draw(streams_of[13], (4,), 0.5, 3.0, (), jnp.float32)
    corner_idx = draw_corner_idx(jax.random.fold_in(streams_of[17], 71), 0)
    corner_wts = draw_corner_wts(jax.random.fold_in(streams_of[17], 71), 0)
    target_color = jnp.clip(1.0 * jax.random.uniform(streams_of[16], (SCENES, 3, RAYS), jnp.float32) ** steps_of(streams_of[16], (SCENES, 3, RAYS), ((0, 8), (2, 16)), -0.2, 0.2), 0.0, 1.0)
    return {"tokens": tokens, "image_tokens": image_tokens, "norm_gain": norm_gain, "w_query": w_query, "w_key": w_key, "w_value": w_value, "w_out": w_out, "w_plane": w_plane, "dec_w1": dec_w1, "dec_b1": dec_b1, "dec_w2": dec_w2, "dec_b2": dec_b2, "dec_w3": dec_w3, "dec_b3": dec_b3, "corner_idx": corner_idx, "corner_wts": corner_wts, "target_color": target_color}


NORM_EPS = 1e-05
DEPTH_STEP = 0.02

def plain_norm(inputs):
    row_mean = lax.optimization_barrier(jnp.mean(inputs, axis=-1, keepdims=True))
    centred = inputs - row_mean
    row_var = lax.optimization_barrier(jnp.mean(centred * centred, axis=-1, keepdims=True))
    return centred * lax.rsqrt(row_var + NORM_EPS)

def render(features, dec_w1, dec_b1, dec_w2, dec_b2, dec_w3, dec_b3):
    hidden = jax.nn.silu(jnp.dot(dec_w1, features, preferred_element_type=jnp.float32) + dec_b1[:, None]).astype(jnp.bfloat16)
    hidden = jax.nn.silu(jnp.dot(dec_w2, hidden, preferred_element_type=jnp.float32) + dec_b2[:, None]).astype(jnp.bfloat16)
    decoded = jnp.dot(dec_w3, hidden, preferred_element_type=jnp.float32) + dec_b3[:, None]
    optical = jax.nn.softplus(decoded[0]).reshape(-1, STEPS) * DEPTH_STEP
    albedo = jax.nn.sigmoid(decoded[1:4]).reshape(3, -1, STEPS)
    before = jnp.cumsum(optical, axis=1) - optical
    weight = jnp.exp(-before) * (1.0 - jnp.exp(-optical))
    return lax.optimization_barrier(jnp.sum(weight[None] * albedo, axis=2))

def reference(tokens, image_tokens, norm_gain, w_query, w_key, w_value, w_out, w_plane, dec_w1, dec_b1, dec_w2, dec_b2, dec_w3, dec_b3, corner_idx, corner_wts, target_color):
    head_dim = D // HEADS
    score_scale = 1.0 / math.sqrt(head_dim)

    def scene(parts):
        own_tokens, images, index_table, weight_table, target = parts
        normed = plain_norm(own_tokens.astype(jnp.float32)).astype(jnp.bfloat16)
        queries = jnp.dot(normed, w_query, preferred_element_type=jnp.float32).astype(jnp.bfloat16)
        key_rows = jnp.dot(images, w_key, preferred_element_type=jnp.float32).astype(jnp.bfloat16)
        values = jnp.dot(images, w_value, preferred_element_type=jnp.float32).astype(jnp.bfloat16)
        query_heads = queries.reshape(TOK, HEADS, head_dim).transpose(1, 0, 2)
        key_heads = key_rows.reshape(NIMG, HEADS, head_dim).transpose(1, 0, 2)
        value_heads = values.reshape(NIMG, HEADS, head_dim).transpose(1, 0, 2)

        def one_head(head_parts):
            query_one, key_one, value_one = head_parts
            scores = jnp.dot(query_one, key_one.T, preferred_element_type=jnp.float32) * score_scale
            row_max = lax.optimization_barrier(jnp.max(scores, axis=1, keepdims=True))
            exp_terms = jnp.exp(scores - row_max)
            prob_sum = lax.optimization_barrier(jnp.sum(exp_terms, axis=1, keepdims=True))
            return jnp.dot(exp_terms.astype(jnp.bfloat16), value_one, preferred_element_type=jnp.float32) / prob_sum
        head_out = lax.map(one_head, (query_heads, key_heads, value_heads))
        attended = head_out.transpose(1, 0, 2).reshape(TOK, D).astype(jnp.bfloat16)
        mixed = (own_tokens.astype(jnp.float32) + jnp.dot(attended, w_out, preferred_element_type=jnp.float32)).astype(jnp.bfloat16)
        plane_in = (plain_norm(mixed.astype(jnp.float32)) * norm_gain).astype(jnp.bfloat16)
        planes = jnp.dot(w_plane.T, plane_in.T, preferred_element_type=jnp.float32).astype(jnp.bfloat16)
        picked = planes[:, index_table].astype(jnp.float32)
        features = lax.optimization_barrier(jnp.sum(picked * weight_table.astype(jnp.float32)[None], axis=1)).astype(jnp.bfloat16)

        def shade_rays(feature_in):
            return render(feature_in, dec_w1, dec_b1, dec_w2, dec_b2, dec_w3, dec_b3)
        colors, pullback = jax.vjp(shade_rays, features)
        feat_grad = pullback(colors - target)[0].astype(jnp.bfloat16)
        grad_terms = (feat_grad.astype(jnp.float32)[:, None, :] * weight_table.astype(jnp.float32)[None]).reshape(CP, -1)
        plane_grad = jnp.zeros((CP, TOK), jnp.float32).at[:, index_table.reshape(-1)].add(grad_terms)
        plane_grad = plane_grad.astype(jnp.bfloat16)
        weight_grad = jnp.dot(plane_in.T, plane_grad.T, preferred_element_type=jnp.float32)
        token_grad = jnp.dot(plane_grad.T, w_plane.T, preferred_element_type=jnp.float32).astype(jnp.bfloat16)
        return (colors, token_grad, weight_grad)
    colors, token_grad, weight_grad = lax.map(scene, (tokens, image_tokens, corner_idx, corner_wts, target_color))
    return (colors, token_grad, lax.optimization_barrier(jnp.sum(weight_grad, axis=0)))
```

```python
import functools
import math

import jax
import jax.numpy as jnp
from jax import lax
from jax.experimental import pallas as pl
from jax.experimental.pallas import tpu as pltpu
from jax.sharding import PartitionSpec as P

HEADS = 16
STEPS = 128
PLANES = 3
LANES = 128
NORM_EPS = 1e-05
DEPTH_STEP = 0.02
VMEM_BYTES = 60000 * 1024

bf16 = jnp.bfloat16
f32 = jnp.float32


def in_vmem(count):
    return [pl.BlockSpec(memory_space=pltpu.VMEM)] * count


def plain_norm(inputs):
    row_mean = jnp.mean(inputs, axis=-1, keepdims=True)
    centred = inputs - row_mean
    row_var = jnp.mean(centred * centred, axis=-1, keepdims=True)
    return centred * lax.rsqrt(row_var + NORM_EPS)


def attention_kernel(q_ref, k_ref, v_ref, out_ref, values_ref, *, tile):
    rows, width = q_ref.shape
    low = lax.broadcasted_iota(jnp.int32, (1, LANES), 1) < LANES // 2

    def pair(pair_id, carry):
        first = pl.multiple_of(pair_id * LANES, LANES)
        values = v_ref[:, pl.ds(first, LANES)]
        one = jnp.ones((), bf16)
        values_ref[0] = jnp.where(low, values, one)
        values_ref[1] = jnp.where(low, one, values)

        def block(block_id, inner):
            start = pl.multiple_of(block_id * tile, tile)
            queries = q_ref[pl.ds(start, tile), pl.ds(first, LANES)]
            parts = []
            for head in range(2):
                own = jnp.where(low if head == 0 else ~low, queries, jnp.zeros((), bf16))
                scores = jnp.dot(
                    own, k_ref[pl.ds(first, LANES), :], preferred_element_type=f32
                )
                row_max = jnp.max(scores, axis=1, keepdims=True)
                terms = jnp.exp2(scores - row_max).astype(bf16)
                parts.append(jnp.dot(terms, values_ref[head], preferred_element_type=f32))
            weighted = jnp.where(low, parts[0], parts[1])
            row_sum = pltpu.roll(jnp.where(low, parts[1], parts[0]), LANES // 2, 1)
            out_ref[pl.ds(start, tile), pl.ds(first, LANES)] = (weighted / row_sum).astype(bf16)
            return inner

        lax.fori_loop(0, rows // tile, block, 0)
        return carry

    lax.fori_loop(0, width // LANES, pair, 0)


def attention(queries, keys, values):
    rows, width = queries.shape
    count = values.shape[0]
    return pl.pallas_call(
        functools.partial(attention_kernel, tile=256),
        out_shape=jax.ShapeDtypeStruct((rows, width), bf16),
        in_specs=in_vmem(3),
        out_specs=pl.BlockSpec(memory_space=pltpu.VMEM),
        scratch_shapes=[pltpu.VMEM((2, count, LANES), bf16)],
        compiler_params=pltpu.CompilerParams(vmem_limit_bytes=VMEM_BYTES),
        cost_estimate=pl.CostEstimate(
            flops=4 * rows * count * width,
            bytes_accessed=4 * (rows + count) * width,
            transcendentals=rows * count * HEADS,
        ),
        name="attention",
    )(queries, keys, values)


def table_rows(col_ref, row_ref, plane, first_row, row_count, start, width, side):
    span = pl.ds(start, width)
    pieces = side // 16
    upper = col_ref[2 * plane, :, span].reshape(pieces, 16, width)
    lower = col_ref[2 * plane + 1, :, span].reshape(pieces, 16, width)
    cell_row = row_ref[plane, :, span]
    zero = jnp.zeros((16, width), bf16)
    row_id = jnp.asarray(first_row, jnp.int32)
    before = cell_row == (row_id - 1).astype(bf16)
    blocks = []
    for step in range(row_count):
        here = cell_row == (row_id + step).astype(bf16)
        for piece in range(pieces):
            blocks.append(
                jnp.where(here, upper[piece], jnp.where(before, lower[piece], zero))
            )
        before = here
    return jnp.concatenate(blocks, axis=0)


def ray_scan(values, lane, reverse):
    width = values.shape[1]
    shift = 1
    while shift < STEPS:
        if reverse:
            moved = pltpu.roll(values, width - shift, 1)
            values = values + jnp.where(lane < STEPS - shift, moved, 0.0)
        else:
            moved = pltpu.roll(values, shift, 1)
            values = values + jnp.where(lane >= shift, moved, 0.0)
        shift *= 2
    return values


def render_kernel(
    idx_ref,
    wts_ref,
    planes_ref,
    target_ref,
    w1_ref,
    b1_ref,
    w2_ref,
    b2_ref,
    w3_ref,
    b3_ref,
    colors_ref,
    grad_ref,
    col_ref,
    row_ref,
    fgrad_ref,
    *,
    side,
    prep_width,
    width,
    grad_rows,
):
    samples = idx_ref.shape[1]
    channels, tokens = planes_ref.shape
    plane_size = side * side

    def prepare(step, carry):
        start = pl.multiple_of(step * prep_width, prep_width)
        span = pl.ds(start, prep_width)
        index = idx_ref[:, span]
        weight = wts_ref[:, span].astype(f32)
        column_id = lax.broadcasted_iota(jnp.int32, (side, prep_width), 0)
        for plane in range(PLANES):
            in_plane = (index >= plane * plane_size) & (index < (plane + 1) * plane_size)
            base = jnp.min(jnp.where(in_plane, index, tokens), axis=0, keepdims=True)
            corner = []
            for offset in (0, 1, side, side + 1):
                corner.append(
                    jnp.sum(
                        jnp.where(index == base + offset, weight, 0.0), axis=0, keepdims=True
                    )
                )
            local = base - plane * plane_size
            cell_row = local // side
            column = local - cell_row * side
            for which in range(2):
                col_ref[2 * plane + which, :, span] = jnp.where(
                    column_id == column,
                    corner[2 * which],
                    jnp.where(column_id == column + 1, corner[2 * which + 1], 0.0),
                ).astype(bf16)
            row_ref[plane, :, span] = jnp.broadcast_to(
                cell_row.astype(f32), (16, prep_width)
            ).astype(bf16)
        return carry

    lax.fori_loop(0, samples // prep_width, prepare, 0)

    rays = width // STEPS
    all_rays = samples // STEPS
    w1, w2, w3 = w1_ref[...], w2_ref[...], w3_ref[...]
    b1, b2, b3 = b1_ref[...], b2_ref[...], b3_ref[...]
    lane = lax.broadcasted_iota(jnp.int32, (1, width), 1) % STEPS
    exact = lax.Precision.HIGHEST
    flip = (((0,), (0,)), ((), ()))

    def shade(step, carry):
        start = pl.multiple_of(step * width, width)

        def add_plane(plane, total):
            table = table_rows(col_ref, row_ref, plane, 0, side, start, width, side)
            block = planes_ref[:, pl.ds(pl.multiple_of(plane * plane_size, LANES), plane_size)]
            return total + jnp.dot(block, table, preferred_element_type=f32)

        features = lax.fori_loop(
            0, PLANES, add_plane, jnp.zeros((channels, width), f32)
        ).astype(bf16)

        z1 = jnp.dot(w1, features, preferred_element_type=f32) + b1
        s1 = jax.nn.sigmoid(z1)
        h1 = (z1 * s1).astype(bf16)
        z2 = jnp.dot(w2, h1, preferred_element_type=f32) + b2
        s2 = jax.nn.sigmoid(z2)
        h2 = (z2 * s2).astype(bf16)
        decoded = jnp.dot(w3, h2, preferred_element_type=f32) + b3
        density = decoded[0:1]
        optical = (
            jnp.maximum(density, 0.0) + jnp.log1p(jnp.exp(-jnp.abs(density)))
        ) * DEPTH_STEP
        albedo = jax.nn.sigmoid(decoded[1:4])
        before = ray_scan(optical, lane, False) - optical
        reach = jnp.exp(-before)
        passed = jnp.exp(-optical)
        weight = reach * (1.0 - passed)

        ray_id = lax.broadcasted_iota(jnp.int32, (all_rays, width), 0)
        ray_of = (
            step * rays + lax.broadcasted_iota(jnp.int32, (all_rays, width), 1) // STEPS
        )
        spread = (ray_id == ray_of).astype(f32)
        seen = lax.dot_general(
            weight * albedo,
            spread,
            (((1,), (1,)), ((), ())),
            precision=exact,
            preferred_element_type=f32,
        )
        mine = (
            lax.broadcasted_iota(jnp.int32, (3, all_rays), 1) // rays == step
        )
        colors_ref[...] = jnp.where(mine, seen, colors_ref[...])
        miss = jnp.dot(
            jnp.where(mine, seen - target_ref[...], 0.0),
            spread,
            precision=exact,
            preferred_element_type=f32,
        )
        weight_grad = jnp.sum(miss * albedo, axis=0, keepdims=True)
        term = weight_grad * weight
        later = ray_scan(term, lane, True) - term
        optical_grad = weight_grad * reach * passed - later
        density_grad = optical_grad * (DEPTH_STEP * jax.nn.sigmoid(density))
        albedo_grad = miss * weight * albedo * (1.0 - albedo)
        decoded_grad = jnp.concatenate([density_grad, albedo_grad], axis=0).astype(bf16)
        g2 = lax.dot_general(w3, decoded_grad, flip, preferred_element_type=f32)
        g2 = g2.astype(bf16).astype(f32) * (s2 * (1.0 + z2 * (1.0 - s2)))
        g1 = lax.dot_general(w2, g2.astype(bf16), flip, preferred_element_type=f32)
        g1 = g1.astype(bf16).astype(f32) * (s1 * (1.0 + z1 * (1.0 - s1)))
        fgrad_ref[:, pl.ds(start, width)] = lax.dot_general(
            w1, g1.astype(bf16), flip, preferred_element_type=f32
        ).astype(bf16)
        return carry

    colors_ref[...] = jnp.zeros_like(colors_ref)
    lax.fori_loop(0, samples // width, shade, 0)

    block_size = grad_rows * side
    blocks = side // grad_rows

    def spread_back(step, carry):
        plane = step // blocks
        first_row = (step - plane * blocks) * grad_rows
        table = table_rows(col_ref, row_ref, plane, first_row, grad_rows, 0, samples, side)
        grad_ref[:, pl.ds(pl.multiple_of(step * block_size, block_size), block_size)] = (
            lax.dot_general(
                fgrad_ref[...], table, (((1,), (1,)), ((), ())), preferred_element_type=f32
            ).astype(bf16)
        )
        return carry

    lax.fori_loop(0, PLANES * blocks, spread_back, 0)


def render_and_grad(index, weight, planes, target, w1, b1, w2, b2, w3, b3):
    channels, tokens = planes.shape
    samples = index.shape[1]
    side = math.isqrt(tokens // PLANES)
    return pl.pallas_call(
        functools.partial(
            render_kernel,
            side=side,
            prep_width=min(1024, samples),
            width=min(512, samples),
            grad_rows=16,
        ),
        out_shape=(
            jax.ShapeDtypeStruct(target.shape, f32),
            jax.ShapeDtypeStruct((channels, tokens), bf16),
        ),
        in_specs=in_vmem(10),
        out_specs=tuple(in_vmem(2)),
        scratch_shapes=[
            pltpu.VMEM((2 * PLANES, side, samples), bf16),
            pltpu.VMEM((PLANES, 16, samples), bf16),
            pltpu.VMEM((channels, samples), bf16),
        ],
        compiler_params=pltpu.CompilerParams(vmem_limit_bytes=VMEM_BYTES),
        cost_estimate=pl.CostEstimate(
            flops=4 * channels * tokens * samples,
            bytes_accessed=4 * channels * tokens,
            transcendentals=400 * samples,
        ),
        name="render",
    )(
        index,
        weight,
        planes,
        target,
        w1,
        b1[:, None],
        w2,
        b2[:, None],
        w3,
        b3[:, None],
    )


def body(
    tokens,
    image_tokens,
    norm_gain,
    w_query,
    w_key,
    w_value,
    w_out,
    w_plane,
    dec_w1,
    dec_b1,
    dec_w2,
    dec_b2,
    dec_w3,
    dec_b3,
    corner_idx,
    corner_wts,
    target_color,
):
    own_tokens = tokens[0]
    model_width = own_tokens.shape[1]
    head_dim = model_width // HEADS
    images = lax.all_gather(image_tokens[0], "seq", axis=0, tiled=True)
    normed = plain_norm(own_tokens.astype(f32)).astype(bf16)
    score_scale = math.log2(math.e) / math.sqrt(head_dim)
    queries = (jnp.dot(normed, w_query, preferred_element_type=f32) * score_scale).astype(bf16)
    keys = lax.dot_general(
        w_key, images, (((0,), (1,)), ((), ())), preferred_element_type=f32
    ).astype(bf16)
    values = jnp.dot(images, w_value, preferred_element_type=f32).astype(bf16)
    attended = attention(queries, keys, values)
    mixed = (
        own_tokens.astype(f32) + jnp.dot(attended, w_out, preferred_element_type=f32)
    ).astype(bf16)
    plane_in = (plain_norm(mixed.astype(f32)) * norm_gain).astype(bf16)
    planes = lax.dot_general(
        w_plane, plane_in, (((0,), (1,)), ((), ())), preferred_element_type=f32
    ).astype(bf16)
    planes = lax.all_gather(planes, "seq", axis=1, tiled=True)
    colors, grad = render_and_grad(
        corner_idx[0],
        corner_wts[0],
        planes,
        target_color[0],
        dec_w1,
        dec_b1,
        dec_w2,
        dec_b2,
        dec_w3,
        dec_b3,
    )
    own_grad = lax.psum_scatter(grad, "seq", scatter_dimension=1, tiled=True)
    weight_grad = lax.dot_general(
        plane_in, own_grad, (((0,), (1,)), ((), ())), preferred_element_type=f32
    )
    weight_grad = lax.psum(weight_grad, ("dp", "seq"))
    token_grad = lax.dot_general(
        own_grad, w_plane, (((0,), (1,)), ((), ())), preferred_element_type=f32
    ).astype(bf16)
    return (colors[None], token_grad[None], weight_grad)


def solution(mesh):
    in_specs = (
        P("dp", "seq", None),
        P("dp", "seq", None),
        *(P() for _ in range(12)),
        P("dp", None, "seq"),
        P("dp", None, "seq"),
        P("dp", None, "seq"),
    )
    out_specs = (P("dp", None, "seq"), P("dp", "seq", None), P())
    return jax.shard_map(body, mesh=mesh, in_specs=in_specs, out_specs=out_specs, check_vma=False)
```

```python
import functools
import math

import jax
import jax.numpy as jnp
from jax import lax
from jax.experimental import pallas as pl
from jax.experimental.pallas import tpu as pltpu
from jax.sharding import PartitionSpec as P

HEADS = 16
STEPS = 128
PLANES = 3
LANES = 128
NORM_EPS = 1e-05
DEPTH_STEP = 0.02
VMEM_BYTES = 60000 * 1024

bf16 = jnp.bfloat16
f32 = jnp.float32


def in_vmem(count):
    return [pl.BlockSpec(memory_space=pltpu.VMEM)] * count


def plain_norm(inputs):
    row_mean = jnp.mean(inputs, axis=-1, keepdims=True)
    centred = inputs - row_mean
    row_var = jnp.mean(centred * centred, axis=-1, keepdims=True)
    return centred * lax.rsqrt(row_var + NORM_EPS)


def attention_kernel(q_ref, k_ref, v_ref, out_ref, values_ref, *, tile):
    rows, width = q_ref.shape
    low = lax.broadcasted_iota(jnp.int32, (1, LANES), 1) < LANES // 2

    def pair(pair_id, carry):
        first = pl.multiple_of(pair_id * LANES, LANES)
        values = v_ref[:, pl.ds(first, LANES)]
        one = jnp.ones((), bf16)
        values_ref[0] = jnp.where(low, values, one)
        values_ref[1] = jnp.where(low, one, values)

        def block(block_id, inner):
            start = pl.multiple_of(block_id * tile, tile)
            queries = q_ref[pl.ds(start, tile), pl.ds(first, LANES)]
            parts = []
            for head in range(2):
                own = jnp.where(low if head == 0 else ~low, queries, jnp.zeros((), bf16))
                scores = jnp.dot(
                    own, k_ref[pl.ds(first, LANES), :], preferred_element_type=f32
                )
                row_max = jnp.max(scores, axis=1, keepdims=True)
                terms = jnp.exp2(scores - row_max).astype(bf16)
                parts.append(jnp.dot(terms, values_ref[head], preferred_element_type=f32))
            weighted = jnp.where(low, parts[0], parts[1])
            row_sum = pltpu.roll(jnp.where(low, parts[1], parts[0]), LANES // 2, 1)
            out_ref[pl.ds(start, tile), pl.ds(first, LANES)] = (weighted / row_sum).astype(bf16)
            return inner

        lax.fori_loop(0, rows // tile, block, 0)
        return carry

    lax.fori_loop(0, width // LANES, pair, 0)


def attention(queries, keys, values):
    rows, width = queries.shape
    count = values.shape[0]
    return pl.pallas_call(
        functools.partial(attention_kernel, tile=256),
        out_shape=jax.ShapeDtypeStruct((rows, width), bf16),
        in_specs=in_vmem(3),
        out_specs=pl.BlockSpec(memory_space=pltpu.VMEM),
        scratch_shapes=[pltpu.VMEM((2, count, LANES), bf16)],
        compiler_params=pltpu.CompilerParams(vmem_limit_bytes=VMEM_BYTES),
        cost_estimate=pl.CostEstimate(
            flops=4 * rows * count * width,
            bytes_accessed=4 * (rows + count) * width,
            transcendentals=rows * count * HEADS,
        ),
        name="attention",
    )(queries, keys, values)


def table_rows(col_ref, row_ref, plane, first_row, row_count, start, width, side):
    span = pl.ds(start, width)
    pieces = side // 16
    upper = col_ref[2 * plane, :, span].reshape(pieces, 16, width)
    lower = col_ref[2 * plane + 1, :, span].reshape(pieces, 16, width)
    cell_row = row_ref[plane, :, span]
    zero = jnp.zeros((16, width), bf16)
    row_id = jnp.asarray(first_row, jnp.int32)
    before = cell_row == (row_id - 1).astype(bf16)
    blocks = []
    for step in range(row_count):
        here = cell_row == (row_id + step).astype(bf16)
        for piece in range(pieces):
            blocks.append(
                jnp.where(here, upper[piece], jnp.where(before, lower[piece], zero))
            )
        before = here
    return jnp.concatenate(blocks, axis=0)


def ray_scan(values, lane, reverse):
    width = values.shape[1]
    shift = 1
    while shift < STEPS:
        if reverse:
            moved = pltpu.roll(values, width - shift, 1)
            values = values + jnp.where(lane < STEPS - shift, moved, 0.0)
        else:
            moved = pltpu.roll(values, shift, 1)
            values = values + jnp.where(lane >= shift, moved, 0.0)
        shift *= 2
    return values


def render_kernel(
    idx_ref,
    wts_ref,
    planes_ref,
    target_ref,
    w1_ref,
    b1_ref,
    w2_ref,
    b2_ref,
    w3_ref,
    b3_ref,
    colors_ref,
    grad_ref,
    col_ref,
    row_ref,
    fgrad_ref,
    *,
    side,
    prep_width,
    width,
    grad_rows,
):
    samples = idx_ref.shape[1]
    channels, tokens = planes_ref.shape
    plane_size = side * side

    def prepare(step, carry):
        start = pl.multiple_of(step * prep_width, prep_width)
        span = pl.ds(start, prep_width)
        index = idx_ref[:, span]
        weight = wts_ref[:, span].astype(f32)
        column_id = lax.broadcasted_iota(jnp.int32, (side, prep_width), 0)
        for plane in range(PLANES):
            in_plane = (index >= plane * plane_size) & (index < (plane + 1) * plane_size)
            base = jnp.min(jnp.where(in_plane, index, tokens), axis=0, keepdims=True)
            corner = []
            for offset in (0, 1, side, side + 1):
                corner.append(
                    jnp.sum(
                        jnp.where(index == base + offset, weight, 0.0), axis=0, keepdims=True
                    )
                )
            local = base - plane * plane_size
            cell_row = local // side
            column = local - cell_row * side
            for which in range(2):
                col_ref[2 * plane + which, :, span] = jnp.where(
                    column_id == column,
                    corner[2 * which],
                    jnp.where(column_id == column + 1, corner[2 * which + 1], 0.0),
                ).astype(bf16)
            row_ref[plane, :, span] = jnp.broadcast_to(
                cell_row.astype(f32), (16, prep_width)
            ).astype(bf16)
        return carry

    lax.fori_loop(0, samples // prep_width, prepare, 0)

    rays = width // STEPS
    all_rays = samples // STEPS
    w1, w2, w3 = w1_ref[...], w2_ref[...], w3_ref[...]
    b1, b2, b3 = b1_ref[...], b2_ref[...], b3_ref[...]
    lane = lax.broadcasted_iota(jnp.int32, (1, width), 1) % STEPS
    exact = lax.Precision.HIGHEST
    flip = (((0,), (0,)), ((), ()))

    def shade(step, carry):
        start = pl.multiple_of(step * width, width)

        def add_plane(plane, total):
            table = table_rows(col_ref, row_ref, plane, 0, side, start, width, side)
            block = planes_ref[:, pl.ds(pl.multiple_of(plane * plane_size, LANES), plane_size)]
            return total + jnp.dot(block, table, preferred_element_type=f32)

        features = lax.fori_loop(
            0, PLANES, add_plane, jnp.zeros((channels, width), f32)
        ).astype(bf16)

        z1 = jnp.dot(w1, features, preferred_element_type=f32) + b1
        s1 = jax.nn.sigmoid(z1)
        h1 = (z1 * s1).astype(bf16)
        z2 = jnp.dot(w2, h1, preferred_element_type=f32) + b2
        s2 = jax.nn.sigmoid(z2)
        h2 = (z2 * s2).astype(bf16)
        decoded = jnp.dot(w3, h2, preferred_element_type=f32) + b3
        density = decoded[0:1]
        optical = (
            jnp.maximum(density, 0.0) + jnp.log1p(jnp.exp(-jnp.abs(density)))
        ) * DEPTH_STEP
        albedo = jax.nn.sigmoid(decoded[1:4])
        before = ray_scan(optical, lane, False) - optical
        reach = jnp.exp(-before)
        passed = jnp.exp(-optical)
        weight = reach * (1.0 - passed)

        ray_id = lax.broadcasted_iota(jnp.int32, (all_rays, width), 0)
        ray_of = (
            step * rays + lax.broadcasted_iota(jnp.int32, (all_rays, width), 1) // STEPS
        )
        spread = (ray_id == ray_of).astype(f32)
        seen = lax.dot_general(
            weight * albedo,
            spread,
            (((1,), (1,)), ((), ())),
            precision=exact,
            preferred_element_type=f32,
        )
        mine = (
            lax.broadcasted_iota(jnp.int32, (3, all_rays), 1) // rays == step
        )
        colors_ref[...] = jnp.where(mine, seen, colors_ref[...])
        miss = jnp.dot(
            jnp.where(mine, seen - target_ref[...], 0.0),
            spread,
            precision=exact,
            preferred_element_type=f32,
        )
        weight_grad = jnp.sum(miss * albedo, axis=0, keepdims=True)
        term = weight_grad * weight
        later = ray_scan(term, lane, True) - term
        optical_grad = weight_grad * reach * passed - later
        density_grad = optical_grad * (DEPTH_STEP * jax.nn.sigmoid(density))
        albedo_grad = miss * weight * albedo * (1.0 - albedo)
        decoded_grad = jnp.concatenate([density_grad, albedo_grad], axis=0).astype(bf16)
        g2 = lax.dot_general(w3, decoded_grad, flip, preferred_element_type=f32)
        g2 = g2.astype(bf16).astype(f32) * (s2 * (1.0 + z2 * (1.0 - s2)))
        g1 = lax.dot_general(w2, g2.astype(bf16), flip, preferred_element_type=f32)
        g1 = g1.astype(bf16).astype(f32) * (s1 * (1.0 + z1 * (1.0 - s1)))
        fgrad_ref[:, pl.ds(start, width)] = lax.dot_general(
            w1, g1.astype(bf16), flip, preferred_element_type=f32
        ).astype(bf16)
        return carry

    colors_ref[...] = jnp.zeros_like(colors_ref)
    lax.fori_loop(0, samples // width, shade, 0)

    block_size = grad_rows * side
    blocks = side // grad_rows

    def spread_back(step, carry):
        plane = step // blocks
        first_row = (step - plane * blocks) * grad_rows
        table = table_rows(col_ref, row_ref, plane, first_row, grad_rows, 0, samples, side)
        grad_ref[:, pl.ds(pl.multiple_of(step * block_size, block_size), block_size)] = (
            lax.dot_general(
                fgrad_ref[...], table, (((1,), (1,)), ((), ())), preferred_element_type=f32
            ).astype(bf16)
        )
        return carry

    lax.fori_loop(0, PLANES * blocks, spread_back, 0)


def render_and_grad(index, weight, planes, target, w1, b1, w2, b2, w3, b3):
    channels, tokens = planes.shape
    samples = index.shape[1]
    side = math.isqrt(tokens // PLANES)
    return pl.pallas_call(
        functools.partial(
            render_kernel,
            side=side,
            prep_width=min(1024, samples),
            width=min(512, samples),
            grad_rows=16,
        ),
        out_shape=(
            jax.ShapeDtypeStruct(target.shape, f32),
            jax.ShapeDtypeStruct((channels, tokens), bf16),
        ),
        in_specs=in_vmem(10),
        out_specs=tuple(in_vmem(2)),
        scratch_shapes=[
            pltpu.VMEM((2 * PLANES, side, samples), bf16),
            pltpu.VMEM((PLANES, 16, samples), bf16),
            pltpu.VMEM((channels, samples), bf16),
        ],
        compiler_params=pltpu.CompilerParams(vmem_limit_bytes=VMEM_BYTES),
        cost_estimate=pl.CostEstimate(
            flops=4 * channels * tokens * samples,
            bytes_accessed=4 * channels * tokens,
            transcendentals=400 * samples,
        ),
        name="render",
    )(
        index,
        weight,
        planes,
        target,
        w1,
        b1[:, None],
        w2,
        b2[:, None],
        w3,
        b3[:, None],
    )


MESH_ID = pl.DeviceIdType.MESH


def greet(peers):
    barrier = pltpu.get_barrier_semaphore()
    for peer in peers:
        pl.semaphore_signal(barrier, inc=1, device_id=peer, device_id_type=MESH_ID)
    pl.semaphore_wait(barrier, len(peers))


def remote(source, target, send_sem, recv_sem, peer):
    return pltpu.make_async_remote_copy(
        src_ref=source,
        dst_ref=target,
        send_sem=send_sem,
        recv_sem=recv_sem,
        device_id=peer,
        device_id_type=MESH_ID,
    )


def partner_of(me):
    return me + 1 - 2 * (me % 2)


def gather_kernel(
    block_ref, out_ref, send_sem, recv_sem, pass_sem, land_sem, own_sem, *, size, axis
):
    me = lax.axis_index("seq")
    partner = {"seq": partner_of(me)}
    chips = size // 2
    extent = block_ref.shape[axis]

    def place(owner):
        span = pl.ds(pl.multiple_of(owner * extent, extent), extent)
        return out_ref.at[span, :] if axis == 0 else out_ref.at[:, span]

    peers = [{"seq": (me + 2 * step) % size} for step in range(1, chips)]
    greet(peers + [partner])
    own = pltpu.make_async_copy(block_ref, place(me), own_sem)
    own.start()
    sends = []
    for step, peer in enumerate(peers):
        sends.append(remote(block_ref, place(me), send_sem.at[step], recv_sem.at[step], peer))
    sends.append(
        remote(block_ref, place(me), pass_sem.at[chips - 1], land_sem.at[chips - 1], partner)
    )
    for copy in sends:
        copy.start()
    for step in range(chips - 1):
        owner = (me + size - 2 * (step + 1)) % size
        remote(
            block_ref, place(owner), send_sem.at[step], recv_sem.at[step], partner
        ).wait_recv()
        handed = remote(
            place(owner), place(owner), pass_sem.at[step], land_sem.at[step], partner
        )
        handed.start()
        sends.append(handed)
    own.wait()
    for copy in sends:
        copy.wait_send()
    for step in range(chips):
        remote(
            block_ref, place(me), pass_sem.at[step], land_sem.at[step], partner
        ).wait_recv()


def gather(block, axis, size, collective_id):
    shape = list(block.shape)
    shape[axis] *= size
    chips = size // 2
    sems = pltpu.SemaphoreType.DMA
    return pl.pallas_call(
        functools.partial(gather_kernel, size=size, axis=axis),
        out_shape=jax.ShapeDtypeStruct(tuple(shape), block.dtype),
        in_specs=in_vmem(1),
        out_specs=pl.BlockSpec(memory_space=pltpu.VMEM),
        scratch_shapes=[
            sems((chips - 1,)),
            sems((chips - 1,)),
            sems((chips,)),
            sems((chips,)),
            sems,
        ],
        compiler_params=pltpu.CompilerParams(
            collective_id=collective_id, has_side_effects=True, vmem_limit_bytes=VMEM_BYTES
        ),
        name="gather",
    )(block)


def reduce_kernel(
    grad_ref,
    plane_in_ref,
    own_ref,
    total_ref,
    pair_ref,
    sum_ref,
    land_ref,
    part_ref,
    chunk_land_ref,
    chunk_ref,
    scene_ref,
    pair_send,
    pair_recv,
    sum_send,
    sum_recv,
    chunk_send,
    chunk_recv,
    scene_send,
    scene_recv,
    last_send,
    last_recv,
    *,
    size,
    scenes,
):
    me = lax.axis_index("seq")
    scene = lax.axis_index("dp")
    core = me % 2
    chip = me // 2
    chips = size // 2
    partner = {"seq": partner_of(me)}
    channels, extent = own_ref.shape
    rows, lanes = chunk_ref.shape

    def columns(owner):
        return pl.ds(pl.multiple_of(owner * extent, extent), extent)

    def chunk_of(owner):
        return (
            pl.ds(pl.multiple_of((owner % 2) * rows, rows), rows),
            pl.ds(pl.multiple_of((owner // 2) * lanes, lanes), lanes),
        )

    others = [(me + step) % size for step in range(1, size)]
    other_scenes = [(scene + step) % scenes for step in range(1, scenes)]
    greet([{"seq": owner} for owner in others] + [{"dp": owner} for owner in other_scenes])

    order = [(chip + step) % chips for step in range(1, chips + 1)]
    waiting = []
    for there in order:
        copy = remote(
            grad_ref.at[:, columns(2 * there + 1 - core)],
            pair_ref.at[there],
            pair_send.at[there],
            pair_recv.at[there],
            partner,
        )
        copy.start()
        waiting.append(copy)
    mine = None
    ready = None
    for there in order:
        remote(
            own_ref, pair_ref.at[there], pair_send.at[there], pair_recv.at[there], partner
        ).wait_recv()
        both = grad_ref[:, columns(2 * there + core)].astype(f32) + pair_ref[there].astype(f32)
        if there is not order[-1]:
            sum_ref[there] = both.astype(bf16)
        else:
            mine = both
        if ready is not None:
            copy = remote(
                sum_ref.at[ready],
                land_ref.at[chip],
                sum_send.at[ready],
                sum_recv.at[chip],
                {"seq": 2 * ready + core},
            )
            copy.start()
            waiting.append(copy)
        ready = there
    for there in order[:-1]:
        remote(
            own_ref, land_ref.at[there], sum_send.at[there], sum_recv.at[there], partner
        ).wait_recv()
        mine = mine + land_ref[there].astype(f32)
    own_grad = mine.astype(bf16)
    own_ref[...] = own_grad

    part_ref[...] = jnp.dot(own_grad, plane_in_ref[...], preferred_element_type=f32)
    for owner in others:
        spot = chunk_of(owner)
        copy = remote(
            part_ref.at[spot],
            chunk_land_ref.at[me],
            chunk_send.at[owner],
            chunk_recv.at[me],
            {"seq": owner},
        )
        copy.start()
        waiting.append(copy)
    chunk = part_ref[chunk_of(me)]
    for owner in others:
        remote(
            chunk_ref,
            chunk_land_ref.at[owner],
            chunk_send.at[owner],
            chunk_recv.at[owner],
            partner,
        ).wait_recv()
        chunk = chunk + chunk_land_ref[owner]
    chunk_ref[...] = chunk
    scene_ref[scene] = chunk
    for other in other_scenes:
        copy = remote(
            chunk_ref,
            scene_ref.at[scene],
            scene_send.at[other],
            scene_recv.at[scene],
            {"dp": other},
        )
        copy.start()
        waiting.append(copy)
    for other in other_scenes:
        remote(
            chunk_ref,
            scene_ref.at[other],
            scene_send.at[other],
            scene_recv.at[other],
            partner,
        ).wait_recv()
    final = scene_ref[0]
    for other in range(1, scenes):
        final = final + scene_ref[other]
    spot = chunk_of(me)
    total_ref[spot] = final
    for owner in others:
        copy = remote(
            total_ref.at[spot],
            total_ref.at[spot],
            last_send.at[owner],
            last_recv.at[me],
            {"seq": owner},
        )
        copy.start()
        waiting.append(copy)
    for owner in others:
        there = chunk_of(owner)
        remote(
            total_ref.at[there],
            total_ref.at[there],
            last_send.at[owner],
            last_recv.at[owner],
            partner,
        ).wait_recv()
    for copy in waiting:
        copy.wait_send()


def reduce_grads(grad, plane_in, size, scenes, collective_id):
    channels, tokens = grad.shape
    extent, width = plane_in.shape
    chips = size // 2
    rows, lanes = channels // 2, width // chips
    sems = pltpu.SemaphoreType.DMA
    block = (chips, channels, extent)
    return pl.pallas_call(
        functools.partial(reduce_kernel, size=size, scenes=scenes),
        out_shape=(
            jax.ShapeDtypeStruct((channels, extent), bf16),
            jax.ShapeDtypeStruct((channels, width), f32),
        ),
        in_specs=in_vmem(2),
        out_specs=tuple(in_vmem(2)),
        scratch_shapes=[
            pltpu.VMEM(block, bf16),
            pltpu.VMEM(block, bf16),
            pltpu.VMEM(block, bf16),
            pltpu.VMEM((channels, width), f32),
            pltpu.VMEM((size, rows, lanes), f32),
            pltpu.VMEM((rows, lanes), f32),
            pltpu.VMEM((scenes, rows, lanes), f32),
            sems((chips,)),
            sems((chips,)),
            sems((chips,)),
            sems((chips,)),
            sems((size,)),
            sems((size,)),
            sems((scenes,)),
            sems((scenes,)),
            sems((size,)),
            sems((size,)),
        ],
        compiler_params=pltpu.CompilerParams(
            collective_id=collective_id, has_side_effects=True, vmem_limit_bytes=VMEM_BYTES
        ),
        name="reduce",
    )(grad, plane_in)


def body(
    tokens,
    image_tokens,
    norm_gain,
    w_query,
    w_key,
    w_value,
    w_out,
    w_plane,
    dec_w1,
    dec_b1,
    dec_w2,
    dec_b2,
    dec_w3,
    dec_b3,
    corner_idx,
    corner_wts,
    target_color,
):
    own_tokens = tokens[0]
    model_width = own_tokens.shape[1]
    head_dim = model_width // HEADS
    size = lax.axis_size("seq")
    images = gather(image_tokens[0], 0, size, 0)
    normed = plain_norm(own_tokens.astype(f32)).astype(bf16)
    score_scale = math.log2(math.e) / math.sqrt(head_dim)
    queries = (jnp.dot(normed, w_query, preferred_element_type=f32) * score_scale).astype(bf16)
    keys = lax.dot_general(
        w_key, images, (((0,), (1,)), ((), ())), preferred_element_type=f32
    ).astype(bf16)
    values = jnp.dot(images, w_value, preferred_element_type=f32).astype(bf16)
    attended = attention(queries, keys, values)
    mixed = (
        own_tokens.astype(f32) + jnp.dot(attended, w_out, preferred_element_type=f32)
    ).astype(bf16)
    plane_in = (plain_norm(mixed.astype(f32)) * norm_gain).astype(bf16)
    planes = lax.dot_general(
        w_plane, plane_in, (((0,), (1,)), ((), ())), preferred_element_type=f32
    ).astype(bf16)
    planes = gather(planes, 1, size, 1)
    colors, grad = render_and_grad(
        corner_idx[0],
        corner_wts[0],
        planes,
        target_color[0],
        dec_w1,
        dec_b1,
        dec_w2,
        dec_b2,
        dec_w3,
        dec_b3,
    )
    own_grad, weight_grad = reduce_grads(grad, plane_in, size, lax.axis_size("dp"), 2)
    weight_grad = weight_grad.T
    token_grad = lax.dot_general(
        own_grad, w_plane, (((0,), (1,)), ((), ())), preferred_element_type=f32
    ).astype(bf16)
    return (colors[None], token_grad[None], weight_grad)


def solution(mesh):
    in_specs = (
        P("dp", "seq", None),
        P("dp", "seq", None),
        *(P() for _ in range(12)),
        P("dp", None, "seq"),
        P("dp", None, "seq"),
        P("dp", None, "seq"),
    )
    out_specs = (P("dp", None, "seq"), P("dp", "seq", None), P())
    return jax.shard_map(body, mesh=mesh, in_specs=in_specs, out_specs=out_specs, check_vma=False)
```

```python
import functools
import math

import jax
import jax.numpy as jnp
from jax import lax
from jax.experimental import pallas as pl
from jax.experimental.pallas import tpu as pltpu
from jax.sharding import PartitionSpec as P

HEADS = 16
STEPS = 128
PLANES = 3
LANES = 128
NORM_EPS = 1e-05
DEPTH_STEP = 0.02
VMEM_BYTES = 60000 * 1024

bf16 = jnp.bfloat16
f32 = jnp.float32


def in_vmem(count):
    return [pl.BlockSpec(memory_space=pltpu.VMEM)] * count


def plain_norm(inputs):
    row_mean = jnp.mean(inputs, axis=-1, keepdims=True)
    centred = inputs - row_mean
    row_var = jnp.mean(centred * centred, axis=-1, keepdims=True)
    return centred * lax.rsqrt(row_var + NORM_EPS)


def attention_kernel(
    q_ref,
    k_ref,
    v_ref,
    tokens_ref,
    w_out_ref,
    gain_ref,
    w_plane_ref,
    plane_in_ref,
    planes_ref,
    values_ref,
    scores_ref,
    maxes_ref,
    attended_ref,
    *,
    tile,
):
    rows, width = q_ref.shape
    count = k_ref.shape[0]
    pairs = width // LANES
    low = lax.broadcasted_iota(jnp.int32, (1, LANES), 1) < LANES // 2
    turned = (((1,), (1,)), ((), ()))

    def score(pair_id, head):
        span = pl.ds(pl.multiple_of(pair_id * LANES, LANES), LANES)
        own = jnp.where(low if head == 0 else ~low, q_ref[:, span], jnp.zeros((), bf16))
        scores = lax.dot_general(own, k_ref[:, span], turned, preferred_element_type=f32)
        scores_ref[head] = scores
        highest = scores[:, :LANES]
        for first in range(LANES, count, LANES):
            highest = jnp.maximum(highest, scores[:, first : first + LANES])
        maxes_ref[head] = highest

    def weigh(head):
        row_max = jnp.max(maxes_ref[head], axis=1, keepdims=True)
        terms = jnp.exp2(scores_ref[head] - row_max).astype(bf16)
        return jnp.dot(terms, values_ref[head], preferred_element_type=f32)

    score(0, 0)

    def pair(pair_id, carry):
        span = pl.ds(pl.multiple_of(pair_id * LANES, LANES), LANES)
        values = v_ref[:, span]
        one = jnp.ones((), bf16)
        values_ref[0] = jnp.where(low, values, one)
        values_ref[1] = jnp.where(low, one, values)
        score(pair_id, 1)
        first = weigh(0)
        score((pair_id + 1) % pairs, 0)
        second = weigh(1)
        row_sum = pltpu.roll(jnp.where(low, second, first), LANES // 2, 1)
        attended_ref[:, span] = (jnp.where(low, first, second) / row_sum).astype(bf16)
        return carry

    lax.fori_loop(0, pairs, pair, 0)

    def project(step, carry):
        span = pl.ds(pl.multiple_of(step * tile, tile), tile)
        mixed = tokens_ref[span, :].astype(f32) + jnp.dot(
            attended_ref[span, :], w_out_ref[...], preferred_element_type=f32
        )
        mixed = mixed.astype(bf16).astype(f32)
        plane_in = (plain_norm(mixed) * gain_ref[...]).astype(bf16)
        plane_in_ref[span, :] = plane_in
        planes_ref[:, span] = lax.dot_general(
            w_plane_ref[...], plane_in, turned, preferred_element_type=f32
        ).astype(bf16)
        return carry

    lax.fori_loop(0, rows // tile, project, 0)


def attention(queries, keys, values, tokens, w_out, gain, w_plane):
    rows, width = queries.shape
    count = values.shape[0]
    channels = w_plane.shape[1]
    return pl.pallas_call(
        functools.partial(attention_kernel, tile=256),
        out_shape=(
            jax.ShapeDtypeStruct((rows, width), bf16),
            jax.ShapeDtypeStruct((channels, rows), bf16),
        ),
        in_specs=in_vmem(7),
        out_specs=tuple(in_vmem(2)),
        scratch_shapes=[
            pltpu.VMEM((2, count, LANES), bf16),
            pltpu.VMEM((2, rows, count), f32),
            pltpu.VMEM((2, rows, LANES), f32),
            pltpu.VMEM((rows, width), bf16),
        ],
        compiler_params=pltpu.CompilerParams(vmem_limit_bytes=36 * 1024 * 1024),
        cost_estimate=pl.CostEstimate(
            flops=4 * rows * count * width,
            bytes_accessed=4 * (rows + count) * width,
            transcendentals=rows * count * HEADS,
        ),
        name="attention",
    )(queries, keys, values, tokens, w_out, gain[None, :], w_plane.T)


def table_rows(col_ref, row_ref, plane, first_row, row_count, start, width, side):
    span = pl.ds(start, width)
    pieces = side // 16
    upper = col_ref[2 * plane, :, span].reshape(pieces, 16, width)
    lower = col_ref[2 * plane + 1, :, span].reshape(pieces, 16, width)
    cell_row = row_ref[plane, :, span]
    zero = jnp.zeros((16, width), bf16)
    row_id = jnp.asarray(first_row, jnp.int32)
    before = cell_row == (row_id - 1).astype(bf16)
    blocks = []
    for step in range(row_count):
        here = cell_row == (row_id + step).astype(bf16)
        for piece in range(pieces):
            blocks.append(
                jnp.where(here, upper[piece], jnp.where(before, lower[piece], zero))
            )
        before = here
    return jnp.concatenate(blocks, axis=0)


def ray_scan(values, lane, reverse):
    width = values.shape[1]
    shift = 1
    while shift < STEPS:
        if reverse:
            moved = pltpu.roll(values, width - shift, 1)
            values = values + jnp.where(lane < STEPS - shift, moved, 0.0)
        else:
            moved = pltpu.roll(values, shift, 1)
            values = values + jnp.where(lane >= shift, moved, 0.0)
        shift *= 2
    return values


def column_of(row_ref):
    count = row_ref.shape[1]
    diagonal = lax.broadcasted_iota(jnp.int32, (count, count), 0) == lax.broadcasted_iota(
        jnp.int32, (count, count), 1
    )
    return jnp.sum(jnp.where(diagonal, row_ref[...], 0.0), axis=1, keepdims=True)


def render_kernel(
    idx_ref,
    wts_ref,
    planes_ref,
    target_ref,
    w1_ref,
    b1_ref,
    w2_ref,
    b2_ref,
    w3_ref,
    b3_ref,
    colors_ref,
    grad_ref,
    col_ref,
    row_ref,
    fgrad_ref,
    z1_ref,
    z2_ref,
    decoded_ref,
    *,
    side,
    prep_width,
    width,
    grad_rows,
):
    samples = idx_ref.shape[1]
    channels, tokens = planes_ref.shape
    plane_size = side * side

    def prepare(step, carry):
        start = pl.multiple_of(step * prep_width, prep_width)
        span = pl.ds(start, prep_width)
        index = idx_ref[:, span]
        weight = wts_ref[:, span].astype(f32)
        column_id = lax.broadcasted_iota(jnp.int32, (side, prep_width), 0)
        for plane in range(PLANES):
            in_plane = (index >= plane * plane_size) & (index < (plane + 1) * plane_size)
            base = jnp.min(jnp.where(in_plane, index, tokens), axis=0, keepdims=True)
            corner = []
            for offset in (0, 1, side, side + 1):
                corner.append(
                    jnp.sum(
                        jnp.where(index == base + offset, weight, 0.0), axis=0, keepdims=True
                    )
                )
            local = base - plane * plane_size
            cell_row = local // side
            column = local - cell_row * side
            for which in range(2):
                col_ref[2 * plane + which, :, span] = jnp.where(
                    column_id == column,
                    corner[2 * which],
                    jnp.where(column_id == column + 1, corner[2 * which + 1], 0.0),
                ).astype(bf16)
            row_ref[plane, :, span] = jnp.broadcast_to(
                cell_row.astype(f32), (16, prep_width)
            ).astype(bf16)
        return carry

    lax.fori_loop(0, samples // prep_width, prepare, 0)

    w1, w2, w3 = w1_ref[...], w2_ref[...], w3_ref[...]
    b1, b2, b3 = column_of(b1_ref), column_of(b2_ref), column_of(b3_ref)
    exact = lax.Precision.HIGHEST
    turned = (((1,), (1,)), ((), ()))
    flip = (((0,), (0,)), ((), ()))

    def decode(step, carry):
        start = pl.multiple_of(step * width, width)
        span = pl.ds(start, width)

        def add_plane(plane, total):
            table = table_rows(col_ref, row_ref, plane, 0, side, start, width, side)
            block = planes_ref[:, pl.ds(pl.multiple_of(plane * plane_size, LANES), plane_size)]
            return total + jnp.dot(block, table, preferred_element_type=f32)

        features = lax.fori_loop(
            0, PLANES, add_plane, jnp.zeros((channels, width), f32)
        ).astype(bf16)
        z1 = jnp.dot(w1, features, preferred_element_type=f32) + b1
        z1_ref[:, span] = z1
        h1 = (z1 * jax.nn.sigmoid(z1)).astype(bf16)
        z2 = jnp.dot(w2, h1, preferred_element_type=f32) + b2
        z2_ref[:, span] = z2
        h2 = (z2 * jax.nn.sigmoid(z2)).astype(bf16)
        decoded_ref[:, span] = jnp.dot(w3, h2, preferred_element_type=f32) + b3
        return carry

    lax.fori_loop(0, samples // width, decode, 0)

    rays = samples // STEPS
    lane = lax.broadcasted_iota(jnp.int32, (1, samples), 1) % STEPS
    density = decoded_ref[0:1]
    optical = (jnp.maximum(density, 0.0) + jnp.log1p(jnp.exp(-jnp.abs(density)))) * DEPTH_STEP
    albedo = jax.nn.sigmoid(decoded_ref[1:4])
    reach = jnp.exp(optical - ray_scan(optical, lane, False))
    passed = jnp.exp(-optical)
    weight = reach * (1.0 - passed)
    spread = (
        lax.broadcasted_iota(jnp.int32, (rays, samples), 0)
        == lax.broadcasted_iota(jnp.int32, (rays, samples), 1) // STEPS
    ).astype(f32)
    colors = lax.dot_general(
        weight * albedo, spread, turned, precision=exact, preferred_element_type=f32
    )
    colors_ref[...] = colors
    miss = jnp.dot(
        colors - target_ref[...], spread, precision=exact, preferred_element_type=f32
    )
    weight_grad = jnp.sum(miss * albedo, axis=0, keepdims=True)
    term = weight_grad * weight
    later = ray_scan(term, lane, True) - term
    optical_grad = weight_grad * reach * passed - later
    decoded_ref[0:1] = optical_grad * (DEPTH_STEP * jax.nn.sigmoid(density))
    decoded_ref[1:4] = miss * weight * albedo * (1.0 - albedo)

    def silu_grad(pre):
        gate = jax.nn.sigmoid(pre)
        return gate * (1.0 + pre * (1.0 - gate))

    def decode_back(step, carry):
        span = pl.ds(pl.multiple_of(step * prep_width, prep_width), prep_width)
        g2 = lax.dot_general(
            w3, decoded_ref[:, span].astype(bf16), flip, preferred_element_type=f32
        )
        g2 = g2.astype(bf16).astype(f32) * silu_grad(z2_ref[:, span])
        g1 = lax.dot_general(w2, g2.astype(bf16), flip, preferred_element_type=f32)
        g1 = g1.astype(bf16).astype(f32) * silu_grad(z1_ref[:, span])
        fgrad_ref[:, span] = lax.dot_general(
            w1, g1.astype(bf16), flip, preferred_element_type=f32
        ).astype(bf16)
        return carry

    lax.fori_loop(0, samples // prep_width, decode_back, 0)

    block_size = grad_rows * side
    blocks = side // grad_rows

    def spread_back(step, carry):
        plane = step // blocks
        first_row = (step - plane * blocks) * grad_rows
        table = table_rows(col_ref, row_ref, plane, first_row, grad_rows, 0, samples, side)
        grad_ref[:, pl.ds(pl.multiple_of(step * block_size, block_size), block_size)] = (
            lax.dot_general(
                fgrad_ref[...], table, (((1,), (1,)), ((), ())), preferred_element_type=f32
            ).astype(bf16)
        )
        return carry

    lax.fori_loop(0, PLANES * blocks, spread_back, 0)


def render_and_grad(index, weight, planes, target, w1, b1, w2, b2, w3, b3):
    channels, tokens = planes.shape
    samples = index.shape[1]
    side = math.isqrt(tokens // PLANES)
    return pl.pallas_call(
        functools.partial(
            render_kernel,
            side=side,
            prep_width=min(1024, samples),
            width=min(512, samples),
            grad_rows=16,
        ),
        out_shape=(
            jax.ShapeDtypeStruct(target.shape, f32),
            jax.ShapeDtypeStruct((channels, tokens), bf16),
        ),
        in_specs=in_vmem(10),
        out_specs=tuple(in_vmem(2)),
        scratch_shapes=[
            pltpu.VMEM((2 * PLANES, side, samples), bf16),
            pltpu.VMEM((PLANES, 16, samples), bf16),
            pltpu.VMEM((channels, samples), bf16),
            pltpu.VMEM((w1.shape[0], samples), f32),
            pltpu.VMEM((w2.shape[0], samples), f32),
            pltpu.VMEM((w3.shape[0], samples), f32),
        ],
        compiler_params=pltpu.CompilerParams(vmem_limit_bytes=40 * 1024 * 1024),
        cost_estimate=pl.CostEstimate(
            flops=4 * channels * tokens * samples,
            bytes_accessed=4 * channels * tokens,
            transcendentals=400 * samples,
        ),
        name="render",
    )(
        index,
        weight,
        planes,
        target,
        w1,
        b1[None, :],
        w2,
        b2[None, :],
        w3,
        b3[None, :],
    )


MESH_ID = pl.DeviceIdType.MESH


def greet(peers):
    barrier = pltpu.get_barrier_semaphore()
    for peer in peers:
        pl.semaphore_signal(barrier, inc=1, device_id=peer, device_id_type=MESH_ID)
    pl.semaphore_wait(barrier, len(peers))


def remote(source, target, send_sem, recv_sem, peer):
    return pltpu.make_async_remote_copy(
        src_ref=source,
        dst_ref=target,
        send_sem=send_sem,
        recv_sem=recv_sem,
        device_id=peer,
        device_id_type=MESH_ID,
    )


def partner_of(me):
    return me + 1 - 2 * (me % 2)


RING = 4
SENDS, ARRIVALS = 19, 10


class Exchange:
    def __init__(self, block_ref, out_ref, axis, sems):
        self.block, self.out, self.axis = block_ref, out_ref, axis
        self.send_sem, self.recv_sem, self.land_sem, self.own_sem = sems
        me = lax.axis_index("seq")
        self.me = me
        self.core = me % 2
        self.y = (me // 2) % 2
        self.x = me // 4
        self.extent = block_ref.shape[axis]
        self.started = []
        self.right = {"seq": self.at(1, 0)}
        self.left = {"seq": self.at(-1, 0)}
        self.over = {"seq": self.at(0, 1)}
        self.partner = {"seq": partner_of(me)}

    def at(self, dx, dy):
        return 4 * ((self.x + dx + RING) % RING) + 2 * ((self.y + dy) % 2) + self.core

    def place(self, owner, half=None):
        size = self.extent if half is None else self.extent // 2
        start = owner * self.extent + (0 if half is None else half * size)
        span = pl.ds(pl.multiple_of(start, size), size)
        return self.out.at[span, :] if self.axis == 0 else self.out.at[:, span]

    def push(self, source, owner, half, recv, peer):
        copy = remote(
            source, self.place(owner, half), self.send_sem.at[len(self.started)], recv, peer
        )
        copy.start()
        self.started.append(copy)

    def relay(self, owner, half, recv, peer):
        self.push(self.place(owner, half), owner, half, recv, peer)

    def hear(self, owner, half, sem):
        spot = self.place(owner, half)
        remote(spot, spot, self.send_sem.at[0], sem, self.partner).wait_recv()

    def begin(self):
        greet([self.right, self.left, self.over, self.partner])
        self.own = pltpu.make_async_copy(self.block, self.place(self.me), self.own_sem)
        self.own.start()
        recv, land = self.recv_sem, self.land_sem
        self.push(self.block, self.me, None, recv.at[0], self.right)
        self.push(self.block, self.me, None, recv.at[1], self.left)
        self.push(self.block, self.me, None, recv.at[2], self.over)
        self.push(self.block, self.me, None, land.at[9], self.partner)

    def arrive(self, number, dx, dy, half, onward):
        owner = self.at(dx, dy)
        self.hear(owner, half, self.recv_sem.at[number])
        for part, target, peer in onward:
            self.relay(owner, part, self.recv_sem.at[target], peer)
        self.relay(owner, half, self.land_sem.at[number], self.partner)

    def beside(self):
        self.arrive(0, -1, 0, None, [(0, 5, self.right)])
        self.arrive(1, 1, 0, None, [(1, 6, self.left)])

    def across(self):
        self.arrive(2, 0, 1, None, [(None, 3, self.right), (None, 4, self.left)])

    def opposite(self):
        self.arrive(5, 2, 0, 0, [])
        self.arrive(6, 2, 0, 1, [])

    def beside_across(self):
        self.arrive(3, -1, 1, None, [(0, 7, self.right)])
        self.arrive(4, 1, 1, None, [(1, 8, self.left)])

    def opposite_across(self):
        self.arrive(7, 2, 1, 0, [])
        self.arrive(8, 2, 1, 1, [])

    def handed(self, number, dx, dy, half):
        other = self.at(dx, dy) + 1 - 2 * self.core
        self.hear(other, half, self.land_sem.at[number])

    def finish(self):
        for copy in self.started:
            copy.wait_send()


def exchange_sems():
    sems = pltpu.SemaphoreType.DMA
    return [sems((SENDS,)), sems((ARRIVALS,)), sems((ARRIVALS,)), sems]


def gather_kernel(block_ref, out_ref, *sems, axis):
    ring = Exchange(block_ref, out_ref, axis, sems)
    ring.begin()
    ring.beside()
    ring.across()
    ring.opposite()
    ring.beside_across()
    ring.opposite_across()
    ring.own.wait()
    ring.handed(9, 0, 0, None)
    ring.handed(0, -1, 0, None)
    ring.handed(1, 1, 0, None)
    ring.handed(2, 0, 1, None)
    ring.handed(5, 2, 0, 0)
    ring.handed(6, 2, 0, 1)
    ring.handed(3, -1, 1, None)
    ring.handed(4, 1, 1, None)
    ring.handed(7, 2, 1, 0)
    ring.handed(8, 2, 1, 1)
    ring.finish()


def gather(block, axis, size, collective_id):
    shape = list(block.shape)
    shape[axis] *= size
    return pl.pallas_call(
        functools.partial(gather_kernel, axis=axis),
        out_shape=jax.ShapeDtypeStruct(tuple(shape), block.dtype),
        in_specs=in_vmem(1),
        out_specs=pl.BlockSpec(memory_space=pltpu.VMEM),
        scratch_shapes=exchange_sems(),
        compiler_params=pltpu.CompilerParams(
            collective_id=collective_id,
            has_side_effects=True,
            vmem_limit_bytes=8 * 1024 * 1024,
        ),
        name="gather",
    )(block)


def front_kernel(
    tokens_ref,
    image_ref,
    w_query_hbm,
    w_key_hbm,
    w_value_hbm,
    q_ref,
    k_ref,
    v_ref,
    images_ref,
    w_query_ref,
    w_key_ref,
    w_value_ref,
    load_sem,
    *sems,
    tile,
    scale,
):
    ring = Exchange(image_ref, images_ref, 0, sems)
    loads = []
    for number, (source, target) in enumerate(
        (
            (w_query_hbm, w_query_ref),
            (w_key_hbm, w_key_ref),
            (w_value_hbm, w_value_ref),
        )
    ):
        copy = pltpu.make_async_copy(source, target, load_sem.at[number])
        copy.start()
        loads.append(copy)
    ring.begin()

    def query(step):
        span = pl.ds(step * tile, tile)
        normed = plain_norm(tokens_ref[span, :].astype(f32)).astype(bf16)
        product = jnp.dot(normed, w_query_ref[...], preferred_element_type=f32)
        q_ref[span, :] = (product * scale).astype(bf16)

    def keys_values(dx, dy):
        owner = ring.at(dx, dy) // 2
        rows = 2 * image_ref.shape[0]
        span = pl.ds(pl.multiple_of(owner * rows, rows), rows)
        images = images_ref[span, :]
        k_ref[span, :] = jnp.dot(
            images, w_key_ref[...], preferred_element_type=f32
        ).astype(bf16)
        v_ref[span, :] = jnp.dot(
            images, w_value_ref[...], preferred_element_type=f32
        ).astype(bf16)

    loads[0].wait()
    query(0)
    ring.beside()
    query(1)
    ring.across()
    query(2)
    ring.opposite()
    loads[1].wait()
    loads[2].wait()
    ring.own.wait()
    ring.handed(9, 0, 0, None)
    keys_values(0, 0)
    ring.beside_across()
    ring.handed(0, -1, 0, None)
    keys_values(-1, 0)
    ring.handed(1, 1, 0, None)
    keys_values(1, 0)
    ring.opposite_across()
    ring.handed(2, 0, 1, None)
    keys_values(0, 1)
    ring.handed(5, 2, 0, 0)
    ring.handed(6, 2, 0, 1)
    keys_values(2, 0)
    ring.handed(3, -1, 1, None)
    keys_values(-1, 1)
    ring.handed(4, 1, 1, None)
    keys_values(1, 1)
    ring.handed(7, 2, 1, 0)
    ring.handed(8, 2, 1, 1)
    keys_values(2, 1)
    ring.finish()


def front(tokens, images, w_query, w_key, w_value, size, scale, collective_id):
    rows, width = tokens.shape
    depth = images.shape[1]
    count = images.shape[0] * size
    heads = w_key.shape[1]
    return pl.pallas_call(
        functools.partial(front_kernel, tile=rows // 3, scale=scale),
        out_shape=(
            jax.ShapeDtypeStruct((rows, width), bf16),
            jax.ShapeDtypeStruct((count, heads), bf16),
            jax.ShapeDtypeStruct((count, heads), bf16),
        ),
        in_specs=in_vmem(2) + [pl.BlockSpec(memory_space=pltpu.HBM)] * 3,
        out_specs=tuple(in_vmem(3)),
        scratch_shapes=[
            pltpu.VMEM((count, depth), bf16),
            pltpu.VMEM(w_query.shape, bf16),
            pltpu.VMEM(w_key.shape, bf16),
            pltpu.VMEM(w_value.shape, bf16),
            pltpu.SemaphoreType.DMA((3,)),
            *exchange_sems(),
        ],
        compiler_params=pltpu.CompilerParams(
            collective_id=collective_id,
            has_side_effects=True,
            vmem_limit_bytes=24 * 1024 * 1024,
        ),
        name="front",
    )(tokens, images, w_query, w_key, w_value)


def reduce_kernel(
    grad_ref,
    plane_in_ref,
    own_ref,
    total_ref,
    pair_ref,
    sum_ref,
    land_ref,
    part_ref,
    chunk_land_ref,
    chunk_ref,
    scene_ref,
    pair_send,
    pair_recv,
    sum_send,
    sum_recv,
    chunk_send,
    chunk_recv,
    scene_send,
    scene_recv,
    last_send,
    last_recv,
    *,
    size,
    scenes,
):
    me = lax.axis_index("seq")
    scene = lax.axis_index("dp")
    core = me % 2
    chip = me // 2
    chips = size // 2
    partner = {"seq": partner_of(me)}
    channels, extent = own_ref.shape
    rows, lanes = chunk_ref.shape

    def columns(owner):
        return pl.ds(pl.multiple_of(owner * extent, extent), extent)

    def chunk_of(owner):
        return (
            pl.ds(pl.multiple_of((owner % 2) * rows, rows), rows),
            pl.ds(pl.multiple_of((owner // 2) * lanes, lanes), lanes),
        )

    others = [(me + step) % size for step in range(1, size)]
    other_scenes = [(scene + step) % scenes for step in range(1, scenes)]
    greet([{"seq": owner} for owner in others] + [{"dp": owner} for owner in other_scenes])

    order = [(chip + step) % chips for step in range(1, chips + 1)]
    waiting = []
    for there in order:
        copy = remote(
            grad_ref.at[:, columns(2 * there + 1 - core)],
            pair_ref.at[there],
            pair_send.at[there],
            pair_recv.at[there],
            partner,
        )
        copy.start()
        waiting.append(copy)
    mine = None
    ready = None
    for there in order:
        remote(
            own_ref, pair_ref.at[there], pair_send.at[there], pair_recv.at[there], partner
        ).wait_recv()
        both = grad_ref[:, columns(2 * there + core)].astype(f32) + pair_ref[there].astype(f32)
        if there is not order[-1]:
            sum_ref[there] = both.astype(bf16)
        else:
            mine = both
        if ready is not None:
            copy = remote(
                sum_ref.at[ready],
                land_ref.at[chip],
                sum_send.at[ready],
                sum_recv.at[chip],
                {"seq": 2 * ready + core},
            )
            copy.start()
            waiting.append(copy)
        ready = there
    for there in order[:-1]:
        remote(
            own_ref, land_ref.at[there], sum_send.at[there], sum_recv.at[there], partner
        ).wait_recv()
        mine = mine + land_ref[there].astype(f32)
    own_grad = mine.astype(bf16)
    own_ref[...] = own_grad

    part_ref[...] = jnp.dot(own_grad, plane_in_ref[...], preferred_element_type=f32)
    for owner in others:
        spot = chunk_of(owner)
        copy = remote(
            part_ref.at[spot],
            chunk_land_ref.at[me],
            chunk_send.at[owner],
            chunk_recv.at[me],
            {"seq": owner},
        )
        copy.start()
        waiting.append(copy)
    chunk = part_ref[chunk_of(me)]
    for owner in others:
        remote(
            chunk_ref,
            chunk_land_ref.at[owner],
            chunk_send.at[owner],
            chunk_recv.at[owner],
            partner,
        ).wait_recv()
        chunk = chunk + chunk_land_ref[owner]
    chunk_ref[...] = chunk
    scene_ref[scene] = chunk
    for other in other_scenes:
        copy = remote(
            chunk_ref,
            scene_ref.at[scene],
            scene_send.at[other],
            scene_recv.at[scene],
            {"dp": other},
        )
        copy.start()
        waiting.append(copy)
    for other in other_scenes:
        remote(
            chunk_ref,
            scene_ref.at[other],
            scene_send.at[other],
            scene_recv.at[other],
            partner,
        ).wait_recv()
    final = scene_ref[0]
    for other in range(1, scenes):
        final = final + scene_ref[other]
    spot = chunk_of(me)
    total_ref[spot] = final
    for owner in others:
        copy = remote(
            total_ref.at[spot],
            total_ref.at[spot],
            last_send.at[owner],
            last_recv.at[me],
            {"seq": owner},
        )
        copy.start()
        waiting.append(copy)
    for owner in others:
        there = chunk_of(owner)
        remote(
            total_ref.at[there],
            total_ref.at[there],
            last_send.at[owner],
            last_recv.at[owner],
            partner,
        ).wait_recv()
    for copy in waiting:
        copy.wait_send()


def reduce_grads(grad, plane_in, size, scenes, collective_id):
    channels, tokens = grad.shape
    extent, width = plane_in.shape
    chips = size // 2
    rows, lanes = channels // 2, width // chips
    sems = pltpu.SemaphoreType.DMA
    block = (chips, channels, extent)
    return pl.pallas_call(
        functools.partial(reduce_kernel, size=size, scenes=scenes),
        out_shape=(
            jax.ShapeDtypeStruct((channels, extent), bf16),
            jax.ShapeDtypeStruct((channels, width), f32),
        ),
        in_specs=in_vmem(2),
        out_specs=tuple(in_vmem(2)),
        scratch_shapes=[
            pltpu.VMEM(block, bf16),
            pltpu.VMEM(block, bf16),
            pltpu.VMEM(block, bf16),
            pltpu.VMEM((channels, width), f32),
            pltpu.VMEM((size, rows, lanes), f32),
            pltpu.VMEM((rows, lanes), f32),
            pltpu.VMEM((scenes, rows, lanes), f32),
            sems((chips,)),
            sems((chips,)),
            sems((chips,)),
            sems((chips,)),
            sems((size,)),
            sems((size,)),
            sems((scenes,)),
            sems((scenes,)),
            sems((size,)),
            sems((size,)),
        ],
        compiler_params=pltpu.CompilerParams(
            collective_id=collective_id,
            has_side_effects=True,
            vmem_limit_bytes=16 * 1024 * 1024,
        ),
        name="reduce",
    )(grad, plane_in)


def body(
    tokens,
    image_tokens,
    norm_gain,
    w_query,
    w_key,
    w_value,
    w_out,
    w_plane,
    dec_w1,
    dec_b1,
    dec_w2,
    dec_b2,
    dec_w3,
    dec_b3,
    corner_idx,
    corner_wts,
    target_color,
):
    own_tokens = tokens[0]
    model_width = own_tokens.shape[1]
    head_dim = model_width // HEADS
    size = lax.axis_size("seq")
    score_scale = math.log2(math.e) / math.sqrt(head_dim)
    queries, keys, values = front(
        own_tokens, image_tokens[0], w_query, w_key, w_value, size, score_scale, 0
    )
    plane_in, planes = attention(
        queries, keys, values, own_tokens, w_out, norm_gain, w_plane
    )
    planes = gather(planes, 1, size, 1)
    colors, grad = render_and_grad(
        corner_idx[0],
        corner_wts[0],
        planes,
        target_color[0],
        dec_w1,
        dec_b1,
        dec_w2,
        dec_b2,
        dec_w3,
        dec_b3,
    )
    own_grad, weight_grad = reduce_grads(grad, plane_in, size, lax.axis_size("dp"), 2)
    weight_grad = weight_grad.T
    token_grad = lax.dot_general(
        own_grad, w_plane, (((0,), (1,)), ((), ())), preferred_element_type=f32
    ).astype(bf16)
    return (colors[None], token_grad[None], weight_grad)


def solution(mesh):
    in_specs = (
        P("dp", "seq", None),
        P("dp", "seq", None),
        *(P() for _ in range(12)),
        P("dp", None, "seq"),
        P("dp", None, "seq"),
        P("dp", None, "seq"),
    )
    out_specs = (P("dp", None, "seq"), P("dp", "seq", None), P())
    return jax.shard_map(body, mesh=mesh, in_specs=in_specs, out_specs=out_specs, check_vma=False)
```

```python
import functools
import math

import jax
import jax.numpy as jnp
from jax import lax
from jax.experimental import pallas as pl
from jax.experimental.pallas import tpu as pltpu
from jax.sharding import PartitionSpec as P

HEADS = 16
STEPS = 128
PLANES = 3
LANES = 128
NORM_EPS = 1e-05
DEPTH_STEP = 0.02
VMEM_BYTES = 60000 * 1024

bf16 = jnp.bfloat16
f32 = jnp.float32


def in_vmem(count):
    return [pl.BlockSpec(memory_space=pltpu.VMEM)] * count


def plain_norm(inputs):
    row_mean = jnp.mean(inputs, axis=-1, keepdims=True)
    centred = inputs - row_mean
    row_var = jnp.mean(centred * centred, axis=-1, keepdims=True)
    return centred * lax.rsqrt(row_var + NORM_EPS)


def attention_kernel(
    q_ref,
    k_ref,
    v_ref,
    tokens_ref,
    w_out_ref,
    gain_ref,
    w_plane_ref,
    plane_in_ref,
    planes_ref,
    values_ref,
    scores_ref,
    maxes_ref,
    attended_ref,
    *,
    tile,
):
    rows, width = q_ref.shape
    count = k_ref.shape[0]
    pairs = width // LANES
    low = lax.broadcasted_iota(jnp.int32, (1, LANES), 1) < LANES // 2
    turned = (((1,), (1,)), ((), ()))

    def score(pair_id, head):
        span = pl.ds(pl.multiple_of(pair_id * LANES, LANES), LANES)
        own = jnp.where(low if head == 0 else ~low, q_ref[:, span], jnp.zeros((), bf16))
        scores = lax.dot_general(own, k_ref[:, span], turned, preferred_element_type=f32)
        scores_ref[head] = scores
        highest = scores[:, :LANES]
        for first in range(LANES, count, LANES):
            highest = jnp.maximum(highest, scores[:, first : first + LANES])
        maxes_ref[head] = highest

    def weigh(head):
        row_max = jnp.max(maxes_ref[head], axis=1, keepdims=True)
        terms = jnp.exp2(scores_ref[head] - row_max).astype(bf16)
        return jnp.dot(terms, values_ref[head], preferred_element_type=f32)

    score(0, 0)

    def pair(pair_id, carry):
        span = pl.ds(pl.multiple_of(pair_id * LANES, LANES), LANES)
        values = v_ref[:, span]
        one = jnp.ones((), bf16)
        values_ref[0] = jnp.where(low, values, one)
        values_ref[1] = jnp.where(low, one, values)
        score(pair_id, 1)
        first = weigh(0)
        score((pair_id + 1) % pairs, 0)
        second = weigh(1)
        row_sum = pltpu.roll(jnp.where(low, second, first), LANES // 2, 1)
        attended_ref[:, span] = (jnp.where(low, first, second) / row_sum).astype(bf16)
        return carry

    lax.fori_loop(0, pairs, pair, 0)

    def project(step, carry):
        span = pl.ds(pl.multiple_of(step * tile, tile), tile)
        mixed = tokens_ref[span, :].astype(f32) + jnp.dot(
            attended_ref[span, :], w_out_ref[...], preferred_element_type=f32
        )
        mixed = mixed.astype(bf16).astype(f32)
        plane_in = (plain_norm(mixed) * gain_ref[...]).astype(bf16)
        plane_in_ref[span, :] = plane_in
        planes_ref[:, span] = lax.dot_general(
            w_plane_ref[...], plane_in, turned, preferred_element_type=f32
        ).astype(bf16)
        return carry

    lax.fori_loop(0, rows // tile, project, 0)


def attention(queries, keys, values, tokens, w_out, gain, w_plane):
    rows, width = queries.shape
    count = values.shape[0]
    channels = w_plane.shape[1]
    return pl.pallas_call(
        functools.partial(attention_kernel, tile=256),
        out_shape=(
            jax.ShapeDtypeStruct((rows, width), bf16),
            jax.ShapeDtypeStruct((channels, rows), bf16),
        ),
        in_specs=in_vmem(7),
        out_specs=tuple(in_vmem(2)),
        scratch_shapes=[
            pltpu.VMEM((2, count, LANES), bf16),
            pltpu.VMEM((2, rows, count), f32),
            pltpu.VMEM((2, rows, LANES), f32),
            pltpu.VMEM((rows, width), bf16),
        ],
        compiler_params=pltpu.CompilerParams(vmem_limit_bytes=36 * 1024 * 1024),
        cost_estimate=pl.CostEstimate(
            flops=4 * rows * count * width,
            bytes_accessed=4 * (rows + count) * width,
            transcendentals=rows * count * HEADS,
        ),
        name="attention",
    )(queries, keys, values, tokens, w_out, gain[None, :], w_plane.T)


MESH_ID = pl.DeviceIdType.MESH


def greet(peers):
    barrier = pltpu.get_barrier_semaphore()
    for peer in peers:
        pl.semaphore_signal(barrier, inc=1, device_id=peer, device_id_type=MESH_ID)
    pl.semaphore_wait(barrier, len(peers))


def remote(source, target, send_sem, recv_sem, peer):
    return pltpu.make_async_remote_copy(
        src_ref=source,
        dst_ref=target,
        send_sem=send_sem,
        recv_sem=recv_sem,
        device_id=peer,
        device_id_type=MESH_ID,
    )


def partner_of(me):
    return me + 1 - 2 * (me % 2)


RING = 4
SENDS, ARRIVALS = 19, 10


class Exchange:
    def __init__(self, block_ref, out_ref, axis, sems):
        self.block, self.out, self.axis = block_ref, out_ref, axis
        self.send_sem, self.recv_sem, self.land_sem, self.own_sem = sems
        me = lax.axis_index("seq")
        self.me = me
        self.core = me % 2
        self.y = (me // 2) % 2
        self.x = me // 4
        self.extent = block_ref.shape[axis]
        self.started = []
        self.right = {"seq": self.at(1, 0)}
        self.left = {"seq": self.at(-1, 0)}
        self.over = {"seq": self.at(0, 1)}
        self.partner = {"seq": partner_of(me)}

    def at(self, dx, dy):
        return 4 * ((self.x + dx + RING) % RING) + 2 * ((self.y + dy) % 2) + self.core

    def place(self, owner, half=None):
        size = self.extent if half is None else self.extent // 2
        start = owner * self.extent + (0 if half is None else half * size)
        span = pl.ds(pl.multiple_of(start, size), size)
        return self.out.at[span, :] if self.axis == 0 else self.out.at[:, span]

    def push(self, source, owner, half, recv, peer):
        remote(
            source, self.place(owner, half), self.send_sem.at[len(self.started)], recv, peer
        ).start()
        self.started.append(half)

    def relay(self, owner, half, recv, peer):
        self.push(self.place(owner, half), owner, half, recv, peer)

    def hear(self, owner, half, sem):
        spot = self.place(owner, half)
        remote(spot, spot, self.send_sem.at[0], sem, self.partner).wait_recv()

    def begin(self):
        self.own = pltpu.make_async_copy(self.block, self.place(self.me), self.own_sem)
        self.own.start()
        recv, land = self.recv_sem, self.land_sem
        self.push(self.block, self.me, None, recv.at[0], self.right)
        self.push(self.block, self.me, None, recv.at[1], self.left)
        self.push(self.block, self.me, None, recv.at[2], self.over)
        self.push(self.block, self.me, None, land.at[9], self.partner)

    def arrive(self, number, dx, dy, half, onward):
        owner = self.at(dx, dy)
        self.hear(owner, half, self.recv_sem.at[number])
        for part, target, peer in onward:
            self.relay(owner, part, self.recv_sem.at[target], peer)
        self.relay(owner, half, self.land_sem.at[number], self.partner)

    def beside(self):
        self.arrive(0, -1, 0, None, [(0, 5, self.right)])
        self.arrive(1, 1, 0, None, [(1, 6, self.left)])

    def across(self):
        self.arrive(2, 0, 1, None, [(None, 3, self.right), (None, 4, self.left)])

    def opposite(self):
        self.arrive(5, 2, 0, 0, [])
        self.arrive(6, 2, 0, 1, [])

    def beside_across(self):
        self.arrive(3, -1, 1, None, [(0, 7, self.right)])
        self.arrive(4, 1, 1, None, [(1, 8, self.left)])

    def opposite_across(self):
        self.arrive(7, 2, 1, 0, [])
        self.arrive(8, 2, 1, 1, [])

    def handed(self, number, dx, dy, half):
        other = self.at(dx, dy) + 1 - 2 * self.core
        self.hear(other, half, self.land_sem.at[number])

    def finish(self):
        for number, half in enumerate(self.started):
            spot = self.place(self.me, half)
            remote(
                spot, spot, self.send_sem.at[number], self.recv_sem.at[0], self.partner
            ).wait_send()

    def neighbours(self):
        return [self.right, self.left, self.over, self.partner]


def exchange_sems():
    sems = pltpu.SemaphoreType.DMA
    return [sems((SENDS,)), sems((ARRIVALS,)), sems((ARRIVALS,)), sems]


def front_kernel(
    tokens_ref,
    image_ref,
    w_query_hbm,
    w_key_hbm,
    w_value_hbm,
    q_ref,
    k_ref,
    v_ref,
    images_ref,
    w_query_ref,
    w_key_ref,
    w_value_ref,
    load_sem,
    *sems,
    tile,
    scale,
):
    ring = Exchange(image_ref, images_ref, 0, sems)
    loads = []
    for number, (source, target) in enumerate(
        (
            (w_query_hbm, w_query_ref),
            (w_key_hbm, w_key_ref),
            (w_value_hbm, w_value_ref),
        )
    ):
        copy = pltpu.make_async_copy(source, target, load_sem.at[number])
        copy.start()
        loads.append(copy)
    greet(ring.neighbours())
    ring.begin()

    def query(step):
        span = pl.ds(step * tile, tile)
        normed = plain_norm(tokens_ref[span, :].astype(f32)).astype(bf16)
        product = jnp.dot(normed, w_query_ref[...], preferred_element_type=f32)
        q_ref[span, :] = (product * scale).astype(bf16)

    def keys_values(dx, dy):
        owner = ring.at(dx, dy) // 2
        rows = 2 * image_ref.shape[0]
        span = pl.ds(pl.multiple_of(owner * rows, rows), rows)
        images = images_ref[span, :]
        k_ref[span, :] = jnp.dot(
            images, w_key_ref[...], preferred_element_type=f32
        ).astype(bf16)
        v_ref[span, :] = jnp.dot(
            images, w_value_ref[...], preferred_element_type=f32
        ).astype(bf16)

    loads[0].wait()
    query(0)
    ring.beside()
    query(1)
    ring.across()
    query(2)
    ring.opposite()
    loads[1].wait()
    loads[2].wait()
    ring.own.wait()
    ring.handed(9, 0, 0, None)
    keys_values(0, 0)
    ring.beside_across()
    ring.handed(0, -1, 0, None)
    keys_values(-1, 0)
    ring.handed(1, 1, 0, None)
    keys_values(1, 0)
    ring.opposite_across()
    ring.handed(2, 0, 1, None)
    keys_values(0, 1)
    ring.handed(5, 2, 0, 0)
    ring.handed(6, 2, 0, 1)
    keys_values(2, 0)
    ring.handed(3, -1, 1, None)
    keys_values(-1, 1)
    ring.handed(4, 1, 1, None)
    keys_values(1, 1)
    ring.handed(7, 2, 1, 0)
    ring.handed(8, 2, 1, 1)
    keys_values(2, 1)
    ring.finish()


def front(tokens, images, w_query, w_key, w_value, size, scale, collective_id):
    rows, width = tokens.shape
    depth = images.shape[1]
    count = images.shape[0] * size
    heads = w_key.shape[1]
    return pl.pallas_call(
        functools.partial(front_kernel, tile=rows // 3, scale=scale),
        out_shape=(
            jax.ShapeDtypeStruct((rows, width), bf16),
            jax.ShapeDtypeStruct((count, heads), bf16),
            jax.ShapeDtypeStruct((count, heads), bf16),
        ),
        in_specs=in_vmem(2) + [pl.BlockSpec(memory_space=pltpu.HBM)] * 3,
        out_specs=tuple(in_vmem(3)),
        scratch_shapes=[
            pltpu.VMEM((count, depth), bf16),
            pltpu.VMEM(w_query.shape, bf16),
            pltpu.VMEM(w_key.shape, bf16),
            pltpu.VMEM(w_value.shape, bf16),
            pltpu.SemaphoreType.DMA((3,)),
            *exchange_sems(),
        ],
        compiler_params=pltpu.CompilerParams(
            collective_id=collective_id,
            has_side_effects=True,
            vmem_limit_bytes=24 * 1024 * 1024,
        ),
        name="front",
    )(tokens, images, w_query, w_key, w_value)


def table_rows(col_ref, row_ref, plane, first_row, row_count, start, width, side):
    span = pl.ds(start, width)
    pieces = side // 16
    upper = col_ref[2 * plane, :, span].reshape(pieces, 16, width)
    lower = col_ref[2 * plane + 1, :, span].reshape(pieces, 16, width)
    cell_row = row_ref[plane, :, span]
    zero = jnp.zeros((16, width), bf16)
    row_id = jnp.asarray(first_row, jnp.int32)
    before = cell_row == (row_id - 1).astype(bf16)
    blocks = []
    for step in range(row_count):
        here = cell_row == (row_id + step).astype(bf16)
        for piece in range(pieces):
            blocks.append(
                jnp.where(here, upper[piece], jnp.where(before, lower[piece], zero))
            )
        before = here
    return jnp.concatenate(blocks, axis=0)


def ray_scan(values, lane, reverse):
    width = values.shape[1]
    shift = 1
    while shift < STEPS:
        if reverse:
            moved = pltpu.roll(values, width - shift, 1)
            values = values + jnp.where(lane < STEPS - shift, moved, 0.0)
        else:
            moved = pltpu.roll(values, shift, 1)
            values = values + jnp.where(lane >= shift, moved, 0.0)
        shift *= 2
    return values


def column_of(row_ref):
    count = row_ref.shape[1]
    diagonal = lax.broadcasted_iota(jnp.int32, (count, count), 0) == lax.broadcasted_iota(
        jnp.int32, (count, count), 1
    )
    return jnp.sum(jnp.where(diagonal, row_ref[...], 0.0), axis=1, keepdims=True)


def token_rows(col_ref, row_ref, chip, start, width, side, grid_rows):
    blocks = []
    for group in range(grid_rows // 4):
        number = chip * (grid_rows // 4) + group
        plane = number // (side // 4)
        first = (number - plane * (side // 4)) * 4
        blocks.append(table_rows(col_ref, row_ref, plane, first, 4, start, width, side))
    return jnp.concatenate(blocks, axis=0)


def scene_kernel(
    block_ref,
    plane_in_ref,
    idx_ref,
    wts_ref,
    target_ref,
    w_plane_ref,
    w1_ref,
    b1_ref,
    w2_ref,
    b2_ref,
    w3_ref,
    b3_ref,
    colors_ref,
    token_grad_ref,
    total_ref,
    planes_ref,
    col_ref,
    row_ref,
    features_ref,
    fgrad_ref,
    z1_ref,
    z2_ref,
    decoded_ref,
    grad_ref,
    pair_ref,
    stage_ref,
    half_ref,
    side_ref,
    over_ref,
    part_ref,
    chunk_land_ref,
    chunk_ref,
    scene_ref,
    pair_send,
    pair_recv,
    half_send,
    half_recv,
    side_send,
    side_recv,
    over_send,
    over_recv,
    chunk_send,
    chunk_recv,
    scene_send,
    scene_recv,
    last_send,
    last_recv,
    *ring_sems,
    side,
    size,
    scenes,
    prep_width,
    width,
    tile,
):
    samples = idx_ref.shape[1]
    channels, tokens = planes_ref.shape
    extent = block_ref.shape[1]
    half_extent = extent // 2
    plane_size = side * side
    chip_tokens = 2 * extent
    grid_rows = chip_tokens // side
    chips = size // 2
    exact = lax.Precision.HIGHEST
    turned = (((1,), (1,)), ((), ()))
    flip = (((0,), (0,)), ((), ()))

    ring = Exchange(block_ref, planes_ref, 1, ring_sems)
    me, core = ring.me, ring.core
    scene = lax.axis_index("dp")
    others = [(me + step) % size for step in range(1, size)]
    other_scenes = [(scene + step) % scenes for step in range(1, scenes)]
    greet([{"seq": owner} for owner in others] + [{"dp": owner} for owner in other_scenes])
    ring.begin()

    def chip_at(dx, dy):
        return 2 * ((ring.x + dx) % RING) + (ring.y + dy) % 2

    def prepare(step, carry):
        start = pl.multiple_of(step * prep_width, prep_width)
        span = pl.ds(start, prep_width)
        index = idx_ref[:, span]
        weight = wts_ref[:, span].astype(f32)
        column_id = lax.broadcasted_iota(jnp.int32, (side, prep_width), 0)
        for plane in range(PLANES):
            in_plane = (index >= plane * plane_size) & (index < (plane + 1) * plane_size)
            base = jnp.min(jnp.where(in_plane, index, tokens), axis=0, keepdims=True)
            corner = []
            for offset in (0, 1, side, side + 1):
                corner.append(
                    jnp.sum(
                        jnp.where(index == base + offset, weight, 0.0), axis=0, keepdims=True
                    )
                )
            local = base - plane * plane_size
            cell_row = local // side
            column = local - cell_row * side
            for which in range(2):
                col_ref[2 * plane + which, :, span] = jnp.where(
                    column_id == column,
                    corner[2 * which],
                    jnp.where(column_id == column + 1, corner[2 * which + 1], 0.0),
                ).astype(bf16)
            row_ref[plane, :, span] = jnp.broadcast_to(
                cell_row.astype(f32), (16, prep_width)
            ).astype(bf16)
        return carry

    lax.fori_loop(0, samples // prep_width, prepare, 0)

    w1, w2, w3 = w1_ref[...], w2_ref[...], w3_ref[...]
    b1, b2, b3 = column_of(b1_ref), column_of(b2_ref), column_of(b3_ref)
    features_ref[...] = jnp.zeros_like(features_ref)

    arrivals = (
        (ring.beside, ((9, 0, 0, None),)),
        (ring.across, ((1, 1, 0, None),)),
        (ring.beside_across, ((0, -1, 0, None),)),
        (ring.opposite, ((5, 2, 0, 0), (6, 2, 0, 1))),
        (ring.opposite_across, ((2, 0, 1, None),)),
        (None, ((4, 1, 1, None),)),
        (None, ((3, -1, 1, None),)),
        (None, ((7, 2, 1, 0), (8, 2, 1, 1))),
    )

    def interpolate(step, carry):
        for number, (receive, handed) in enumerate(arrivals):

            @pl.when(step == number)
            def _(number=number, receive=receive, handed=handed):
                if receive is not None:
                    receive()
                if number == 0:
                    ring.own.wait()
                for item in handed:
                    ring.handed(*item)

        place = step % 4
        chip = chip_at(place + place // 2 - 2 * (place // 3), step // 4)
        block = pl.ds(pl.multiple_of(chip * chip_tokens, chip_tokens), chip_tokens)

        def add(part, inner):
            start = pl.multiple_of(part * width, width)
            span = pl.ds(start, width)
            table = token_rows(col_ref, row_ref, chip, start, width, side, grid_rows)
            features_ref[:, span] = features_ref[:, span] + jnp.dot(
                planes_ref[:, block], table, preferred_element_type=f32
            )
            return inner

        lax.fori_loop(0, samples // width, add, 0)
        return carry

    lax.fori_loop(0, chips, interpolate, 0)

    def decode(step, carry):
        span = pl.ds(pl.multiple_of(step * prep_width, prep_width), prep_width)
        z1 = jnp.dot(w1, features_ref[:, span].astype(bf16), preferred_element_type=f32) + b1
        z1_ref[:, span] = z1
        h1 = (z1 * jax.nn.sigmoid(z1)).astype(bf16)
        z2 = jnp.dot(w2, h1, preferred_element_type=f32) + b2
        z2_ref[:, span] = z2
        h2 = (z2 * jax.nn.sigmoid(z2)).astype(bf16)
        decoded_ref[:, span] = jnp.dot(w3, h2, preferred_element_type=f32) + b3
        return carry

    lax.fori_loop(0, samples // prep_width, decode, 0)

    rays = samples // STEPS
    lane = lax.broadcasted_iota(jnp.int32, (1, samples), 1) % STEPS
    density = decoded_ref[0:1]
    optical = (jnp.maximum(density, 0.0) + jnp.log1p(jnp.exp(-jnp.abs(density)))) * DEPTH_STEP
    albedo = jax.nn.sigmoid(decoded_ref[1:4])
    reach = jnp.exp(optical - ray_scan(optical, lane, False))
    passed = jnp.exp(-optical)
    weight = reach * (1.0 - passed)
    spread = (
        lax.broadcasted_iota(jnp.int32, (rays, samples), 0)
        == lax.broadcasted_iota(jnp.int32, (rays, samples), 1) // STEPS
    ).astype(f32)
    colors = lax.dot_general(
        weight * albedo, spread, turned, precision=exact, preferred_element_type=f32
    )
    colors_ref[...] = colors
    miss = jnp.dot(
        colors - target_ref[...], spread, precision=exact, preferred_element_type=f32
    )
    weight_grad = jnp.sum(miss * albedo, axis=0, keepdims=True)
    term = weight_grad * weight
    later = ray_scan(term, lane, True) - term
    optical_grad = weight_grad * reach * passed - later
    decoded_ref[0:1] = optical_grad * (DEPTH_STEP * jax.nn.sigmoid(density))
    decoded_ref[1:4] = miss * weight * albedo * (1.0 - albedo)

    def silu_grad(pre):
        gate = jax.nn.sigmoid(pre)
        return gate * (1.0 + pre * (1.0 - gate))

    def decode_back(step, carry):
        span = pl.ds(pl.multiple_of(step * prep_width, prep_width), prep_width)
        g2 = lax.dot_general(
            w3, decoded_ref[:, span].astype(bf16), flip, preferred_element_type=f32
        )
        g2 = g2.astype(bf16).astype(f32) * silu_grad(z2_ref[:, span])
        g1 = lax.dot_general(w2, g2.astype(bf16), flip, preferred_element_type=f32)
        g1 = g1.astype(bf16).astype(f32) * silu_grad(z1_ref[:, span])
        fgrad_ref[:, span] = lax.dot_general(
            w1, g1.astype(bf16), flip, preferred_element_type=f32
        ).astype(bf16)
        return carry

    lax.fori_loop(0, samples // prep_width, decode_back, 0)

    def own_part(number):
        return grad_ref[number, :, pl.ds(pl.multiple_of(core * extent, extent), extent)]

    def swap(number, step):
        return remote(
            grad_ref.at[
                step, :, pl.ds(pl.multiple_of((1 - core) * extent, extent), extent)
            ],
            pair_ref.at[step],
            pair_send.at[number],
            pair_recv.at[number],
            ring.partner,
        )

    def push_half(way, row, number):
        part = pl.ds(way * half_extent, half_extent)
        return remote(
            stage_ref.at[number, :, part],
            half_ref.at[way, row],
            half_send.at[way, row],
            half_recv.at[way, row],
            ring.right if way == 0 else ring.left,
        )

    def push_side(way, row, number):
        return remote(
            stage_ref.at[number],
            side_ref.at[way, row],
            side_send.at[way, row],
            side_recv.at[way, row],
            ring.right if way == 0 else ring.left,
        )

    def push_over(number):
        return remote(stage_ref.at[number], over_ref, over_send, over_recv, ring.over)

    def stage(number):
        swap(number, number).wait_recv()
        row = 1 - number // 4
        kind = number % 4
        both = own_part(number).astype(f32) + pair_ref[number].astype(f32)
        if kind == 0:
            stage_ref[number] = both.astype(bf16)
            push_half(0, row, number).start()
            push_half(1, row, number).start()
        elif kind < 3:
            way = kind - 1
            push_half(way, row, number).wait_recv()
            part = pl.ds(way * half_extent, half_extent)
            stage_ref[number] = both.astype(bf16)
            first = way * half_extent
            stage_ref[number, :, part] = (
                both[:, first : first + half_extent] + half_ref[way, row].astype(f32)
            ).astype(bf16)
            push_side(way, row, number).start()
        else:
            for way in range(2):
                push_side(way, row, number).wait_recv()
                both = both + side_ref[way, row].astype(f32)
            if row == 1:
                stage_ref[number] = both.astype(bf16)
                push_over(number).start()
        return both

    def spread_back(step, carry):
        place = step % 4
        across = 2 + 3 * place + 3 * (place // 2) + 2 * (place // 3)
        chip = chip_at(across, 1 - step // 4)
        table = token_rows(col_ref, row_ref, chip, 0, samples, side, grid_rows)
        grad_ref[step] = lax.dot_general(
            fgrad_ref[...], table, turned, preferred_element_type=f32
        ).astype(bf16)
        swap(step, step).start()
        for number in range(chips - 1):

            @pl.when(step == number + 1)
            def _(number=number):
                stage(number)

        return carry

    lax.fori_loop(0, chips, spread_back, 0)
    both = stage(chips - 1)
    push_over(3).wait_recv()
    own_grad = (both + over_ref[...].astype(f32)).astype(bf16)

    rows, lanes = chunk_ref.shape

    def chunk_of(owner):
        return (
            pl.ds(pl.multiple_of((owner % 2) * rows, rows), rows),
            pl.ds(pl.multiple_of((owner // 2) * lanes, lanes), lanes),
        )

    part_ref[...] = jnp.dot(own_grad, plane_in_ref[...], preferred_element_type=f32)
    waiting = []
    for owner in others:
        copy = remote(
            part_ref.at[chunk_of(owner)],
            chunk_land_ref.at[me],
            chunk_send.at[owner],
            chunk_recv.at[me],
            {"seq": owner},
        )
        copy.start()
        waiting.append(copy)
    for first in range(0, extent, tile):
        token_grad_ref[first : first + tile, :] = lax.dot_general(
            own_grad[:, first : first + tile],
            w_plane_ref[...],
            flip,
            preferred_element_type=f32,
        ).astype(bf16)
    chunk = part_ref[chunk_of(me)]
    for owner in others:
        remote(
            chunk_ref,
            chunk_land_ref.at[owner],
            chunk_send.at[owner],
            chunk_recv.at[owner],
            ring.partner,
        ).wait_recv()
        chunk = chunk + chunk_land_ref[owner]
    chunk_ref[...] = chunk
    scene_ref[scene] = chunk
    for other in other_scenes:
        copy = remote(
            chunk_ref,
            scene_ref.at[scene],
            scene_send.at[other],
            scene_recv.at[scene],
            {"dp": other},
        )
        copy.start()
        waiting.append(copy)
    for other in other_scenes:
        remote(
            chunk_ref,
            scene_ref.at[other],
            scene_send.at[other],
            scene_recv.at[other],
            ring.partner,
        ).wait_recv()
    final = scene_ref[0]
    for other in range(1, scenes):
        final = final + scene_ref[other]
    spot = chunk_of(me)
    total_ref[spot] = final
    for owner in others:
        copy = remote(
            total_ref.at[spot],
            total_ref.at[spot],
            last_send.at[owner],
            last_recv.at[me],
            {"seq": owner},
        )
        copy.start()
        waiting.append(copy)
    for owner in others:
        there = chunk_of(owner)
        remote(
            total_ref.at[there],
            total_ref.at[there],
            last_send.at[owner],
            last_recv.at[owner],
            ring.partner,
        ).wait_recv()
    for copy in waiting:
        copy.wait_send()
    for number in range(chips):
        swap(number, number).wait_send()
    for row in range(2):
        base = 4 * (1 - row)
        for way in range(2):
            push_half(way, row, base).wait_send()
            push_side(way, row, base + 1 + way).wait_send()
    push_over(3).wait_send()
    ring.finish()


def render_scene(
    block,
    plane_in,
    index,
    weight,
    target,
    w_plane,
    w1,
    b1,
    w2,
    b2,
    w3,
    b3,
    size,
    scenes,
    collective_id,
):
    channels, extent = block.shape
    width = plane_in.shape[1]
    samples = index.shape[1]
    tokens = extent * size
    side = math.isqrt(tokens // PLANES)
    chips = size // 2
    rows, lanes = channels // 2, width // chips
    sems = pltpu.SemaphoreType.DMA
    return pl.pallas_call(
        functools.partial(
            scene_kernel,
            side=side,
            size=size,
            scenes=scenes,
            prep_width=1024,
            width=1024,
            tile=256,
        ),
        out_shape=(
            jax.ShapeDtypeStruct(target.shape, f32),
            jax.ShapeDtypeStruct((extent, width), bf16),
            jax.ShapeDtypeStruct((channels, width), f32),
        ),
        in_specs=in_vmem(12),
        out_specs=tuple(in_vmem(3)),
        scratch_shapes=[
            pltpu.VMEM((channels, tokens), bf16),
            pltpu.VMEM((2 * PLANES, side, samples), bf16),
            pltpu.VMEM((PLANES, 16, samples), bf16),
            pltpu.VMEM((channels, samples), f32),
            pltpu.VMEM((channels, samples), bf16),
            pltpu.VMEM((w1.shape[0], samples), f32),
            pltpu.VMEM((w2.shape[0], samples), f32),
            pltpu.VMEM((w3.shape[0], samples), f32),
            pltpu.VMEM((chips, channels, 2 * extent), bf16),
            pltpu.VMEM((chips, channels, extent), bf16),
            pltpu.VMEM((chips, channels, extent), bf16),
            pltpu.VMEM((2, 2, channels, extent // 2), bf16),
            pltpu.VMEM((2, 2, channels, extent), bf16),
            pltpu.VMEM((channels, extent), bf16),
            pltpu.VMEM((channels, width), f32),
            pltpu.VMEM((size, rows, lanes), f32),
            pltpu.VMEM((rows, lanes), f32),
            pltpu.VMEM((scenes, rows, lanes), f32),
            sems((chips,)),
            sems((chips,)),
            sems((2, 2)),
            sems((2, 2)),
            sems((2, 2)),
            sems((2, 2)),
            sems,
            sems,
            sems((size,)),
            sems((size,)),
            sems((scenes,)),
            sems((scenes,)),
            sems((size,)),
            sems((size,)),
            *exchange_sems(),
        ],
        compiler_params=pltpu.CompilerParams(
            collective_id=collective_id,
            has_side_effects=True,
            vmem_limit_bytes=52 * 1024 * 1024,
        ),
        name="scene",
    )(
        block,
        plane_in,
        index,
        weight,
        target,
        w_plane.T,
        w1,
        b1[None, :],
        w2,
        b2[None, :],
        w3,
        b3[None, :],
    )


def body(
    tokens,
    image_tokens,
    norm_gain,
    w_query,
    w_key,
    w_value,
    w_out,
    w_plane,
    dec_w1,
    dec_b1,
    dec_w2,
    dec_b2,
    dec_w3,
    dec_b3,
    corner_idx,
    corner_wts,
    target_color,
):
    own_tokens = tokens[0]
    model_width = own_tokens.shape[1]
    head_dim = model_width // HEADS
    size = lax.axis_size("seq")
    score_scale = math.log2(math.e) / math.sqrt(head_dim)
    queries, keys, values = front(
        own_tokens, image_tokens[0], w_query, w_key, w_value, size, score_scale, 0
    )
    plane_in, planes = attention(
        queries, keys, values, own_tokens, w_out, norm_gain, w_plane
    )
    colors, token_grad, weight_grad = render_scene(
        planes,
        plane_in,
        corner_idx[0],
        corner_wts[0],
        target_color[0],
        w_plane,
        dec_w1,
        dec_b1,
        dec_w2,
        dec_b2,
        dec_w3,
        dec_b3,
        size,
        lax.axis_size("dp"),
        1,
    )
    return (colors[None], token_grad[None], weight_grad.T)


def solution(mesh):
    in_specs = (
        P("dp", "seq", None),
        P("dp", "seq", None),
        *(P() for _ in range(12)),
        P("dp", None, "seq"),
        P("dp", None, "seq"),
        P("dp", None, "seq"),
    )
    out_specs = (P("dp", None, "seq"), P("dp", "seq", None), P())
    return jax.shard_map(body, mesh=mesh, in_specs=in_specs, out_specs=out_specs, check_vma=False)
```

```python
import functools
import math

import jax
import jax.numpy as jnp
from jax import lax
from jax.experimental import pallas as pl
from jax.experimental.pallas import tpu as pltpu
from jax.sharding import PartitionSpec as P

HEADS = 16
STEPS = 128
PLANES = 3
LANES = 128
NORM_EPS = 1e-05
DEPTH_STEP = 0.02
VMEM_BYTES = 60000 * 1024

bf16 = jnp.bfloat16
f32 = jnp.float32


def in_vmem(count):
    return [pl.BlockSpec(memory_space=pltpu.VMEM)] * count


def plain_norm(inputs):
    row_mean = jnp.mean(inputs, axis=-1, keepdims=True)
    centred = inputs - row_mean
    row_var = jnp.mean(centred * centred, axis=-1, keepdims=True)
    return centred * lax.rsqrt(row_var + NORM_EPS)


def attention_kernel(
    q_ref,
    k_ref,
    v_ref,
    tokens_ref,
    w_out_ref,
    gain_ref,
    w_plane_ref,
    plane_in_ref,
    planes_ref,
    values_ref,
    scores_ref,
    maxes_ref,
    attended_ref,
    *,
    tile,
):
    rows, width = q_ref.shape
    count = k_ref.shape[0]
    pairs = width // LANES
    low = lax.broadcasted_iota(jnp.int32, (1, LANES), 1) < LANES // 2
    turned = (((1,), (1,)), ((), ()))

    def score(pair_id, head):
        span = pl.ds(pl.multiple_of(pair_id * LANES, LANES), LANES)
        own = jnp.where(low if head == 0 else ~low, q_ref[:, span], jnp.zeros((), bf16))
        scores = lax.dot_general(own, k_ref[:, span], turned, preferred_element_type=f32)
        scores_ref[head] = scores
        highest = scores[:, :LANES]
        for first in range(LANES, count, LANES):
            highest = jnp.maximum(highest, scores[:, first : first + LANES])
        maxes_ref[head] = highest

    def weigh(head):
        row_max = jnp.max(maxes_ref[head], axis=1, keepdims=True)
        terms = jnp.exp2(scores_ref[head] - row_max).astype(bf16)
        return jnp.dot(terms, values_ref[head], preferred_element_type=f32)

    score(0, 0)

    def pair(pair_id, carry):
        span = pl.ds(pl.multiple_of(pair_id * LANES, LANES), LANES)
        values = v_ref[:, span]
        one = jnp.ones((), bf16)
        values_ref[0] = jnp.where(low, values, one)
        values_ref[1] = jnp.where(low, one, values)
        score(pair_id, 1)
        first = weigh(0)
        score((pair_id + 1) % pairs, 0)
        second = weigh(1)
        row_sum = pltpu.roll(jnp.where(low, second, first), LANES // 2, 1)
        attended_ref[:, span] = (jnp.where(low, first, second) / row_sum).astype(bf16)
        return carry

    lax.fori_loop(0, pairs, pair, 0)

    def project(step, carry):
        span = pl.ds(pl.multiple_of(step * tile, tile), tile)
        mixed = tokens_ref[span, :].astype(f32) + jnp.dot(
            attended_ref[span, :], w_out_ref[...], preferred_element_type=f32
        )
        mixed = mixed.astype(bf16).astype(f32)
        plane_in = (plain_norm(mixed) * gain_ref[...]).astype(bf16)
        plane_in_ref[span, :] = plane_in
        planes_ref[:, span] = lax.dot_general(
            w_plane_ref[...], plane_in, turned, preferred_element_type=f32
        ).astype(bf16)
        return carry

    lax.fori_loop(0, rows // tile, project, 0)


def attention(queries, keys, values, tokens, w_out, gain, w_plane):
    rows, width = queries.shape
    count = values.shape[0]
    channels = w_plane.shape[1]
    return pl.pallas_call(
        functools.partial(attention_kernel, tile=256),
        out_shape=(
            jax.ShapeDtypeStruct((rows, width), bf16),
            jax.ShapeDtypeStruct((channels, rows), bf16),
        ),
        in_specs=in_vmem(7),
        out_specs=tuple(in_vmem(2)),
        scratch_shapes=[
            pltpu.VMEM((2, count, LANES), bf16),
            pltpu.VMEM((2, rows, count), f32),
            pltpu.VMEM((2, rows, LANES), f32),
            pltpu.VMEM((rows, width), bf16),
        ],
        compiler_params=pltpu.CompilerParams(vmem_limit_bytes=36 * 1024 * 1024),
        cost_estimate=pl.CostEstimate(
            flops=4 * rows * count * width,
            bytes_accessed=4 * (rows + count) * width,
            transcendentals=rows * count * HEADS,
        ),
        name="attention",
    )(queries, keys, values, tokens, w_out, gain[None, :], w_plane.T)


MESH_ID = pl.DeviceIdType.MESH


def greet(peers):
    barrier = pltpu.get_barrier_semaphore()
    for peer in peers:
        pl.semaphore_signal(barrier, inc=1, device_id=peer, device_id_type=MESH_ID)
    pl.semaphore_wait(barrier, len(peers))


def remote(source, target, send_sem, recv_sem, peer):
    return pltpu.make_async_remote_copy(
        src_ref=source,
        dst_ref=target,
        send_sem=send_sem,
        recv_sem=recv_sem,
        device_id=peer,
        device_id_type=MESH_ID,
    )


def partner_of(me):
    return me + 1 - 2 * (me % 2)


RING = 4
SENDS, ARRIVALS = 19, 10


class Exchange:
    def __init__(self, block_ref, out_ref, axis, sems):
        self.block, self.out, self.axis = block_ref, out_ref, axis
        self.send_sem, self.recv_sem, self.land_sem, self.own_sem = sems
        me = lax.axis_index("seq")
        self.me = me
        self.core = me % 2
        self.y = (me // 2) % 2
        self.x = me // 4
        self.extent = block_ref.shape[axis]
        self.started = []
        self.right = {"seq": self.at(1, 0)}
        self.left = {"seq": self.at(-1, 0)}
        self.over = {"seq": self.at(0, 1)}
        self.partner = {"seq": partner_of(me)}

    def at(self, dx, dy):
        return 4 * ((self.x + dx + RING) % RING) + 2 * ((self.y + dy) % 2) + self.core

    def place(self, owner, half=None):
        size = self.extent if half is None else self.extent // 2
        start = owner * self.extent + (0 if half is None else half * size)
        span = pl.ds(pl.multiple_of(start, size), size)
        return self.out.at[span, :] if self.axis == 0 else self.out.at[:, span]

    def push(self, source, owner, half, recv, peer):
        remote(
            source, self.place(owner, half), self.send_sem.at[len(self.started)], recv, peer
        ).start()
        self.started.append(half)

    def relay(self, owner, half, recv, peer):
        self.push(self.place(owner, half), owner, half, recv, peer)

    def hear(self, owner, half, sem):
        spot = self.place(owner, half)
        remote(spot, spot, self.send_sem.at[0], sem, self.partner).wait_recv()

    def begin(self):
        self.own = pltpu.make_async_copy(self.block, self.place(self.me), self.own_sem)
        self.own.start()
        recv, land = self.recv_sem, self.land_sem
        self.push(self.block, self.me, None, recv.at[0], self.right)
        self.push(self.block, self.me, None, recv.at[1], self.left)
        self.push(self.block, self.me, None, recv.at[2], self.over)
        self.push(self.block, self.me, None, land.at[9], self.partner)

    def arrive(self, number, dx, dy, half, onward):
        owner = self.at(dx, dy)
        self.hear(owner, half, self.recv_sem.at[number])
        for part, target, peer in onward:
            self.relay(owner, part, self.recv_sem.at[target], peer)
        self.relay(owner, half, self.land_sem.at[number], self.partner)

    def beside(self):
        self.arrive(0, -1, 0, None, [(0, 5, self.right)])
        self.arrive(1, 1, 0, None, [(1, 6, self.left)])

    def across(self):
        self.arrive(2, 0, 1, None, [(None, 3, self.right), (None, 4, self.left)])

    def opposite(self):
        self.arrive(5, 2, 0, 0, [])
        self.arrive(6, 2, 0, 1, [])

    def beside_across(self):
        self.arrive(3, -1, 1, None, [(0, 7, self.right)])
        self.arrive(4, 1, 1, None, [(1, 8, self.left)])

    def opposite_across(self):
        self.arrive(7, 2, 1, 0, [])
        self.arrive(8, 2, 1, 1, [])

    def handed(self, number, dx, dy, half):
        other = self.at(dx, dy) + 1 - 2 * self.core
        self.hear(other, half, self.land_sem.at[number])

    def finish(self):
        for number, half in enumerate(self.started):
            spot = self.place(self.me, half)
            remote(
                spot, spot, self.send_sem.at[number], self.recv_sem.at[0], self.partner
            ).wait_send()

    def neighbours(self):
        return [self.right, self.left, self.over, self.partner]


def exchange_sems():
    sems = pltpu.SemaphoreType.DMA
    return [sems((SENDS,)), sems((ARRIVALS,)), sems((ARRIVALS,)), sems]


def front_kernel(
    tokens_hbm,
    image_hbm,
    w_query_hbm,
    w_key_hbm,
    w_value_hbm,
    q_ref,
    k_ref,
    v_ref,
    tokens_ref,
    image_ref,
    images_ref,
    w_query_ref,
    w_key_ref,
    w_value_ref,
    load_sem,
    *sems,
    tile,
    scale,
):
    ring = Exchange(image_ref, images_ref, 0, sems)
    loads = []
    for number, (source, target) in enumerate(
        (
            (image_hbm, image_ref),
            (tokens_hbm, tokens_ref),
            (w_query_hbm, w_query_ref),
            (w_key_hbm, w_key_ref),
            (w_value_hbm, w_value_ref),
        )
    ):
        copy = pltpu.make_async_copy(source, target, load_sem.at[number])
        copy.start()
        loads.append(copy)
    greet(ring.neighbours())
    loads[0].wait()
    ring.begin()

    def query(step):
        span = pl.ds(step * tile, tile)
        normed = plain_norm(tokens_ref[span, :].astype(f32)).astype(bf16)
        product = jnp.dot(normed, w_query_ref[...], preferred_element_type=f32)
        q_ref[span, :] = (product * scale).astype(bf16)

    def keys_values(dx, dy):
        owner = ring.at(dx, dy) // 2
        rows = 2 * image_ref.shape[0]
        span = pl.ds(pl.multiple_of(owner * rows, rows), rows)
        images = images_ref[span, :]
        k_ref[span, :] = jnp.dot(
            images, w_key_ref[...], preferred_element_type=f32
        ).astype(bf16)
        v_ref[span, :] = jnp.dot(
            images, w_value_ref[...], preferred_element_type=f32
        ).astype(bf16)

    loads[1].wait()
    loads[2].wait()
    query(0)
    query(1)
    ring.beside()
    query(2)
    ring.across()
    loads[3].wait()
    loads[4].wait()
    ring.own.wait()
    ring.handed(9, 0, 0, None)
    keys_values(0, 0)
    ring.handed(0, -1, 0, None)
    keys_values(-1, 0)
    ring.handed(1, 1, 0, None)
    keys_values(1, 0)
    ring.opposite()
    ring.handed(2, 0, 1, None)
    keys_values(0, 1)
    ring.handed(5, 2, 0, 0)
    ring.handed(6, 2, 0, 1)
    keys_values(2, 0)
    ring.beside_across()
    ring.handed(3, -1, 1, None)
    keys_values(-1, 1)
    ring.handed(4, 1, 1, None)
    keys_values(1, 1)
    ring.opposite_across()
    ring.handed(7, 2, 1, 0)
    ring.handed(8, 2, 1, 1)
    keys_values(2, 1)
    ring.finish()


def front(tokens, images, w_query, w_key, w_value, size, scale, collective_id):
    rows, width = tokens.shape
    depth = images.shape[1]
    count = images.shape[0] * size
    heads = w_key.shape[1]
    return pl.pallas_call(
        functools.partial(front_kernel, tile=rows // 3, scale=scale),
        out_shape=(
            jax.ShapeDtypeStruct((rows, width), bf16),
            jax.ShapeDtypeStruct((count, heads), bf16),
            jax.ShapeDtypeStruct((count, heads), bf16),
        ),
        in_specs=[pl.BlockSpec(memory_space=pltpu.HBM)] * 5,
        out_specs=tuple(in_vmem(3)),
        scratch_shapes=[
            pltpu.VMEM(tokens.shape, bf16),
            pltpu.VMEM(images.shape, bf16),
            pltpu.VMEM((count, depth), bf16),
            pltpu.VMEM(w_query.shape, bf16),
            pltpu.VMEM(w_key.shape, bf16),
            pltpu.VMEM(w_value.shape, bf16),
            pltpu.SemaphoreType.DMA((5,)),
            *exchange_sems(),
        ],
        compiler_params=pltpu.CompilerParams(
            collective_id=collective_id,
            has_side_effects=True,
            vmem_limit_bytes=24 * 1024 * 1024,
        ),
        name="front",
    )(
        *(
            pltpu.with_memory_space_constraint(array, pltpu.HBM)
            for array in (tokens, images, w_query, w_key, w_value)
        )
    )


def table_rows(col_ref, row_ref, plane, first_row, row_count, start, width, side):
    span = pl.ds(start, width)
    pieces = side // 16
    upper = col_ref[2 * plane, :, span].reshape(pieces, 16, width)
    lower = col_ref[2 * plane + 1, :, span].reshape(pieces, 16, width)
    cell_row = row_ref[plane, :, span]
    zero = jnp.zeros((16, width), bf16)
    row_id = jnp.asarray(first_row, jnp.int32)
    before = cell_row == (row_id - 1).astype(bf16)
    blocks = []
    for step in range(row_count):
        here = cell_row == (row_id + step).astype(bf16)
        for piece in range(pieces):
            blocks.append(
                jnp.where(here, upper[piece], jnp.where(before, lower[piece], zero))
            )
        before = here
    return jnp.concatenate(blocks, axis=0)


def ray_scan(values, lane, reverse):
    width = values.shape[1]
    shift = 1
    while shift < STEPS:
        if reverse:
            moved = pltpu.roll(values, width - shift, 1)
            values = values + jnp.where(lane < STEPS - shift, moved, 0.0)
        else:
            moved = pltpu.roll(values, shift, 1)
            values = values + jnp.where(lane >= shift, moved, 0.0)
        shift *= 2
    return values


def column_of(row_ref):
    count = row_ref.shape[1]
    diagonal = lax.broadcasted_iota(jnp.int32, (count, count), 0) == lax.broadcasted_iota(
        jnp.int32, (count, count), 1
    )
    return jnp.sum(jnp.where(diagonal, row_ref[...], 0.0), axis=1, keepdims=True)


def token_rows(col_ref, row_ref, chip, start, width, side, grid_rows):
    blocks = []
    for group in range(grid_rows // 4):
        number = chip * (grid_rows // 4) + group
        plane = number // (side // 4)
        first = (number - plane * (side // 4)) * 4
        blocks.append(table_rows(col_ref, row_ref, plane, first, 4, start, width, side))
    return jnp.concatenate(blocks, axis=0)


def scene_kernel(
    block_ref,
    plane_in_ref,
    idx_ref,
    wts_ref,
    target_ref,
    w_plane_ref,
    w1_ref,
    b1_ref,
    w2_ref,
    b2_ref,
    w3_ref,
    b3_ref,
    colors_ref,
    token_grad_ref,
    total_ref,
    planes_ref,
    col_ref,
    row_ref,
    features_ref,
    fgrad_ref,
    z1_ref,
    z2_ref,
    decoded_ref,
    give_ref,
    keep_ref,
    pair_ref,
    stage_ref,
    half_ref,
    side_ref,
    over_ref,
    part_ref,
    chunk_land_ref,
    chunk_ref,
    scene_ref,
    pair_send,
    pair_recv,
    half_send,
    half_recv,
    side_send,
    side_recv,
    over_send,
    over_recv,
    chunk_send,
    chunk_recv,
    scene_send,
    scene_recv,
    last_send,
    last_recv,
    *ring_sems,
    side,
    size,
    scenes,
    prep_width,
    width,
    tile,
):
    samples = idx_ref.shape[1]
    channels, tokens = planes_ref.shape
    extent = block_ref.shape[1]
    half_extent = extent // 2
    plane_size = side * side
    chip_tokens = 2 * extent
    grid_rows = chip_tokens // side
    chips = size // 2
    exact = lax.Precision.HIGHEST
    turned = (((1,), (1,)), ((), ()))
    flip = (((0,), (0,)), ((), ()))

    ring = Exchange(block_ref, planes_ref, 1, ring_sems)
    me, core = ring.me, ring.core
    scene = lax.axis_index("dp")
    others = [(me + step) % size for step in range(1, size)]
    other_scenes = [(scene + step) % scenes for step in range(1, scenes)]
    greet([{"seq": owner} for owner in others] + [{"dp": owner} for owner in other_scenes])
    ring.begin()

    def chip_at(dx, dy):
        return 2 * ((ring.x + dx) % RING) + (ring.y + dy) % 2

    def prepare(step, carry):
        start = pl.multiple_of(step * prep_width, prep_width)
        span = pl.ds(start, prep_width)
        index = idx_ref[:, span]
        weight = wts_ref[:, span].astype(f32)
        column_id = lax.broadcasted_iota(jnp.int32, (side, prep_width), 0)
        for plane in range(PLANES):
            in_plane = (index >= plane * plane_size) & (index < (plane + 1) * plane_size)
            base = jnp.min(jnp.where(in_plane, index, tokens), axis=0, keepdims=True)
            corner = []
            for offset in (0, 1, side, side + 1):
                corner.append(
                    jnp.sum(
                        jnp.where(index == base + offset, weight, 0.0), axis=0, keepdims=True
                    )
                )
            local = base - plane * plane_size
            cell_row = local // side
            column = local - cell_row * side
            for which in range(2):
                col_ref[2 * plane + which, :, span] = jnp.where(
                    column_id == column,
                    corner[2 * which],
                    jnp.where(column_id == column + 1, corner[2 * which + 1], 0.0),
                ).astype(bf16)
            row_ref[plane, :, span] = jnp.broadcast_to(
                cell_row.astype(f32), (16, prep_width)
            ).astype(bf16)
        return carry

    lax.fori_loop(0, samples // prep_width, prepare, 0)

    w1, w2, w3 = w1_ref[...], w2_ref[...], w3_ref[...]
    b1, b2, b3 = column_of(b1_ref), column_of(b2_ref), column_of(b3_ref)
    features_ref[...] = jnp.zeros_like(features_ref)

    arrivals = (
        (ring.beside, ((9, 0, 0, None),)),
        (ring.across, ((1, 1, 0, None),)),
        (ring.beside_across, ((0, -1, 0, None),)),
        (ring.opposite, ((5, 2, 0, 0), (6, 2, 0, 1))),
        (ring.opposite_across, ((2, 0, 1, None),)),
        (None, ((4, 1, 1, None),)),
        (None, ((3, -1, 1, None),)),
        (None, ((7, 2, 1, 0), (8, 2, 1, 1))),
    )

    def interpolate(step, carry):
        for number, (receive, handed) in enumerate(arrivals):

            @pl.when(step == number)
            def _(number=number, receive=receive, handed=handed):
                if receive is not None:
                    receive()
                if number == 0:
                    ring.own.wait()
                for item in handed:
                    ring.handed(*item)

        place = step % 4
        chip = chip_at(place + place // 2 - 2 * (place // 3), step // 4)
        block = pl.ds(pl.multiple_of(chip * chip_tokens, chip_tokens), chip_tokens)

        def add(part, inner):
            start = pl.multiple_of(part * width, width)
            span = pl.ds(start, width)
            table = token_rows(col_ref, row_ref, chip, start, width, side, grid_rows)
            features_ref[:, span] = features_ref[:, span] + jnp.dot(
                planes_ref[:, block], table, preferred_element_type=f32
            )
            return inner

        lax.fori_loop(0, samples // width, add, 0)
        return carry

    lax.fori_loop(0, chips, interpolate, 0)

    def decode(step, carry):
        span = pl.ds(pl.multiple_of(step * prep_width, prep_width), prep_width)
        z1 = jnp.dot(w1, features_ref[:, span].astype(bf16), preferred_element_type=f32) + b1
        z1_ref[:, span] = z1
        h1 = (z1 * jax.nn.sigmoid(z1)).astype(bf16)
        z2 = jnp.dot(w2, h1, preferred_element_type=f32) + b2
        z2_ref[:, span] = z2
        h2 = (z2 * jax.nn.sigmoid(z2)).astype(bf16)
        decoded_ref[:, span] = jnp.dot(w3, h2, preferred_element_type=f32) + b3
        return carry

    lax.fori_loop(0, samples // prep_width, decode, 0)

    rays = samples // STEPS
    lane = lax.broadcasted_iota(jnp.int32, (1, samples), 1) % STEPS
    density = decoded_ref[0:1]
    optical = (jnp.maximum(density, 0.0) + jnp.log1p(jnp.exp(-jnp.abs(density)))) * DEPTH_STEP
    albedo = jax.nn.sigmoid(decoded_ref[1:4])
    reach = jnp.exp(optical - ray_scan(optical, lane, False))
    passed = jnp.exp(-optical)
    weight = reach * (1.0 - passed)
    spread = (
        lax.broadcasted_iota(jnp.int32, (rays, samples), 0)
        == lax.broadcasted_iota(jnp.int32, (rays, samples), 1) // STEPS
    ).astype(f32)
    colors = lax.dot_general(
        weight * albedo, spread, turned, precision=exact, preferred_element_type=f32
    )
    colors_ref[...] = colors
    miss = jnp.dot(
        colors - target_ref[...], spread, precision=exact, preferred_element_type=f32
    )
    weight_grad = jnp.sum(miss * albedo, axis=0, keepdims=True)
    term = weight_grad * weight
    later = ray_scan(term, lane, True) - term
    optical_grad = weight_grad * reach * passed - later
    decoded_ref[0:1] = optical_grad * (DEPTH_STEP * jax.nn.sigmoid(density))
    decoded_ref[1:4] = miss * weight * albedo * (1.0 - albedo)

    def silu_grad(pre):
        gate = jax.nn.sigmoid(pre)
        return gate * (1.0 + pre * (1.0 - gate))

    def decode_back(step, carry):
        span = pl.ds(pl.multiple_of(step * prep_width, prep_width), prep_width)
        g2 = lax.dot_general(
            w3, decoded_ref[:, span].astype(bf16), flip, preferred_element_type=f32
        )
        g2 = g2.astype(bf16).astype(f32) * silu_grad(z2_ref[:, span])
        g1 = lax.dot_general(w2, g2.astype(bf16), flip, preferred_element_type=f32)
        g1 = g1.astype(bf16).astype(f32) * silu_grad(z1_ref[:, span])
        fgrad_ref[:, span] = lax.dot_general(
            w1, g1.astype(bf16), flip, preferred_element_type=f32
        ).astype(bf16)
        return carry

    lax.fori_loop(0, samples // prep_width, decode_back, 0)

    def swap(number):
        return remote(
            give_ref.at[number],
            pair_ref.at[number],
            pair_send.at[number],
            pair_recv.at[number],
            ring.partner,
        )

    def push_half(way, row, number):
        part = pl.ds(way * half_extent, half_extent)
        return remote(
            stage_ref.at[number, :, part],
            half_ref.at[way, row],
            half_send.at[way, row],
            half_recv.at[way, row],
            ring.right if way == 0 else ring.left,
        )

    def push_side(way, row, number):
        return remote(
            stage_ref.at[number],
            side_ref.at[way, row],
            side_send.at[way, row],
            side_recv.at[way, row],
            ring.right if way == 0 else ring.left,
        )

    def push_over(number):
        return remote(stage_ref.at[number], over_ref, over_send, over_recv, ring.over)

    def stage(number):
        swap(number).wait_recv()
        row = 1 - number // 4
        kind = number % 4
        both = keep_ref[...] + pair_ref[number].astype(f32)
        if kind == 0:
            stage_ref[number] = both.astype(bf16)
            push_half(0, row, number).start()
            push_half(1, row, number).start()
        elif kind < 3:
            way = kind - 1
            push_half(way, row, number).wait_recv()
            part = pl.ds(way * half_extent, half_extent)
            stage_ref[number] = both.astype(bf16)
            first = way * half_extent
            stage_ref[number, :, part] = (
                both[:, first : first + half_extent] + half_ref[way, row].astype(f32)
            ).astype(bf16)
            push_side(way, row, number).start()
        else:
            for way in range(2):
                push_side(way, row, number).wait_recv()
                both = both + side_ref[way, row].astype(f32)
            if row == 1:
                stage_ref[number] = both.astype(bf16)
                push_over(number).start()
        return both

    def spread_back(step, carry):
        place = step % 4
        across = 2 + 3 * place + 3 * (place // 2) + 2 * (place // 3)
        chip = chip_at(across, 1 - step // 4)

        def product(owner):
            table = token_rows(col_ref, row_ref, owner, 0, samples, side, extent // side)
            return lax.dot_general(fgrad_ref[...], table, turned, preferred_element_type=f32)

        give_ref[step] = product(2 * chip + 1 - core).astype(bf16)
        swap(step).start()
        keep_ref[...] = product(2 * chip + core)
        for number in range(chips - 1):

            @pl.when(step == number)
            def _(number=number):
                stage(number)

        return carry

    lax.fori_loop(0, chips, spread_back, 0)
    both = stage(chips - 1)
    push_over(3).wait_recv()
    own_grad = (both + over_ref[...].astype(f32)).astype(bf16)

    rows, lanes = chunk_ref.shape

    def chunk_of(owner):
        return (
            pl.ds(pl.multiple_of((owner % 2) * rows, rows), rows),
            pl.ds(pl.multiple_of((owner // 2) * lanes, lanes), lanes),
        )

    part_ref[...] = jnp.dot(own_grad, plane_in_ref[...], preferred_element_type=f32)
    waiting = []
    for owner in others:
        copy = remote(
            part_ref.at[chunk_of(owner)],
            chunk_land_ref.at[me],
            chunk_send.at[owner],
            chunk_recv.at[me],
            {"seq": owner},
        )
        copy.start()
        waiting.append(copy)
    for first in range(0, extent, tile):
        token_grad_ref[first : first + tile, :] = lax.dot_general(
            own_grad[:, first : first + tile],
            w_plane_ref[...],
            flip,
            preferred_element_type=f32,
        ).astype(bf16)
    chunk = part_ref[chunk_of(me)]
    for owner in others:
        remote(
            chunk_ref,
            chunk_land_ref.at[owner],
            chunk_send.at[owner],
            chunk_recv.at[owner],
            ring.partner,
        ).wait_recv()
        chunk = chunk + chunk_land_ref[owner]
    chunk_ref[...] = chunk
    scene_ref[scene] = chunk
    for other in other_scenes:
        copy = remote(
            chunk_ref,
            scene_ref.at[scene],
            scene_send.at[other],
            scene_recv.at[scene],
            {"dp": other},
        )
        copy.start()
        waiting.append(copy)
    for other in other_scenes:
        remote(
            chunk_ref,
            scene_ref.at[other],
            scene_send.at[other],
            scene_recv.at[other],
            ring.partner,
        ).wait_recv()
    final = scene_ref[0]
    for other in range(1, scenes):
        final = final + scene_ref[other]
    spot = chunk_of(me)
    total_ref[spot] = final
    for owner in others:
        copy = remote(
            total_ref.at[spot],
            total_ref.at[spot],
            last_send.at[owner],
            last_recv.at[me],
            {"seq": owner},
        )
        copy.start()
        waiting.append(copy)
    for owner in others:
        there = chunk_of(owner)
        remote(
            total_ref.at[there],
            total_ref.at[there],
            last_send.at[owner],
            last_recv.at[owner],
            ring.partner,
        ).wait_recv()
    for copy in waiting:
        copy.wait_send()
    for number in range(chips):
        swap(number).wait_send()
    for row in range(2):
        base = 4 * (1 - row)
        for way in range(2):
            push_half(way, row, base).wait_send()
            push_side(way, row, base + 1 + way).wait_send()
    push_over(3).wait_send()
    ring.finish()


def render_scene(
    block,
    plane_in,
    index,
    weight,
    target,
    w_plane,
    w1,
    b1,
    w2,
    b2,
    w3,
    b3,
    size,
    scenes,
    collective_id,
):
    channels, extent = block.shape
    width = plane_in.shape[1]
    samples = index.shape[1]
    tokens = extent * size
    side = math.isqrt(tokens // PLANES)
    chips = size // 2
    rows, lanes = channels // 2, width // chips
    sems = pltpu.SemaphoreType.DMA
    return pl.pallas_call(
        functools.partial(
            scene_kernel,
            side=side,
            size=size,
            scenes=scenes,
            prep_width=1024,
            width=2048,
            tile=256,
        ),
        out_shape=(
            jax.ShapeDtypeStruct(target.shape, f32),
            jax.ShapeDtypeStruct((extent, width), bf16),
            jax.ShapeDtypeStruct((channels, width), f32),
        ),
        in_specs=in_vmem(12),
        out_specs=tuple(in_vmem(3)),
        scratch_shapes=[
            pltpu.VMEM((channels, tokens), bf16),
            pltpu.VMEM((2 * PLANES, side, samples), bf16),
            pltpu.VMEM((PLANES, 16, samples), bf16),
            pltpu.VMEM((channels, samples), f32),
            pltpu.VMEM((channels, samples), bf16),
            pltpu.VMEM((w1.shape[0], samples), f32),
            pltpu.VMEM((w2.shape[0], samples), f32),
            pltpu.VMEM((w3.shape[0], samples), f32),
            pltpu.VMEM((chips, channels, extent), bf16),
            pltpu.VMEM((channels, extent), f32),
            pltpu.VMEM((chips, channels, extent), bf16),
            pltpu.VMEM((chips, channels, extent), bf16),
            pltpu.VMEM((2, 2, channels, extent // 2), bf16),
            pltpu.VMEM((2, 2, channels, extent), bf16),
            pltpu.VMEM((channels, extent), bf16),
            pltpu.VMEM((channels, width), f32),
            pltpu.VMEM((size, rows, lanes), f32),
            pltpu.VMEM((rows, lanes), f32),
            pltpu.VMEM((scenes, rows, lanes), f32),
            sems((chips,)),
            sems((chips,)),
            sems((2, 2)),
            sems((2, 2)),
            sems((2, 2)),
            sems((2, 2)),
            sems,
            sems,
            sems((size,)),
            sems((size,)),
            sems((scenes,)),
            sems((scenes,)),
            sems((size,)),
            sems((size,)),
            *exchange_sems(),
        ],
        compiler_params=pltpu.CompilerParams(
            collective_id=collective_id,
            has_side_effects=True,
            vmem_limit_bytes=40 * 1024 * 1024,
        ),
        name="scene",
    )(
        block,
        plane_in,
        index,
        weight,
        target,
        w_plane.T,
        w1,
        b1[None, :],
        w2,
        b2[None, :],
        w3,
        b3[None, :],
    )


def body(
    tokens,
    image_tokens,
    norm_gain,
    w_query,
    w_key,
    w_value,
    w_out,
    w_plane,
    dec_w1,
    dec_b1,
    dec_w2,
    dec_b2,
    dec_w3,
    dec_b3,
    corner_idx,
    corner_wts,
    target_color,
):
    own_tokens = tokens[0]
    model_width = own_tokens.shape[1]
    head_dim = model_width // HEADS
    size = lax.axis_size("seq")
    score_scale = math.log2(math.e) / math.sqrt(head_dim)
    queries, keys, values = front(
        own_tokens, image_tokens[0], w_query, w_key, w_value, size, score_scale, 0
    )
    plane_in, planes = attention(
        queries, keys, values, own_tokens, w_out, norm_gain, w_plane
    )
    colors, token_grad, weight_grad = render_scene(
        planes,
        plane_in,
        corner_idx[0],
        corner_wts[0],
        target_color[0],
        w_plane,
        dec_w1,
        dec_b1,
        dec_w2,
        dec_b2,
        dec_w3,
        dec_b3,
        size,
        lax.axis_size("dp"),
        1,
    )
    return (colors[None], token_grad[None], weight_grad.T)


def solution(mesh):
    in_specs = (
        P("dp", "seq", None),
        P("dp", "seq", None),
        *(P() for _ in range(12)),
        P("dp", None, "seq"),
        P("dp", None, "seq"),
        P("dp", None, "seq"),
    )
    out_specs = (P("dp", None, "seq"), P("dp", "seq", None), P())
    return jax.shard_map(body, mesh=mesh, in_specs=in_specs, out_specs=out_specs, check_vma=False)
```

```python
import functools
import math

import jax
import jax.numpy as jnp
from jax import lax
from jax.experimental import pallas as pl
from jax.experimental.pallas import tpu as pltpu
from jax.sharding import PartitionSpec as P

HEADS = 16
STEPS = 128
PLANES = 3
LANES = 128
NORM_EPS = 1e-05
DEPTH_STEP = 0.02
VMEM_BYTES = 60000 * 1024

bf16 = jnp.bfloat16
f32 = jnp.float32


def in_vmem(count):
    return [pl.BlockSpec(memory_space=pltpu.VMEM)] * count


def plain_norm(inputs):
    row_mean = jnp.mean(inputs, axis=-1, keepdims=True)
    centred = inputs - row_mean
    row_var = jnp.mean(centred * centred, axis=-1, keepdims=True)
    return centred * lax.rsqrt(row_var + NORM_EPS)


def attention_kernel(
    q_ref,
    k_ref,
    v_ref,
    tokens_ref,
    w_out_ref,
    gain_ref,
    w_plane_ref,
    plane_in_ref,
    planes_ref,
    values_ref,
    scores_ref,
    maxes_ref,
    attended_ref,
    *,
    tile,
):
    rows, width = q_ref.shape
    count = k_ref.shape[0]
    pairs = width // LANES
    low = lax.broadcasted_iota(jnp.int32, (1, LANES), 1) < LANES // 2
    turned = (((1,), (1,)), ((), ()))

    def score(pair_id, head):
        span = pl.ds(pl.multiple_of(pair_id * LANES, LANES), LANES)
        own = jnp.where(low if head == 0 else ~low, q_ref[:, span], jnp.zeros((), bf16))
        scores = lax.dot_general(own, k_ref[:, span], turned, preferred_element_type=f32)
        scores_ref[head] = scores
        highest = scores[:, :LANES]
        for first in range(LANES, count, LANES):
            highest = jnp.maximum(highest, scores[:, first : first + LANES])
        maxes_ref[head] = highest

    def weigh(head):
        row_max = jnp.max(maxes_ref[head], axis=1, keepdims=True)
        terms = jnp.exp2(scores_ref[head] - row_max).astype(bf16)
        return jnp.dot(terms, values_ref[head], preferred_element_type=f32)

    score(0, 0)

    def pair(pair_id, carry):
        span = pl.ds(pl.multiple_of(pair_id * LANES, LANES), LANES)
        values = v_ref[:, span]
        one = jnp.ones((), bf16)
        values_ref[0] = jnp.where(low, values, one)
        values_ref[1] = jnp.where(low, one, values)
        score(pair_id, 1)
        first = weigh(0)
        score((pair_id + 1) % pairs, 0)
        second = weigh(1)
        row_sum = pltpu.roll(jnp.where(low, second, first), LANES // 2, 1)
        attended_ref[:, span] = (jnp.where(low, first, second) / row_sum).astype(bf16)
        return carry

    lax.fori_loop(0, pairs, pair, 0)

    def project(step, carry):
        span = pl.ds(pl.multiple_of(step * tile, tile), tile)
        mixed = tokens_ref[span, :].astype(f32) + jnp.dot(
            attended_ref[span, :], w_out_ref[...], preferred_element_type=f32
        )
        mixed = mixed.astype(bf16).astype(f32)
        plane_in = (plain_norm(mixed) * gain_ref[...]).astype(bf16)
        plane_in_ref[span, :] = plane_in
        planes_ref[:, span] = lax.dot_general(
            w_plane_ref[...], plane_in, turned, preferred_element_type=f32
        ).astype(bf16)
        return carry

    lax.fori_loop(0, rows // tile, project, 0)


def attention(queries, keys, values, tokens, w_out, gain, w_plane):
    rows, width = queries.shape
    count = values.shape[0]
    channels = w_plane.shape[1]
    return pl.pallas_call(
        functools.partial(attention_kernel, tile=256),
        out_shape=(
            jax.ShapeDtypeStruct((rows, width), bf16),
            jax.ShapeDtypeStruct((channels, rows), bf16),
        ),
        in_specs=in_vmem(7),
        out_specs=tuple(in_vmem(2)),
        scratch_shapes=[
            pltpu.VMEM((2, count, LANES), bf16),
            pltpu.VMEM((2, rows, count), f32),
            pltpu.VMEM((2, rows, LANES), f32),
            pltpu.VMEM((rows, width), bf16),
        ],
        compiler_params=pltpu.CompilerParams(
            vmem_limit_bytes=36 * 1024 * 1024,
        ),
        cost_estimate=pl.CostEstimate(
            flops=4 * rows * count * width,
            bytes_accessed=4 * (rows + count) * width,
            transcendentals=rows * count * HEADS,
        ),
        name="attention",
    )(queries, keys, values, tokens, w_out, gain[None, :], w_plane.T)


MESH_ID = pl.DeviceIdType.MESH


def greet(peers):
    barrier = pltpu.get_barrier_semaphore()
    for peer in peers:
        pl.semaphore_signal(barrier, inc=1, device_id=peer, device_id_type=MESH_ID)
    pl.semaphore_wait(barrier, len(peers))


def remote(source, target, send_sem, recv_sem, peer):
    return pltpu.make_async_remote_copy(
        src_ref=source,
        dst_ref=target,
        send_sem=send_sem,
        recv_sem=recv_sem,
        device_id=peer,
        device_id_type=MESH_ID,
    )


def partner_of(me):
    return me + 1 - 2 * (me % 2)


RING = 4
SENDS, ARRIVALS = 19, 10


class Exchange:
    def __init__(self, block_ref, out_ref, axis, sems):
        self.block, self.out, self.axis = block_ref, out_ref, axis
        self.send_sem, self.recv_sem, self.land_sem, self.own_sem = sems
        me = lax.axis_index("seq")
        self.me = me
        self.core = me % 2
        self.y = (me // 2) % 2
        self.x = me // 4
        self.extent = block_ref.shape[axis]
        self.started = []
        self.right = {"seq": self.at(1, 0)}
        self.left = {"seq": self.at(-1, 0)}
        self.over = {"seq": self.at(0, 1)}
        self.partner = {"seq": partner_of(me)}

    def at(self, dx, dy):
        return 4 * ((self.x + dx + RING) % RING) + 2 * ((self.y + dy) % 2) + self.core

    def place(self, owner, half=None):
        size = self.extent if half is None else self.extent // 2
        start = owner * self.extent + (0 if half is None else half * size)
        span = pl.ds(pl.multiple_of(start, size), size)
        return self.out.at[span, :] if self.axis == 0 else self.out.at[:, span]

    def push(self, source, owner, half, recv, peer):
        remote(
            source, self.place(owner, half), self.send_sem.at[len(self.started)], recv, peer
        ).start()
        self.started.append(half)

    def relay(self, owner, half, recv, peer):
        self.push(self.place(owner, half), owner, half, recv, peer)

    def hear(self, owner, half, sem):
        spot = self.place(owner, half)
        remote(spot, spot, self.send_sem.at[0], sem, self.partner).wait_recv()

    def begin(self):
        self.own = pltpu.make_async_copy(self.block, self.place(self.me), self.own_sem)
        self.own.start()
        recv, land = self.recv_sem, self.land_sem
        self.push(self.block, self.me, None, recv.at[0], self.right)
        self.push(self.block, self.me, None, recv.at[1], self.left)
        self.push(self.block, self.me, None, recv.at[2], self.over)
        self.push(self.block, self.me, None, land.at[9], self.partner)

    def arrive(self, number, dx, dy, half, onward):
        owner = self.at(dx, dy)
        self.hear(owner, half, self.recv_sem.at[number])
        for part, target, peer in onward:
            self.relay(owner, part, self.recv_sem.at[target], peer)
        self.relay(owner, half, self.land_sem.at[number], self.partner)

    def beside(self):
        self.arrive(0, -1, 0, None, [(0, 5, self.right)])
        self.arrive(1, 1, 0, None, [(1, 6, self.left)])

    def across(self):
        self.arrive(2, 0, 1, None, [(None, 3, self.right), (None, 4, self.left)])

    def opposite(self):
        self.arrive(5, 2, 0, 0, [])
        self.arrive(6, 2, 0, 1, [])

    def beside_across(self):
        self.arrive(3, -1, 1, None, [(0, 7, self.right)])
        self.arrive(4, 1, 1, None, [(1, 8, self.left)])

    def opposite_across(self):
        self.arrive(7, 2, 1, 0, [])
        self.arrive(8, 2, 1, 1, [])

    def handed(self, number, dx, dy, half):
        other = self.at(dx, dy) + 1 - 2 * self.core
        self.hear(other, half, self.land_sem.at[number])

    def finish(self):
        for number, half in enumerate(self.started):
            spot = self.place(self.me, half)
            remote(
                spot, spot, self.send_sem.at[number], self.recv_sem.at[0], self.partner
            ).wait_send()

    def neighbours(self):
        return [self.right, self.left, self.over, self.partner]


def exchange_sems():
    sems = pltpu.SemaphoreType.DMA
    return [sems((SENDS,)), sems((ARRIVALS,)), sems((ARRIVALS,)), sems]


def front_kernel(
    tokens_hbm,
    image_hbm,
    w_query_hbm,
    w_key_hbm,
    w_value_hbm,
    q_ref,
    k_ref,
    v_ref,
    tokens_ref,
    image_ref,
    images_ref,
    w_query_ref,
    w_key_ref,
    w_value_ref,
    load_sem,
    *sems,
    tile,
    scale,
):
    ring = Exchange(image_ref, images_ref, 0, sems)
    loads = []
    for number, (source, target) in enumerate(
        (
            (image_hbm, image_ref),
            (tokens_hbm, tokens_ref),
            (w_query_hbm, w_query_ref),
            (w_key_hbm, w_key_ref),
            (w_value_hbm, w_value_ref),
        )
    ):
        copy = pltpu.make_async_copy(source, target, load_sem.at[number])
        copy.start()
        loads.append(copy)
    greet(ring.neighbours())
    loads[0].wait()
    ring.begin()

    def query(step):
        span = pl.ds(step * tile, tile)
        normed = plain_norm(tokens_ref[span, :].astype(f32)).astype(bf16)
        product = jnp.dot(normed, w_query_ref[...], preferred_element_type=f32)
        q_ref[span, :] = (product * scale).astype(bf16)

    def keys_values(dx, dy):
        owner = ring.at(dx, dy) // 2
        rows = 2 * image_ref.shape[0]
        span = pl.ds(pl.multiple_of(owner * rows, rows), rows)
        images = images_ref[span, :]
        k_ref[span, :] = jnp.dot(
            images, w_key_ref[...], preferred_element_type=f32
        ).astype(bf16)
        v_ref[span, :] = jnp.dot(
            images, w_value_ref[...], preferred_element_type=f32
        ).astype(bf16)

    loads[1].wait()
    loads[2].wait()
    query(0)
    query(1)
    ring.beside()
    query(2)
    ring.across()
    loads[3].wait()
    loads[4].wait()
    ring.own.wait()
    ring.handed(9, 0, 0, None)
    keys_values(0, 0)
    ring.handed(0, -1, 0, None)
    keys_values(-1, 0)
    ring.handed(1, 1, 0, None)
    keys_values(1, 0)
    ring.opposite()
    ring.handed(2, 0, 1, None)
    keys_values(0, 1)
    ring.handed(5, 2, 0, 0)
    ring.handed(6, 2, 0, 1)
    keys_values(2, 0)
    ring.beside_across()
    ring.handed(3, -1, 1, None)
    keys_values(-1, 1)
    ring.handed(4, 1, 1, None)
    keys_values(1, 1)
    ring.opposite_across()
    ring.handed(7, 2, 1, 0)
    ring.handed(8, 2, 1, 1)
    keys_values(2, 1)
    ring.finish()


def front(tokens, images, w_query, w_key, w_value, size, scale, collective_id):
    rows, width = tokens.shape
    depth = images.shape[1]
    count = images.shape[0] * size
    heads = w_key.shape[1]
    return pl.pallas_call(
        functools.partial(front_kernel, tile=rows // 3, scale=scale),
        out_shape=(
            jax.ShapeDtypeStruct((rows, width), bf16),
            jax.ShapeDtypeStruct((count, heads), bf16),
            jax.ShapeDtypeStruct((count, heads), bf16),
        ),
        in_specs=[pl.BlockSpec(memory_space=pltpu.HBM)] * 5,
        out_specs=tuple(in_vmem(3)),
        scratch_shapes=[
            pltpu.VMEM(tokens.shape, bf16),
            pltpu.VMEM(images.shape, bf16),
            pltpu.VMEM((count, depth), bf16),
            pltpu.VMEM(w_query.shape, bf16),
            pltpu.VMEM(w_key.shape, bf16),
            pltpu.VMEM(w_value.shape, bf16),
            pltpu.SemaphoreType.DMA((5,)),
            *exchange_sems(),
        ],
        compiler_params=pltpu.CompilerParams(
            collective_id=collective_id,
            has_side_effects=True,
            vmem_limit_bytes=24 * 1024 * 1024,
        ),
        name="front",
    )(
        *(
            pltpu.with_memory_space_constraint(array, pltpu.HBM)
            for array in (tokens, images, w_query, w_key, w_value)
        )
    )


def table_rows(col_ref, row_ref, plane, first_row, row_count, start, width, side):
    span = pl.ds(start, width)
    pieces = side // 16
    upper = col_ref[2 * plane, :, span].reshape(pieces, 16, width)
    lower = col_ref[2 * plane + 1, :, span].reshape(pieces, 16, width)
    cell_row = row_ref[plane, :, span]
    zero = jnp.zeros((16, width), bf16)
    row_id = jnp.asarray(first_row, jnp.int32)
    before = cell_row == (row_id - 1).astype(bf16)
    blocks = []
    for step in range(row_count):
        here = cell_row == (row_id + step).astype(bf16)
        for piece in range(pieces):
            blocks.append(
                jnp.where(here, upper[piece], jnp.where(before, lower[piece], zero))
            )
        before = here
    return jnp.concatenate(blocks, axis=0)


def ray_scan(values, lane, reverse):
    width = values.shape[1]
    shift = 1
    while shift < STEPS:
        if reverse:
            moved = pltpu.roll(values, width - shift, 1)
            values = values + jnp.where(lane < STEPS - shift, moved, 0.0)
        else:
            moved = pltpu.roll(values, shift, 1)
            values = values + jnp.where(lane >= shift, moved, 0.0)
        shift *= 2
    return values


def column_of(row_ref):
    count = row_ref.shape[1]
    diagonal = lax.broadcasted_iota(jnp.int32, (count, count), 0) == lax.broadcasted_iota(
        jnp.int32, (count, count), 1
    )
    return jnp.sum(jnp.where(diagonal, row_ref[...], 0.0), axis=1, keepdims=True)


def token_rows(col_ref, row_ref, chip, start, width, side, grid_rows):
    blocks = []
    for group in range(grid_rows // 4):
        number = chip * (grid_rows // 4) + group
        plane = number // (side // 4)
        first = (number - plane * (side // 4)) * 4
        blocks.append(table_rows(col_ref, row_ref, plane, first, 4, start, width, side))
    return jnp.concatenate(blocks, axis=0)


def scene_kernel(
    block_ref,
    plane_in_ref,
    idx_ref,
    wts_ref,
    target_ref,
    w_plane_ref,
    w1_ref,
    b1_ref,
    w2_ref,
    b2_ref,
    w3_ref,
    b3_ref,
    colors_ref,
    token_grad_ref,
    total_ref,
    planes_ref,
    col_ref,
    row_ref,
    features_ref,
    fgrad_ref,
    z1_ref,
    z2_ref,
    decoded_ref,
    give_ref,
    keep_ref,
    pair_ref,
    stage_ref,
    half_ref,
    side_ref,
    over_ref,
    part_ref,
    chunk_land_ref,
    chunk_ref,
    scene_ref,
    last_ref,
    pair_send,
    pair_recv,
    half_send,
    half_recv,
    side_send,
    side_recv,
    over_send,
    over_recv,
    chunk_send,
    chunk_recv,
    scene_send,
    scene_recv,
    last_send,
    last_recv,
    *ring_sems,
    side,
    size,
    scenes,
    prep_width,
    width,
    tile,
):
    samples = idx_ref.shape[1]
    channels, tokens = planes_ref.shape
    extent = block_ref.shape[1]
    half_extent = extent // 2
    plane_size = side * side
    chip_tokens = 2 * extent
    grid_rows = chip_tokens // side
    chips = size // 2
    exact = lax.Precision.HIGHEST
    turned = (((1,), (1,)), ((), ()))
    flip = (((0,), (0,)), ((), ()))

    ring = Exchange(block_ref, planes_ref, 1, ring_sems)
    me, core = ring.me, ring.core
    scene = lax.axis_index("dp")
    others = [(me + step) % size for step in range(1, size)]
    other_scenes = [(scene + step) % scenes for step in range(1, scenes)]
    greet([{"seq": owner} for owner in others] + [{"dp": owner} for owner in other_scenes])
    ring.begin()

    def chip_at(dx, dy):
        return 2 * ((ring.x + dx) % RING) + (ring.y + dy) % 2

    def prepare(step, carry):
        start = pl.multiple_of(step * prep_width, prep_width)
        span = pl.ds(start, prep_width)
        index = idx_ref[:, span]
        weight = wts_ref[:, span].astype(f32)
        column_id = lax.broadcasted_iota(jnp.int32, (side, prep_width), 0)
        for plane in range(PLANES):
            in_plane = (index >= plane * plane_size) & (index < (plane + 1) * plane_size)
            base = jnp.min(jnp.where(in_plane, index, tokens), axis=0, keepdims=True)
            corner = []
            for offset in (0, 1, side, side + 1):
                corner.append(
                    jnp.sum(
                        jnp.where(index == base + offset, weight, 0.0), axis=0, keepdims=True
                    )
                )
            local = base - plane * plane_size
            cell_row = local // side
            column = local - cell_row * side
            for which in range(2):
                col_ref[2 * plane + which, :, span] = jnp.where(
                    column_id == column,
                    corner[2 * which],
                    jnp.where(column_id == column + 1, corner[2 * which + 1], 0.0),
                ).astype(bf16)
            row_ref[plane, :, span] = jnp.broadcast_to(
                cell_row.astype(f32), (16, prep_width)
            ).astype(bf16)
        return carry

    lax.fori_loop(0, samples // prep_width, prepare, 0)

    w1, w2, w3 = w1_ref[...], w2_ref[...], w3_ref[...]
    b1, b2, b3 = column_of(b1_ref), column_of(b2_ref), column_of(b3_ref)
    features_ref[...] = jnp.zeros_like(features_ref)

    arrivals = (
        ((), ((9, 0, 0, None),)),
        ((ring.beside, ring.across), ((1, 1, 0, None),)),
        ((), ((0, -1, 0, None),)),
        ((ring.opposite, ring.beside_across), ((5, 2, 0, 0), (6, 2, 0, 1))),
        ((), ((2, 0, 1, None),)),
        ((ring.opposite_across,), ((4, 1, 1, None),)),
        ((), ((3, -1, 1, None),)),
        ((), ((7, 2, 1, 0), (8, 2, 1, 1))),
    )

    def interpolate(step, carry):
        for number, (receive, handed) in enumerate(arrivals):

            @pl.when(step == number)
            def _(number=number, receive=receive, handed=handed):
                for take in receive:
                    take()
                if number == 0:
                    ring.own.wait()
                for item in handed:
                    ring.handed(*item)

        place = step % 4
        chip = chip_at(place + place // 2 - 2 * (place // 3), step // 4)
        block = pl.ds(pl.multiple_of(chip * chip_tokens, chip_tokens), chip_tokens)

        def add(part, inner):
            start = pl.multiple_of(part * width, width)
            span = pl.ds(start, width)
            table = token_rows(col_ref, row_ref, chip, start, width, side, grid_rows)
            features_ref[:, span] = features_ref[:, span] + jnp.dot(
                planes_ref[:, block], table, preferred_element_type=f32
            )
            return inner

        lax.fori_loop(0, samples // width, add, 0)
        return carry

    lax.fori_loop(0, chips, interpolate, 0)

    def decode(step, carry):
        span = pl.ds(pl.multiple_of(step * prep_width, prep_width), prep_width)
        z1 = jnp.dot(w1, features_ref[:, span].astype(bf16), preferred_element_type=f32) + b1
        z1_ref[:, span] = z1
        h1 = (z1 * jax.nn.sigmoid(z1)).astype(bf16)
        z2 = jnp.dot(w2, h1, preferred_element_type=f32) + b2
        z2_ref[:, span] = z2
        h2 = (z2 * jax.nn.sigmoid(z2)).astype(bf16)
        decoded_ref[:, span] = jnp.dot(w3, h2, preferred_element_type=f32) + b3
        return carry

    lax.fori_loop(0, samples // prep_width, decode, 0)

    rays = samples // STEPS
    lane = lax.broadcasted_iota(jnp.int32, (1, samples), 1) % STEPS
    density = decoded_ref[0:1]
    optical = (jnp.maximum(density, 0.0) + jnp.log1p(jnp.exp(-jnp.abs(density)))) * DEPTH_STEP
    albedo = jax.nn.sigmoid(decoded_ref[1:4])
    reach = jnp.exp(optical - ray_scan(optical, lane, False))
    passed = jnp.exp(-optical)
    weight = reach * (1.0 - passed)
    spread = (
        lax.broadcasted_iota(jnp.int32, (rays, samples), 0)
        == lax.broadcasted_iota(jnp.int32, (rays, samples), 1) // STEPS
    ).astype(f32)
    colors = lax.dot_general(
        weight * albedo, spread, turned, precision=exact, preferred_element_type=f32
    )
    colors_ref[...] = colors
    miss = jnp.dot(
        colors - target_ref[...], spread, precision=exact, preferred_element_type=f32
    )
    weight_grad = jnp.sum(miss * albedo, axis=0, keepdims=True)
    term = weight_grad * weight
    later = ray_scan(term, lane, True) - term
    optical_grad = weight_grad * reach * passed - later
    decoded_ref[0:1] = optical_grad * (DEPTH_STEP * jax.nn.sigmoid(density))
    decoded_ref[1:4] = miss * weight * albedo * (1.0 - albedo)

    def silu_grad(pre):
        gate = jax.nn.sigmoid(pre)
        return gate * (1.0 + pre * (1.0 - gate))

    def decode_back(step, carry):
        span = pl.ds(pl.multiple_of(step * prep_width, prep_width), prep_width)
        g2 = lax.dot_general(
            w3, decoded_ref[:, span].astype(bf16), flip, preferred_element_type=f32
        )
        g2 = g2.astype(bf16).astype(f32) * silu_grad(z2_ref[:, span])
        g1 = lax.dot_general(w2, g2.astype(bf16), flip, preferred_element_type=f32)
        g1 = g1.astype(bf16).astype(f32) * silu_grad(z1_ref[:, span])
        fgrad_ref[:, span] = lax.dot_general(
            w1, g1.astype(bf16), flip, preferred_element_type=f32
        ).astype(bf16)
        return carry

    lax.fori_loop(0, samples // prep_width, decode_back, 0)

    def swap(number):
        return remote(
            give_ref.at[number],
            pair_ref.at[number],
            pair_send.at[number],
            pair_recv.at[number],
            ring.partner,
        )

    def push_half(way, row, number):
        part = pl.ds(way * half_extent, half_extent)
        return remote(
            stage_ref.at[number, :, part],
            half_ref.at[way, row],
            half_send.at[way, row],
            half_recv.at[way, row],
            ring.right if way == 0 else ring.left,
        )

    def push_side(way, row, number):
        return remote(
            stage_ref.at[number],
            side_ref.at[way, row],
            side_send.at[way, row],
            side_recv.at[way, row],
            ring.right if way == 0 else ring.left,
        )

    def push_over(number):
        return remote(stage_ref.at[number], over_ref, over_send, over_recv, ring.over)

    def stage(number):
        swap(number).wait_recv()
        row = 1 - number // 4
        kind = number % 4
        both = keep_ref[...] + pair_ref[number].astype(f32)
        if kind == 0:
            stage_ref[number] = both.astype(bf16)
            push_half(0, row, number).start()
            push_half(1, row, number).start()
        elif kind < 3:
            way = kind - 1
            push_half(way, row, number).wait_recv()
            part = pl.ds(way * half_extent, half_extent)
            stage_ref[number] = both.astype(bf16)
            first = way * half_extent
            stage_ref[number, :, part] = (
                both[:, first : first + half_extent] + half_ref[way, row].astype(f32)
            ).astype(bf16)
            push_side(way, row, number).start()
        else:
            for way in range(2):
                push_side(way, row, number).wait_recv()
                both = both + side_ref[way, row].astype(f32)
            if row == 1:
                stage_ref[number] = both.astype(bf16)
                push_over(number).start()
        return both

    def spread_back(step, carry):
        place = step % 4
        across = 2 + 3 * place + 3 * (place // 2) + 2 * (place // 3)
        chip = chip_at(across, 1 - step // 4)

        def product(owner):
            table = token_rows(col_ref, row_ref, owner, 0, samples, side, extent // side)
            return lax.dot_general(fgrad_ref[...], table, turned, preferred_element_type=f32)

        give_ref[step] = product(2 * chip + 1 - core).astype(bf16)
        swap(step).start()
        keep_ref[...] = product(2 * chip + core)
        for number in range(chips - 1):

            @pl.when(step == number)
            def _(number=number):
                stage(number)

        return carry

    lax.fori_loop(0, chips, spread_back, 0)
    both = stage(chips - 1)
    push_over(3).wait_recv()
    own_grad = (both + over_ref[...].astype(f32)).astype(bf16)

    rows, lanes = chunk_ref.shape

    def chunk_of(owner):
        return (
            pl.ds(pl.multiple_of((owner % 2) * rows, rows), rows),
            pl.ds(pl.multiple_of((owner // 2) * lanes, lanes), lanes),
        )

    part_ref[0:channels] = jnp.dot(
        own_grad, plane_in_ref[...], preferred_element_type=f32
    ).astype(bf16)
    part_ref[channels:] = jnp.zeros((2 * rows - channels, part_ref.shape[1]), bf16)
    waiting = []
    for owner in others:
        copy = remote(
            part_ref.at[chunk_of(owner)],
            chunk_land_ref.at[me],
            chunk_send.at[owner],
            chunk_recv.at[me],
            {"seq": owner},
        )
        copy.start()
        waiting.append(copy)
    for first in range(0, extent, tile):
        token_grad_ref[first : first + tile, :] = lax.dot_general(
            own_grad[:, first : first + tile],
            w_plane_ref[...],
            flip,
            preferred_element_type=f32,
        ).astype(bf16)
    chunk = part_ref[chunk_of(me)].astype(f32)
    for owner in others:
        remote(
            last_ref.at[chunk_of(me)],
            chunk_land_ref.at[owner],
            chunk_send.at[owner],
            chunk_recv.at[owner],
            ring.partner,
        ).wait_recv()
        chunk = chunk + chunk_land_ref[owner].astype(f32)
    chunk_ref[...] = chunk
    scene_ref[scene] = chunk
    for other in other_scenes:
        copy = remote(
            chunk_ref,
            scene_ref.at[scene],
            scene_send.at[other],
            scene_recv.at[scene],
            {"dp": other},
        )
        copy.start()
        waiting.append(copy)
    for other in other_scenes:
        remote(
            chunk_ref,
            scene_ref.at[other],
            scene_send.at[other],
            scene_recv.at[other],
            ring.partner,
        ).wait_recv()
    final = scene_ref[0]
    for other in range(1, scenes):
        final = final + scene_ref[other]
    spot = chunk_of(me)
    last_ref[spot] = final.astype(bf16)
    for owner in others:
        copy = remote(
            last_ref.at[spot],
            last_ref.at[spot],
            last_send.at[owner],
            last_recv.at[me],
            {"seq": owner},
        )
        copy.start()
        waiting.append(copy)
    for owner in others:
        there = chunk_of(owner)
        remote(
            last_ref.at[there],
            last_ref.at[there],
            last_send.at[owner],
            last_recv.at[owner],
            ring.partner,
        ).wait_recv()
    total_ref[...] = last_ref[0:channels].astype(f32)
    for copy in waiting:
        copy.wait_send()
    for number in range(chips):
        swap(number).wait_send()
    for row in range(2):
        base = 4 * (1 - row)
        for way in range(2):
            push_half(way, row, base).wait_send()
            push_side(way, row, base + 1 + way).wait_send()
    push_over(3).wait_send()
    ring.finish()


def render_scene(
    block,
    plane_in,
    index,
    weight,
    target,
    w_plane,
    w1,
    b1,
    w2,
    b2,
    w3,
    b3,
    size,
    scenes,
    collective_id,
):
    channels, extent = block.shape
    width = plane_in.shape[1]
    samples = index.shape[1]
    tokens = extent * size
    side = math.isqrt(tokens // PLANES)
    chips = size // 2
    rows, lanes = -(-channels // 32) * 16, width // chips
    sems = pltpu.SemaphoreType.DMA
    return pl.pallas_call(
        functools.partial(
            scene_kernel,
            side=side,
            size=size,
            scenes=scenes,
            prep_width=1024,
            width=2048,
            tile=256,
        ),
        out_shape=(
            jax.ShapeDtypeStruct(target.shape, f32),
            jax.ShapeDtypeStruct((extent, width), bf16),
            jax.ShapeDtypeStruct((channels, width), f32),
        ),
        in_specs=in_vmem(12),
        out_specs=tuple(in_vmem(3)),
        scratch_shapes=[
            pltpu.VMEM((channels, tokens), bf16),
            pltpu.VMEM((2 * PLANES, side, samples), bf16),
            pltpu.VMEM((PLANES, 16, samples), bf16),
            pltpu.VMEM((channels, samples), f32),
            pltpu.VMEM((channels, samples), bf16),
            pltpu.VMEM((w1.shape[0], samples), f32),
            pltpu.VMEM((w2.shape[0], samples), f32),
            pltpu.VMEM((w3.shape[0], samples), f32),
            pltpu.VMEM((chips, channels, extent), bf16),
            pltpu.VMEM((channels, extent), f32),
            pltpu.VMEM((chips, channels, extent), bf16),
            pltpu.VMEM((chips, channels, extent), bf16),
            pltpu.VMEM((2, 2, channels, extent // 2), bf16),
            pltpu.VMEM((2, 2, channels, extent), bf16),
            pltpu.VMEM((channels, extent), bf16),
            pltpu.VMEM((2 * rows, width), bf16),
            pltpu.VMEM((size, rows, lanes), bf16),
            pltpu.VMEM((rows, lanes), f32),
            pltpu.VMEM((scenes, rows, lanes), f32),
            pltpu.VMEM((2 * rows, width), bf16),
            sems((chips,)),
            sems((chips,)),
            sems((2, 2)),
            sems((2, 2)),
            sems((2, 2)),
            sems((2, 2)),
            sems,
            sems,
            sems((size,)),
            sems((size,)),
            sems((scenes,)),
            sems((scenes,)),
            sems((size,)),
            sems((size,)),
            *exchange_sems(),
        ],
        compiler_params=pltpu.CompilerParams(
            collective_id=collective_id,
            has_side_effects=True,
            vmem_limit_bytes=40 * 1024 * 1024,
        ),
        name="scene",
    )(
        block,
        plane_in,
        index,
        weight,
        target,
        w_plane.T,
        w1,
        b1[None, :],
        w2,
        b2[None, :],
        w3,
        b3[None, :],
    )


def body(
    tokens,
    image_tokens,
    norm_gain,
    w_query,
    w_key,
    w_value,
    w_out,
    w_plane,
    dec_w1,
    dec_b1,
    dec_w2,
    dec_b2,
    dec_w3,
    dec_b3,
    corner_idx,
    corner_wts,
    target_color,
):
    own_tokens = tokens[0]
    model_width = own_tokens.shape[1]
    head_dim = model_width // HEADS
    size = lax.axis_size("seq")
    score_scale = math.log2(math.e) / math.sqrt(head_dim)
    queries, keys, values = front(
        own_tokens, image_tokens[0], w_query, w_key, w_value, size, score_scale, 0
    )
    plane_in, planes = attention(
        queries, keys, values, own_tokens, w_out, norm_gain, w_plane
    )
    colors, token_grad, weight_grad = render_scene(
        planes,
        plane_in,
        corner_idx[0],
        corner_wts[0],
        target_color[0],
        w_plane,
        dec_w1,
        dec_b1,
        dec_w2,
        dec_b2,
        dec_w3,
        dec_b3,
        size,
        lax.axis_size("dp"),
        1,
    )
    return (colors[None], token_grad[None], weight_grad.T)


def solution(mesh):
    in_specs = (
        P("dp", "seq", None),
        P("dp", "seq", None),
        *(P() for _ in range(12)),
        P("dp", None, "seq"),
        P("dp", None, "seq"),
        P("dp", None, "seq"),
    )
    out_specs = (P("dp", None, "seq"), P("dp", "seq", None), P())
    return jax.shard_map(body, mesh=mesh, in_specs=in_specs, out_specs=out_specs, check_vma=False)
```

```python
import functools
import math

import jax
import jax.numpy as jnp
from jax import lax
from jax.experimental import pallas as pl
from jax.experimental.pallas import tpu as pltpu
from jax.sharding import PartitionSpec as P

HEADS = 16
STEPS = 128
PLANES = 3
LANES = 128
NORM_EPS = 1e-05
DEPTH_STEP = 0.02
VMEM_BYTES = 60000 * 1024

bf16 = jnp.bfloat16
f32 = jnp.float32


def in_vmem(count):
    return [pl.BlockSpec(memory_space=pltpu.VMEM)] * count


def plain_norm(inputs):
    row_mean = jnp.mean(inputs, axis=-1, keepdims=True)
    centred = inputs - row_mean
    row_var = jnp.mean(centred * centred, axis=-1, keepdims=True)
    return centred * lax.rsqrt(row_var + NORM_EPS)


def attention_kernel(
    q_ref,
    k_ref,
    v_ref,
    tokens_ref,
    w_out_ref,
    gain_ref,
    w_plane_ref,
    plane_in_ref,
    planes_ref,
    values_ref,
    scores_ref,
    maxes_ref,
    attended_ref,
    *,
    tile,
):
    rows, width = q_ref.shape
    count = k_ref.shape[0]
    pairs = width // LANES
    low = lax.broadcasted_iota(jnp.int32, (1, LANES), 1) < LANES // 2
    turned = (((1,), (1,)), ((), ()))

    def score(pair_id, head):
        span = pl.ds(pl.multiple_of(pair_id * LANES, LANES), LANES)
        own = jnp.where(low if head == 0 else ~low, q_ref[:, span], jnp.zeros((), bf16))
        scores = lax.dot_general(own, k_ref[:, span], turned, preferred_element_type=f32)
        scores_ref[head] = scores
        highest = scores[:, :LANES]
        for first in range(LANES, count, LANES):
            highest = jnp.maximum(highest, scores[:, first : first + LANES])
        maxes_ref[head] = highest

    def weigh(head):
        row_max = jnp.max(maxes_ref[head], axis=1, keepdims=True)
        terms = jnp.exp2(scores_ref[head] - row_max).astype(bf16)
        return jnp.dot(terms, values_ref[head], preferred_element_type=f32)

    score(0, 0)

    def pair(pair_id, carry):
        span = pl.ds(pl.multiple_of(pair_id * LANES, LANES), LANES)
        values = v_ref[:, span]
        one = jnp.ones((), bf16)
        values_ref[0] = jnp.where(low, values, one)
        values_ref[1] = jnp.where(low, one, values)
        score(pair_id, 1)
        first = weigh(0)
        score((pair_id + 1) % pairs, 0)
        second = weigh(1)
        row_sum = pltpu.roll(jnp.where(low, second, first), LANES // 2, 1)
        attended_ref[:, span] = (jnp.where(low, first, second) / row_sum).astype(bf16)
        return carry

    lax.fori_loop(0, pairs, pair, 0)

    def project(step, carry):
        span = pl.ds(pl.multiple_of(step * tile, tile), tile)
        mixed = tokens_ref[span, :].astype(f32) + jnp.dot(
            attended_ref[span, :], w_out_ref[...], preferred_element_type=f32
        )
        mixed = mixed.astype(bf16).astype(f32)
        plane_in = (plain_norm(mixed) * gain_ref[...]).astype(bf16)
        plane_in_ref[span, :] = plane_in
        planes_ref[:, span] = lax.dot_general(
            w_plane_ref[...], plane_in, turned, preferred_element_type=f32
        ).astype(bf16)
        return carry

    lax.fori_loop(0, rows // tile, project, 0)


def attention(queries, keys, values, tokens, w_out, gain, w_plane):
    rows, width = queries.shape
    count = values.shape[0]
    channels = w_plane.shape[1]
    return pl.pallas_call(
        functools.partial(attention_kernel, tile=256),
        out_shape=(
            jax.ShapeDtypeStruct((rows, width), bf16),
            jax.ShapeDtypeStruct((channels, rows), bf16),
        ),
        in_specs=in_vmem(7),
        out_specs=tuple(in_vmem(2)),
        scratch_shapes=[
            pltpu.VMEM((2, count, LANES), bf16),
            pltpu.VMEM((2, rows, count), f32),
            pltpu.VMEM((2, rows, LANES), f32),
            pltpu.VMEM((rows, width), bf16),
        ],
        compiler_params=pltpu.CompilerParams(
            vmem_limit_bytes=36 * 1024 * 1024,
        ),
        cost_estimate=pl.CostEstimate(
            flops=4 * rows * count * width,
            bytes_accessed=4 * (rows + count) * width,
            transcendentals=rows * count * HEADS,
        ),
        name="attention",
    )(queries, keys, values, tokens, w_out, gain[None, :], w_plane.T)


MESH_ID = pl.DeviceIdType.MESH


def greet(peers):
    barrier = pltpu.get_barrier_semaphore()
    for peer in peers:
        pl.semaphore_signal(barrier, inc=1, device_id=peer, device_id_type=MESH_ID)
    pl.semaphore_wait(barrier, len(peers))


def remote(source, target, send_sem, recv_sem, peer):
    return pltpu.make_async_remote_copy(
        src_ref=source,
        dst_ref=target,
        send_sem=send_sem,
        recv_sem=recv_sem,
        device_id=peer,
        device_id_type=MESH_ID,
    )


def partner_of(me):
    return me + 1 - 2 * (me % 2)


RING = 4
SENDS, ARRIVALS = 25, 13


class Exchange:
    def __init__(self, block_ref, out_ref, axis, sems):
        self.block, self.out, self.axis = block_ref, out_ref, axis
        self.send_sem, self.recv_sem, self.land_sem, self.own_sem = sems
        me = lax.axis_index("seq")
        self.me = me
        self.core = me % 2
        self.y = (me // 2) % 2
        self.x = me // 4
        self.extent = block_ref.shape[axis]
        self.started = []
        self.right = {"seq": self.at(1, 0)}
        self.left = {"seq": self.at(-1, 0)}
        self.over = {"seq": self.at(0, 1)}
        self.partner = {"seq": partner_of(me)}

    def at(self, dx, dy):
        return 4 * ((self.x + dx + RING) % RING) + 2 * ((self.y + dy) % 2) + self.core

    def place(self, owner, half=None):
        size = self.extent if half is None else self.extent // 2
        start = owner * self.extent + (0 if half is None else half * size)
        span = pl.ds(pl.multiple_of(start, size), size)
        return self.out.at[span, :] if self.axis == 0 else self.out.at[:, span]

    def push(self, source, owner, half, recv, peer):
        remote(
            source, self.place(owner, half), self.send_sem.at[len(self.started)], recv, peer
        ).start()
        self.started.append(half)

    def relay(self, owner, half, recv, peer):
        self.push(self.place(owner, half), owner, half, recv, peer)

    def hear(self, owner, half, sem):
        spot = self.place(owner, half)
        remote(spot, spot, self.send_sem.at[0], sem, self.partner).wait_recv()

    def begin(self):
        self.own = pltpu.make_async_copy(self.block, self.place(self.me), self.own_sem)
        self.own.start()
        recv, land = self.recv_sem, self.land_sem
        for half in range(2):
            size = self.extent // 2
            span = pl.ds(half * size, size)
            part = self.block.at[span, :] if self.axis == 0 else self.block.at[:, span]
            self.push(part, self.me, half, recv.at[2 + half], self.over)
        self.push(self.block, self.me, None, recv.at[0], self.right)
        self.push(self.block, self.me, None, recv.at[1], self.left)
        self.push(self.block, self.me, None, land.at[12], self.partner)

    def arrive(self, number, dx, dy, half, onward):
        owner = self.at(dx, dy)
        self.hear(owner, half, self.recv_sem.at[number])
        for part, target, peer in onward:
            self.relay(owner, part, self.recv_sem.at[target], peer)
        self.relay(owner, half, self.land_sem.at[number], self.partner)

    def beside(self):
        self.arrive(0, -1, 0, None, [(0, 8, self.right)])
        self.arrive(1, 1, 0, None, [(1, 9, self.left)])

    def across(self, half):
        self.arrive(
            2 + half, 0, 1, half, [(half, 4 + half, self.right), (half, 6 + half, self.left)]
        )

    def opposite(self):
        self.arrive(8, 2, 0, 0, [])
        self.arrive(9, 2, 0, 1, [])

    def beside_across(self, half):
        self.arrive(4 + half, -1, 1, half, [(0, 10, self.right)] if half == 0 else [])
        self.arrive(6 + half, 1, 1, half, [(1, 11, self.left)] if half == 1 else [])

    def opposite_across(self):
        self.arrive(10, 2, 1, 0, [])
        self.arrive(11, 2, 1, 1, [])

    def crossed(self):
        self.across(0)
        self.across(1)

    def crossed_beside(self):
        self.beside_across(0)
        self.beside_across(1)

    def handed(self, number, dx, dy, half):
        other = self.at(dx, dy) + 1 - 2 * self.core
        self.hear(other, half, self.land_sem.at[number])

    def finish(self):
        for number, half in enumerate(self.started):
            spot = self.place(self.me, half)
            remote(
                spot, spot, self.send_sem.at[number], self.recv_sem.at[0], self.partner
            ).wait_send()

    def neighbours(self):
        return [self.right, self.left, self.over, self.partner]


def exchange_sems():
    sems = pltpu.SemaphoreType.DMA
    return [sems((SENDS,)), sems((ARRIVALS,)), sems((ARRIVALS,)), sems]


def front_kernel(
    tokens_hbm,
    image_hbm,
    w_query_hbm,
    w_key_hbm,
    w_value_hbm,
    q_ref,
    k_ref,
    v_ref,
    tokens_ref,
    image_ref,
    images_ref,
    w_query_ref,
    w_key_ref,
    w_value_ref,
    load_sem,
    *sems,
    tile,
    scale,
):
    ring = Exchange(image_ref, images_ref, 0, sems)
    loads = []
    for number, (source, target) in enumerate(
        (
            (image_hbm, image_ref),
            (tokens_hbm, tokens_ref),
            (w_query_hbm, w_query_ref),
            (w_key_hbm, w_key_ref),
            (w_value_hbm, w_value_ref),
        )
    ):
        copy = pltpu.make_async_copy(source, target, load_sem.at[number])
        copy.start()
        loads.append(copy)
    greet(ring.neighbours())
    loads[0].wait()
    ring.begin()

    def query(step):
        span = pl.ds(step * tile, tile)
        normed = plain_norm(tokens_ref[span, :].astype(f32)).astype(bf16)
        product = jnp.dot(normed, w_query_ref[...], preferred_element_type=f32)
        q_ref[span, :] = (product * scale).astype(bf16)

    def keys_values(dx, dy):
        owner = ring.at(dx, dy) // 2
        rows = 2 * image_ref.shape[0]
        span = pl.ds(pl.multiple_of(owner * rows, rows), rows)
        images = images_ref[span, :]
        k_ref[span, :] = jnp.dot(
            images, w_key_ref[...], preferred_element_type=f32
        ).astype(bf16)
        v_ref[span, :] = jnp.dot(
            images, w_value_ref[...], preferred_element_type=f32
        ).astype(bf16)

    loads[1].wait()
    loads[2].wait()
    query(0)
    query(1)
    ring.beside()
    ring.across(0)
    query(2)
    ring.across(1)
    loads[3].wait()
    loads[4].wait()
    ring.own.wait()
    ring.handed(12, 0, 0, None)
    keys_values(0, 0)
    ring.handed(0, -1, 0, None)
    keys_values(-1, 0)
    ring.opposite()
    ring.beside_across(0)
    ring.handed(1, 1, 0, None)
    keys_values(1, 0)
    ring.handed(2, 0, 1, 0)
    ring.handed(3, 0, 1, 1)
    keys_values(0, 1)
    ring.beside_across(1)
    ring.handed(8, 2, 0, 0)
    ring.handed(9, 2, 0, 1)
    keys_values(2, 0)
    ring.handed(4, -1, 1, 0)
    ring.handed(5, -1, 1, 1)
    keys_values(-1, 1)
    ring.handed(6, 1, 1, 0)
    ring.handed(7, 1, 1, 1)
    keys_values(1, 1)
    ring.opposite_across()
    ring.handed(10, 2, 1, 0)
    ring.handed(11, 2, 1, 1)
    keys_values(2, 1)
    ring.finish()


def front(tokens, images, w_query, w_key, w_value, size, scale, collective_id):
    rows, width = tokens.shape
    depth = images.shape[1]
    count = images.shape[0] * size
    heads = w_key.shape[1]
    return pl.pallas_call(
        functools.partial(front_kernel, tile=rows // 3, scale=scale),
        out_shape=(
            jax.ShapeDtypeStruct((rows, width), bf16),
            jax.ShapeDtypeStruct((count, heads), bf16),
            jax.ShapeDtypeStruct((count, heads), bf16),
        ),
        in_specs=[pl.BlockSpec(memory_space=pltpu.HBM)] * 5,
        out_specs=tuple(in_vmem(3)),
        scratch_shapes=[
            pltpu.VMEM(tokens.shape, bf16),
            pltpu.VMEM(images.shape, bf16),
            pltpu.VMEM((count, depth), bf16),
            pltpu.VMEM(w_query.shape, bf16),
            pltpu.VMEM(w_key.shape, bf16),
            pltpu.VMEM(w_value.shape, bf16),
            pltpu.SemaphoreType.DMA((5,)),
            *exchange_sems(),
        ],
        compiler_params=pltpu.CompilerParams(
            collective_id=collective_id,
            has_side_effects=True,
            vmem_limit_bytes=24 * 1024 * 1024,
        ),
        name="front",
    )(
        *(
            pltpu.with_memory_space_constraint(array, pltpu.HBM)
            for array in (tokens, images, w_query, w_key, w_value)
        )
    )


def table_rows(col_ref, row_ref, plane, first_row, row_count, start, width, side):
    span = pl.ds(start, width)
    pieces = side // 16
    upper = col_ref[2 * plane, :, span].reshape(pieces, 16, width)
    lower = col_ref[2 * plane + 1, :, span].reshape(pieces, 16, width)
    cell_row = row_ref[plane, :, span]
    zero = jnp.zeros((16, width), bf16)
    row_id = jnp.asarray(first_row, jnp.int32)
    before = cell_row == (row_id - 1).astype(bf16)
    blocks = []
    for step in range(row_count):
        here = cell_row == (row_id + step).astype(bf16)
        for piece in range(pieces):
            blocks.append(
                jnp.where(here, upper[piece], jnp.where(before, lower[piece], zero))
            )
        before = here
    return jnp.concatenate(blocks, axis=0)


def ray_scan(values, lane, reverse):
    width = values.shape[1]
    shift = 1
    while shift < STEPS:
        if reverse:
            moved = pltpu.roll(values, width - shift, 1)
            values = values + jnp.where(lane < STEPS - shift, moved, 0.0)
        else:
            moved = pltpu.roll(values, shift, 1)
            values = values + jnp.where(lane >= shift, moved, 0.0)
        shift *= 2
    return values


def parts_of(values):
    first = values.astype(bf16)
    rest = values - first.astype(f32)
    second = rest.astype(bf16)
    third = (rest - second.astype(f32)).astype(bf16)
    return jnp.concatenate([first, second, third], axis=0)


def join(product):
    count = product.shape[0] // 3
    return product[:count] + product[count : 2 * count] + product[2 * count :]


def column_of(row_ref):
    count = row_ref.shape[1]
    diagonal = lax.broadcasted_iota(jnp.int32, (count, count), 0) == lax.broadcasted_iota(
        jnp.int32, (count, count), 1
    )
    return jnp.sum(jnp.where(diagonal, row_ref[...], 0.0), axis=1, keepdims=True)


def token_rows(col_ref, row_ref, chip, start, width, side, grid_rows):
    blocks = []
    for group in range(grid_rows // 4):
        number = chip * (grid_rows // 4) + group
        plane = number // (side // 4)
        first = (number - plane * (side // 4)) * 4
        blocks.append(table_rows(col_ref, row_ref, plane, first, 4, start, width, side))
    return jnp.concatenate(blocks, axis=0)


def scene_kernel(
    block_ref,
    plane_in_ref,
    idx_ref,
    wts_ref,
    target_ref,
    w_plane_ref,
    w1_ref,
    b1_ref,
    w2_ref,
    b2_ref,
    w3_ref,
    b3_ref,
    colors_ref,
    token_grad_ref,
    total_ref,
    planes_ref,
    col_ref,
    row_ref,
    features_ref,
    fgrad_ref,
    z1_ref,
    z2_ref,
    decoded_ref,
    give_ref,
    keep_ref,
    pair_ref,
    stage_ref,
    half_ref,
    side_ref,
    over_ref,
    part_ref,
    chunk_land_ref,
    chunk_ref,
    scene_ref,
    last_ref,
    pair_send,
    pair_recv,
    half_send,
    half_recv,
    side_send,
    side_recv,
    over_send,
    over_recv,
    chunk_send,
    chunk_recv,
    scene_send,
    scene_recv,
    last_send,
    last_recv,
    *ring_sems,
    side,
    size,
    scenes,
    prep_width,
    width,
    tile,
):
    samples = idx_ref.shape[1]
    channels, tokens = planes_ref.shape
    extent = block_ref.shape[1]
    half_extent = extent // 2
    plane_size = side * side
    chip_tokens = 2 * extent
    grid_rows = chip_tokens // side
    chips = size // 2
    turned = (((1,), (1,)), ((), ()))
    flip = (((0,), (0,)), ((), ()))

    ring = Exchange(block_ref, planes_ref, 1, ring_sems)
    me, core = ring.me, ring.core
    scene = lax.axis_index("dp")
    others = [(me + step) % size for step in range(1, size)]
    other_scenes = [(scene + step) % scenes for step in range(1, scenes)]
    greet([{"seq": owner} for owner in others] + [{"dp": owner} for owner in other_scenes])
    ring.begin()

    def chip_at(dx, dy):
        return 2 * ((ring.x + dx) % RING) + (ring.y + dy) % 2

    def prepare(step, carry):
        start = pl.multiple_of(step * prep_width, prep_width)
        span = pl.ds(start, prep_width)
        index = idx_ref[:, span]
        weight = wts_ref[:, span].astype(f32)
        column_id = lax.broadcasted_iota(jnp.int32, (side, prep_width), 0)
        for plane in range(PLANES):
            in_plane = (index >= plane * plane_size) & (index < (plane + 1) * plane_size)
            base = jnp.min(jnp.where(in_plane, index, tokens), axis=0, keepdims=True)
            corner = []
            for offset in (0, 1, side, side + 1):
                corner.append(
                    jnp.sum(
                        jnp.where(index == base + offset, weight, 0.0), axis=0, keepdims=True
                    )
                )
            local = base - plane * plane_size
            cell_row = local // side
            column = local - cell_row * side
            for which in range(2):
                col_ref[2 * plane + which, :, span] = jnp.where(
                    column_id == column,
                    corner[2 * which],
                    jnp.where(column_id == column + 1, corner[2 * which + 1], 0.0),
                ).astype(bf16)
            row_ref[plane, :, span] = jnp.broadcast_to(
                cell_row.astype(f32), (16, prep_width)
            ).astype(bf16)
        return carry

    lax.fori_loop(0, samples // prep_width, prepare, 0)

    w1, w2, w3 = w1_ref[...], w2_ref[...], w3_ref[...]
    b1, b2, b3 = column_of(b1_ref), column_of(b2_ref), column_of(b3_ref)
    features_ref[...] = jnp.zeros_like(features_ref)

    arrivals = (
        ((), ((12, 0, 0, None),)),
        ((ring.beside, ring.crossed), ((1, 1, 0, None),)),
        ((), ((0, -1, 0, None),)),
        ((ring.opposite, ring.crossed_beside), ((8, 2, 0, 0), (9, 2, 0, 1))),
        ((), ((2, 0, 1, 0), (3, 0, 1, 1))),
        ((ring.opposite_across,), ((6, 1, 1, 0), (7, 1, 1, 1))),
        ((), ((4, -1, 1, 0), (5, -1, 1, 1))),
        ((), ((10, 2, 1, 0), (11, 2, 1, 1))),
    )

    def interpolate(step, carry):
        for number, (receive, handed) in enumerate(arrivals):

            @pl.when(step == number)
            def _(number=number, receive=receive, handed=handed):
                for take in receive:
                    take()
                if number == 0:
                    ring.own.wait()
                for item in handed:
                    ring.handed(*item)

        place = step % 4
        chip = chip_at(place + place // 2 - 2 * (place // 3), step // 4)
        block = pl.ds(pl.multiple_of(chip * chip_tokens, chip_tokens), chip_tokens)

        def add(part, inner):
            start = pl.multiple_of(part * width, width)
            span = pl.ds(start, width)
            table = token_rows(col_ref, row_ref, chip, start, width, side, grid_rows)
            features_ref[:, span] = features_ref[:, span] + jnp.dot(
                planes_ref[:, block], table, preferred_element_type=f32
            )
            return inner

        lax.fori_loop(0, samples // width, add, 0)
        return carry

    lax.fori_loop(0, chips, interpolate, 0)

    def decode(step, carry):
        span = pl.ds(pl.multiple_of(step * prep_width, prep_width), prep_width)
        z1 = jnp.dot(w1, features_ref[:, span].astype(bf16), preferred_element_type=f32) + b1
        z1_ref[:, span] = z1
        h1 = (z1 * jax.nn.sigmoid(z1)).astype(bf16)
        z2 = jnp.dot(w2, h1, preferred_element_type=f32) + b2
        z2_ref[:, span] = z2
        h2 = (z2 * jax.nn.sigmoid(z2)).astype(bf16)
        decoded_ref[:, span] = jnp.dot(w3, h2, preferred_element_type=f32) + b3
        return carry

    lax.fori_loop(0, samples // prep_width, decode, 0)

    rays = samples // STEPS
    lane = lax.broadcasted_iota(jnp.int32, (1, samples), 1) % STEPS
    density = decoded_ref[0:1]
    optical = (jnp.maximum(density, 0.0) + jnp.log1p(jnp.exp(-jnp.abs(density)))) * DEPTH_STEP
    albedo = jax.nn.sigmoid(decoded_ref[1:4])
    reach = jnp.exp(optical - ray_scan(optical, lane, False))
    passed = jnp.exp(-optical)
    weight = reach * (1.0 - passed)
    spread = (
        lax.broadcasted_iota(jnp.int32, (rays, samples), 0)
        == lax.broadcasted_iota(jnp.int32, (rays, samples), 1) // STEPS
    ).astype(bf16)
    colors = join(
        lax.dot_general(
            parts_of(weight * albedo), spread, turned, preferred_element_type=f32
        )
    )
    colors_ref[...] = colors
    miss = join(
        jnp.dot(parts_of(colors - target_ref[...]), spread, preferred_element_type=f32)
    )
    weight_grad = jnp.sum(miss * albedo, axis=0, keepdims=True)
    term = weight_grad * weight
    later = ray_scan(term, lane, True) - term
    optical_grad = weight_grad * reach * passed - later
    decoded_ref[0:1] = optical_grad * (DEPTH_STEP * jax.nn.sigmoid(density))
    decoded_ref[1:4] = miss * weight * albedo * (1.0 - albedo)

    def silu_grad(pre):
        gate = jax.nn.sigmoid(pre)
        return gate * (1.0 + pre * (1.0 - gate))

    def decode_back(step, carry):
        span = pl.ds(pl.multiple_of(step * prep_width, prep_width), prep_width)
        g2 = lax.dot_general(
            w3, decoded_ref[:, span].astype(bf16), flip, preferred_element_type=f32
        )
        g2 = g2.astype(bf16).astype(f32) * silu_grad(z2_ref[:, span])
        g1 = lax.dot_general(w2, g2.astype(bf16), flip, preferred_element_type=f32)
        g1 = g1.astype(bf16).astype(f32) * silu_grad(z1_ref[:, span])
        fgrad_ref[:, span] = lax.dot_general(
            w1, g1.astype(bf16), flip, preferred_element_type=f32
        ).astype(bf16)
        return carry

    lax.fori_loop(0, samples // prep_width, decode_back, 0)

    def swap(number):
        return remote(
            give_ref.at[number],
            pair_ref.at[number],
            pair_send.at[number],
            pair_recv.at[number],
            ring.partner,
        )

    def push_half(way, row, number):
        part = pl.ds(way * half_extent, half_extent)
        return remote(
            stage_ref.at[number, :, part],
            half_ref.at[way, row],
            half_send.at[way, row],
            half_recv.at[way, row],
            ring.right if way == 0 else ring.left,
        )

    def push_side(way, row, number):
        return remote(
            stage_ref.at[number],
            side_ref.at[way, row],
            side_send.at[way, row],
            side_recv.at[way, row],
            ring.right if way == 0 else ring.left,
        )

    def push_over(number):
        return remote(stage_ref.at[number], over_ref, over_send, over_recv, ring.over)

    def stage(number):
        swap(number).wait_recv()
        row = 1 - number // 4
        kind = number % 4
        both = keep_ref[...] + pair_ref[number].astype(f32)
        if kind == 0:
            stage_ref[number] = both.astype(bf16)
            push_half(0, row, number).start()
            push_half(1, row, number).start()
        elif kind < 3:
            way = kind - 1
            push_half(way, row, number).wait_recv()
            part = pl.ds(way * half_extent, half_extent)
            stage_ref[number] = both.astype(bf16)
            first = way * half_extent
            stage_ref[number, :, part] = (
                both[:, first : first + half_extent] + half_ref[way, row].astype(f32)
            ).astype(bf16)
            push_side(way, row, number).start()
        else:
            for way in range(2):
                push_side(way, row, number).wait_recv()
                both = both + side_ref[way, row].astype(f32)
            if row == 1:
                stage_ref[number] = both.astype(bf16)
                push_over(number).start()
        return both

    def spread_back(step, carry):
        place = step % 4
        across = 2 + 3 * place + 3 * (place // 2) + 2 * (place // 3)
        chip = chip_at(across, 1 - step // 4)

        def product(owner):
            table = token_rows(col_ref, row_ref, owner, 0, samples, side, extent // side)
            return lax.dot_general(fgrad_ref[...], table, turned, preferred_element_type=f32)

        give_ref[step] = product(2 * chip + 1 - core).astype(bf16)
        swap(step).start()
        keep_ref[...] = product(2 * chip + core)
        for number in range(chips - 1):

            @pl.when(step == number)
            def _(number=number):
                stage(number)

        return carry

    lax.fori_loop(0, chips, spread_back, 0)
    both = stage(chips - 1)
    push_over(3).wait_recv()
    own_grad = (both + over_ref[...].astype(f32)).astype(bf16)

    rows, lanes = chunk_ref.shape

    def chunk_of(owner):
        return (
            pl.ds(pl.multiple_of((owner % 2) * rows, rows), rows),
            pl.ds(pl.multiple_of((owner // 2) * lanes, lanes), lanes),
        )

    part_ref[0:channels] = jnp.dot(
        own_grad, plane_in_ref[...], preferred_element_type=f32
    ).astype(bf16)
    part_ref[channels:] = jnp.zeros((2 * rows - channels, part_ref.shape[1]), bf16)
    waiting = []
    for owner in others:
        copy = remote(
            part_ref.at[chunk_of(owner)],
            chunk_land_ref.at[me],
            chunk_send.at[owner],
            chunk_recv.at[me],
            {"seq": owner},
        )
        copy.start()
        waiting.append(copy)
    for first in range(0, extent, tile):
        token_grad_ref[first : first + tile, :] = lax.dot_general(
            own_grad[:, first : first + tile],
            w_plane_ref[...],
            flip,
            preferred_element_type=f32,
        ).astype(bf16)
    chunk = part_ref[chunk_of(me)].astype(f32)
    for owner in others:
        remote(
            last_ref.at[chunk_of(me)],
            chunk_land_ref.at[owner],
            chunk_send.at[owner],
            chunk_recv.at[owner],
            ring.partner,
        ).wait_recv()
        chunk = chunk + chunk_land_ref[owner].astype(f32)
    chunk_ref[...] = chunk
    scene_ref[scene] = chunk
    for other in other_scenes:
        copy = remote(
            chunk_ref,
            scene_ref.at[scene],
            scene_send.at[other],
            scene_recv.at[scene],
            {"dp": other},
        )
        copy.start()
        waiting.append(copy)
    for other in other_scenes:
        remote(
            chunk_ref,
            scene_ref.at[other],
            scene_send.at[other],
            scene_recv.at[other],
            ring.partner,
        ).wait_recv()
    final = scene_ref[0]
    for other in range(1, scenes):
        final = final + scene_ref[other]
    spot = chunk_of(me)
    last_ref[spot] = final.astype(bf16)
    for owner in others:
        copy = remote(
            last_ref.at[spot],
            last_ref.at[spot],
            last_send.at[owner],
            last_recv.at[me],
            {"seq": owner},
        )
        copy.start()
        waiting.append(copy)
    for owner in others:
        there = chunk_of(owner)
        remote(
            last_ref.at[there],
            last_ref.at[there],
            last_send.at[owner],
            last_recv.at[owner],
            ring.partner,
        ).wait_recv()
    total_ref[...] = last_ref[0:channels].astype(f32)
    for copy in waiting:
        copy.wait_send()
    for number in range(chips):
        swap(number).wait_send()
    for row in range(2):
        base = 4 * (1 - row)
        for way in range(2):
            push_half(way, row, base).wait_send()
            push_side(way, row, base + 1 + way).wait_send()
    push_over(3).wait_send()
    ring.finish()


def render_scene(
    block,
    plane_in,
    index,
    weight,
    target,
    w_plane,
    w1,
    b1,
    w2,
    b2,
    w3,
    b3,
    size,
    scenes,
    collective_id,
):
    channels, extent = block.shape
    width = plane_in.shape[1]
    samples = index.shape[1]
    tokens = extent * size
    side = math.isqrt(tokens // PLANES)
    chips = size // 2
    rows, lanes = -(-channels // 32) * 16, width // chips
    sems = pltpu.SemaphoreType.DMA
    return pl.pallas_call(
        functools.partial(
            scene_kernel,
            side=side,
            size=size,
            scenes=scenes,
            prep_width=1024,
            width=2048,
            tile=256,
        ),
        out_shape=(
            jax.ShapeDtypeStruct(target.shape, f32),
            jax.ShapeDtypeStruct((extent, width), bf16),
            jax.ShapeDtypeStruct((channels, width), f32),
        ),
        in_specs=in_vmem(12),
        out_specs=tuple(in_vmem(3)),
        scratch_shapes=[
            pltpu.VMEM((channels, tokens), bf16),
            pltpu.VMEM((2 * PLANES, side, samples), bf16),
            pltpu.VMEM((PLANES, 16, samples), bf16),
            pltpu.VMEM((channels, samples), f32),
            pltpu.VMEM((channels, samples), bf16),
            pltpu.VMEM((w1.shape[0], samples), f32),
            pltpu.VMEM((w2.shape[0], samples), f32),
            pltpu.VMEM((w3.shape[0], samples), f32),
            pltpu.VMEM((chips, channels, extent), bf16),
            pltpu.VMEM((channels, extent), f32),
            pltpu.VMEM((chips, channels, extent), bf16),
            pltpu.VMEM((chips, channels, extent), bf16),
            pltpu.VMEM((2, 2, channels, extent // 2), bf16),
            pltpu.VMEM((2, 2, channels, extent), bf16),
            pltpu.VMEM((channels, extent), bf16),
            pltpu.VMEM((2 * rows, width), bf16),
            pltpu.VMEM((size, rows, lanes), bf16),
            pltpu.VMEM((rows, lanes), f32),
            pltpu.VMEM((scenes, rows, lanes), f32),
            pltpu.VMEM((2 * rows, width), bf16),
            sems((chips,)),
            sems((chips,)),
            sems((2, 2)),
            sems((2, 2)),
            sems((2, 2)),
            sems((2, 2)),
            sems,
            sems,
            sems((size,)),
            sems((size,)),
            sems((scenes,)),
            sems((scenes,)),
            sems((size,)),
            sems((size,)),
            *exchange_sems(),
        ],
        compiler_params=pltpu.CompilerParams(
            collective_id=collective_id,
            has_side_effects=True,
            vmem_limit_bytes=40 * 1024 * 1024,
        ),
        name="scene",
    )(
        block,
        plane_in,
        index,
        weight,
        target,
        w_plane.T,
        w1,
        b1[None, :],
        w2,
        b2[None, :],
        w3,
        b3[None, :],
    )


def body(
    tokens,
    image_tokens,
    norm_gain,
    w_query,
    w_key,
    w_value,
    w_out,
    w_plane,
    dec_w1,
    dec_b1,
    dec_w2,
    dec_b2,
    dec_w3,
    dec_b3,
    corner_idx,
    corner_wts,
    target_color,
):
    own_tokens = tokens[0]
    model_width = own_tokens.shape[1]
    head_dim = model_width // HEADS
    size = lax.axis_size("seq")
    score_scale = math.log2(math.e) / math.sqrt(head_dim)
    queries, keys, values = front(
        own_tokens, image_tokens[0], w_query, w_key, w_value, size, score_scale, 0
    )
    plane_in, planes = attention(
        queries, keys, values, own_tokens, w_out, norm_gain, w_plane
    )
    colors, token_grad, weight_grad = render_scene(
        planes,
        plane_in,
        corner_idx[0],
        corner_wts[0],
        target_color[0],
        w_plane,
        dec_w1,
        dec_b1,
        dec_w2,
        dec_b2,
        dec_w3,
        dec_b3,
        size,
        lax.axis_size("dp"),
        1,
    )
    return (colors[None], token_grad[None], weight_grad.T)


def solution(mesh):
    in_specs = (
        P("dp", "seq", None),
        P("dp", "seq", None),
        *(P() for _ in range(12)),
        P("dp", None, "seq"),
        P("dp", None, "seq"),
        P("dp", None, "seq"),
    )
    out_specs = (P("dp", None, "seq"), P("dp", "seq", None), P())
    return jax.shard_map(body, mesh=mesh, in_specs=in_specs, out_specs=out_specs, check_vma=False)
```

```python
import functools
import math

import jax
import jax.numpy as jnp
from jax import lax
from jax.experimental import pallas as pl
from jax.experimental.pallas import tpu as pltpu
from jax.sharding import PartitionSpec as P

HEADS = 16
STEPS = 128
PLANES = 3
LANES = 128
NORM_EPS = 1e-05
DEPTH_STEP = 0.02
VMEM_BYTES = 60000 * 1024

bf16 = jnp.bfloat16
f32 = jnp.float32


def in_vmem(count):
    return [pl.BlockSpec(memory_space=pltpu.VMEM)] * count


def plain_norm(inputs):
    row_mean = jnp.mean(inputs, axis=-1, keepdims=True)
    centred = inputs - row_mean
    row_var = jnp.mean(centred * centred, axis=-1, keepdims=True)
    return centred * lax.rsqrt(row_var + NORM_EPS)


def attention_kernel(
    q_ref,
    k_ref,
    v_ref,
    tokens_ref,
    w_out_ref,
    gain_ref,
    w_plane_ref,
    plane_in_ref,
    planes_ref,
    values_ref,
    scores_ref,
    maxes_ref,
    attended_ref,
    *,
    tile,
):
    rows, width = q_ref.shape
    count = k_ref.shape[0]
    pairs = width // LANES
    low = lax.broadcasted_iota(jnp.int32, (1, LANES), 1) < LANES // 2
    turned = (((1,), (1,)), ((), ()))

    def score(pair_id, head):
        span = pl.ds(pl.multiple_of(pair_id * LANES, LANES), LANES)
        own = jnp.where(low if head == 0 else ~low, q_ref[:, span], jnp.zeros((), bf16))
        scores = lax.dot_general(own, k_ref[:, span], turned, preferred_element_type=f32)
        scores_ref[head] = scores
        highest = scores[:, :LANES]
        for first in range(LANES, count, LANES):
            highest = jnp.maximum(highest, scores[:, first : first + LANES])
        maxes_ref[head] = highest

    def weigh(head):
        row_max = jnp.max(maxes_ref[head], axis=1, keepdims=True)
        terms = jnp.exp2(scores_ref[head] - row_max).astype(bf16)
        return jnp.dot(terms, values_ref[head], preferred_element_type=f32)

    score(0, 0)

    def pair(pair_id, carry):
        span = pl.ds(pl.multiple_of(pair_id * LANES, LANES), LANES)
        values = v_ref[:, span]
        one = jnp.ones((), bf16)
        values_ref[0] = jnp.where(low, values, one)
        values_ref[1] = jnp.where(low, one, values)
        score(pair_id, 1)
        first = weigh(0)
        score((pair_id + 1) % pairs, 0)
        second = weigh(1)
        row_sum = pltpu.roll(jnp.where(low, second, first), LANES // 2, 1)
        attended_ref[:, span] = (jnp.where(low, first, second) / row_sum).astype(bf16)
        return carry

    lax.fori_loop(0, pairs, pair, 0)

    def project(step, carry):
        span = pl.ds(pl.multiple_of(step * tile, tile), tile)
        mixed = tokens_ref[span, :].astype(f32) + jnp.dot(
            attended_ref[span, :], w_out_ref[...], preferred_element_type=f32
        )
        mixed = mixed.astype(bf16).astype(f32)
        plane_in = (plain_norm(mixed) * gain_ref[...]).astype(bf16)
        plane_in_ref[span, :] = plane_in
        planes_ref[:, span] = lax.dot_general(
            w_plane_ref[...], plane_in, turned, preferred_element_type=f32
        ).astype(bf16)
        return carry

    lax.fori_loop(0, rows // tile, project, 0)


def attention(queries, keys, values, tokens, w_out, gain, w_plane):
    rows, width = queries.shape
    count = values.shape[0]
    channels = w_plane.shape[1]
    return pl.pallas_call(
        functools.partial(attention_kernel, tile=256),
        out_shape=(
            jax.ShapeDtypeStruct((rows, width), bf16),
            jax.ShapeDtypeStruct((channels, rows), bf16),
        ),
        in_specs=in_vmem(7),
        out_specs=tuple(in_vmem(2)),
        scratch_shapes=[
            pltpu.VMEM((2, count, LANES), bf16),
            pltpu.VMEM((2, rows, count), f32),
            pltpu.VMEM((2, rows, LANES), f32),
            pltpu.VMEM((rows, width), bf16),
        ],
        compiler_params=pltpu.CompilerParams(
            vmem_limit_bytes=36 * 1024 * 1024,
        ),
        cost_estimate=pl.CostEstimate(
            flops=4 * rows * count * width,
            bytes_accessed=4 * (rows + count) * width,
            transcendentals=rows * count * HEADS,
        ),
        name="attention",
    )(queries, keys, values, tokens, w_out, gain[None, :], w_plane.T)


MESH_ID = pl.DeviceIdType.MESH


def greet(peers):
    barrier = pltpu.get_barrier_semaphore()
    for peer in peers:
        pl.semaphore_signal(barrier, inc=1, device_id=peer, device_id_type=MESH_ID)
    pl.semaphore_wait(barrier, len(peers))


def remote(source, target, send_sem, recv_sem, peer):
    return pltpu.make_async_remote_copy(
        src_ref=source,
        dst_ref=target,
        send_sem=send_sem,
        recv_sem=recv_sem,
        device_id=peer,
        device_id_type=MESH_ID,
    )


def partner_of(me):
    return me + 1 - 2 * (me % 2)


RING = 4
SENDS, ARRIVALS = 25, 13


class Exchange:
    def __init__(self, block_ref, out_ref, axis, sems):
        self.block, self.out, self.axis = block_ref, out_ref, axis
        self.send_sem, self.recv_sem, self.land_sem, self.own_sem = sems
        me = lax.axis_index("seq")
        self.me = me
        self.core = me % 2
        self.y = (me // 2) % 2
        self.x = me // 4
        self.extent = block_ref.shape[axis]
        self.started = []
        self.right = {"seq": self.at(1, 0)}
        self.left = {"seq": self.at(-1, 0)}
        self.over = {"seq": self.at(0, 1)}
        self.partner = {"seq": partner_of(me)}

    def at(self, dx, dy):
        return 4 * ((self.x + dx + RING) % RING) + 2 * ((self.y + dy) % 2) + self.core

    def place(self, owner, half=None):
        size = self.extent if half is None else self.extent // 2
        start = owner * self.extent + (0 if half is None else half * size)
        span = pl.ds(pl.multiple_of(start, size), size)
        return self.out.at[span, :] if self.axis == 0 else self.out.at[:, span]

    def push(self, source, owner, half, recv, peer):
        remote(
            source, self.place(owner, half), self.send_sem.at[len(self.started)], recv, peer
        ).start()
        self.started.append(half)

    def relay(self, owner, half, recv, peer):
        self.push(self.place(owner, half), owner, half, recv, peer)

    def hear(self, owner, half, sem):
        spot = self.place(owner, half)
        remote(spot, spot, self.send_sem.at[0], sem, self.partner).wait_recv()

    def begin(self):
        self.own = pltpu.make_async_copy(self.block, self.place(self.me), self.own_sem)
        self.own.start()
        recv, land = self.recv_sem, self.land_sem
        for half in range(2):
            size = self.extent // 2
            span = pl.ds(half * size, size)
            part = self.block.at[span, :] if self.axis == 0 else self.block.at[:, span]
            self.push(part, self.me, half, recv.at[2 + half], self.over)
        self.push(self.block, self.me, None, recv.at[0], self.right)
        self.push(self.block, self.me, None, recv.at[1], self.left)
        self.push(self.block, self.me, None, land.at[12], self.partner)

    def arrive(self, number, dx, dy, half, onward):
        owner = self.at(dx, dy)
        self.hear(owner, half, self.recv_sem.at[number])
        for part, target, peer in onward:
            self.relay(owner, part, self.recv_sem.at[target], peer)
        self.relay(owner, half, self.land_sem.at[number], self.partner)

    def beside(self):
        self.arrive(0, -1, 0, None, [(0, 8, self.right)])
        self.arrive(1, 1, 0, None, [(1, 9, self.left)])

    def across(self, half):
        self.arrive(
            2 + half, 0, 1, half, [(half, 4 + half, self.right), (half, 6 + half, self.left)]
        )

    def opposite(self):
        self.arrive(8, 2, 0, 0, [])
        self.arrive(9, 2, 0, 1, [])

    def beside_across(self, half):
        self.arrive(4 + half, -1, 1, half, [(0, 10, self.right)] if half == 0 else [])
        self.arrive(6 + half, 1, 1, half, [(1, 11, self.left)] if half == 1 else [])

    def opposite_across(self):
        self.arrive(10, 2, 1, 0, [])
        self.arrive(11, 2, 1, 1, [])

    def crossed(self):
        self.across(0)
        self.across(1)

    def crossed_beside(self):
        self.beside_across(0)
        self.beside_across(1)

    def handed(self, number, dx, dy, half):
        other = self.at(dx, dy) + 1 - 2 * self.core
        self.hear(other, half, self.land_sem.at[number])

    def finish(self):
        for number, half in enumerate(self.started):
            spot = self.place(self.me, half)
            remote(
                spot, spot, self.send_sem.at[number], self.recv_sem.at[0], self.partner
            ).wait_send()

    def neighbours(self):
        return [self.right, self.left, self.over, self.partner]


def exchange_sems():
    sems = pltpu.SemaphoreType.DMA
    return [sems((SENDS,)), sems((ARRIVALS,)), sems((ARRIVALS,)), sems]


def make_tables(idx_ref, wts_ref, col_ref, row_ref, first, prep_width, side, tokens):
    plane_size = side * side

    def prepare(step, carry):
        start = pl.multiple_of(step * prep_width, prep_width)
        span = pl.ds(start, prep_width)
        index = idx_ref[:, span]
        weight = wts_ref[:, span].astype(f32)
        column_id = lax.broadcasted_iota(jnp.int32, (side, prep_width), 0)
        for plane in range(PLANES):
            in_plane = (index >= plane * plane_size) & (index < (plane + 1) * plane_size)
            base = jnp.min(jnp.where(in_plane, index, tokens), axis=0, keepdims=True)
            corner = []
            for offset in (0, 1, side, side + 1):
                corner.append(
                    jnp.sum(
                        jnp.where(index == base + offset, weight, 0.0), axis=0, keepdims=True
                    )
                )
            local = base - plane * plane_size
            cell_row = local // side
            column = local - cell_row * side
            for which in range(2):
                col_ref[2 * plane + which, :, span] = jnp.where(
                    column_id == column,
                    corner[2 * which],
                    jnp.where(column_id == column + 1, corner[2 * which + 1], 0.0),
                ).astype(bf16)
            row_ref[plane, :, span] = jnp.broadcast_to(
                cell_row.astype(f32), (16, prep_width)
            ).astype(bf16)
        return carry

    lax.fori_loop(first, first + 1, prepare, 0)


def front_kernel(
    tokens_hbm,
    image_hbm,
    w_query_hbm,
    w_key_hbm,
    w_value_hbm,
    idx_ref,
    wts_ref,
    q_ref,
    k_ref,
    v_ref,
    col_ref,
    row_ref,
    tokens_ref,
    image_ref,
    images_ref,
    w_query_ref,
    w_key_ref,
    w_value_ref,
    load_sem,
    *sems,
    tile,
    scale,
    side,
    prep_width,
):
    ring = Exchange(image_ref, images_ref, 0, sems)
    loads = []
    for number, (source, target) in enumerate(
        (
            (image_hbm, image_ref),
            (tokens_hbm, tokens_ref),
            (w_query_hbm, w_query_ref),
            (w_key_hbm, w_key_ref),
            (w_value_hbm, w_value_ref),
        )
    ):
        copy = pltpu.make_async_copy(source, target, load_sem.at[number])
        copy.start()
        loads.append(copy)
    greet(ring.neighbours())
    loads[0].wait()
    ring.begin()

    all_tokens = PLANES * side * side

    def tables(first, last):
        for part in range(first, last):
            make_tables(idx_ref, wts_ref, col_ref, row_ref, part, prep_width, side, all_tokens)

    def query(step):
        span = pl.ds(step * tile, tile)
        normed = plain_norm(tokens_ref[span, :].astype(f32)).astype(bf16)
        product = jnp.dot(normed, w_query_ref[...], preferred_element_type=f32)
        q_ref[span, :] = (product * scale).astype(bf16)

    def keys_values(dx, dy):
        owner = ring.at(dx, dy) // 2
        rows = 2 * image_ref.shape[0]
        span = pl.ds(pl.multiple_of(owner * rows, rows), rows)
        images = images_ref[span, :]
        k_ref[span, :] = jnp.dot(
            images, w_key_ref[...], preferred_element_type=f32
        ).astype(bf16)
        v_ref[span, :] = jnp.dot(
            images, w_value_ref[...], preferred_element_type=f32
        ).astype(bf16)

    loads[1].wait()
    loads[2].wait()
    query(0)
    query(1)
    ring.beside()
    ring.across(0)
    query(2)
    ring.across(1)
    loads[3].wait()
    loads[4].wait()
    ring.own.wait()
    ring.handed(12, 0, 0, None)
    keys_values(0, 0)
    ring.handed(0, -1, 0, None)
    keys_values(-1, 0)
    tables(0, 1)
    ring.opposite()
    ring.beside_across(0)
    ring.handed(1, 1, 0, None)
    keys_values(1, 0)
    ring.handed(2, 0, 1, 0)
    ring.handed(3, 0, 1, 1)
    keys_values(0, 1)
    tables(1, 2)
    ring.beside_across(1)
    ring.handed(8, 2, 0, 0)
    ring.handed(9, 2, 0, 1)
    keys_values(2, 0)
    ring.handed(4, -1, 1, 0)
    ring.handed(5, -1, 1, 1)
    keys_values(-1, 1)
    ring.handed(6, 1, 1, 0)
    ring.handed(7, 1, 1, 1)
    keys_values(1, 1)
    tables(2, 4)
    ring.opposite_across()
    ring.handed(10, 2, 1, 0)
    ring.handed(11, 2, 1, 1)
    keys_values(2, 1)
    ring.finish()


def front(tokens, images, w_query, w_key, w_value, index, weight, size, scale, collective_id):
    rows, width = tokens.shape
    depth = images.shape[1]
    count = images.shape[0] * size
    heads = w_key.shape[1]
    samples = index.shape[1]
    side = math.isqrt(rows * size // PLANES)
    return pl.pallas_call(
        functools.partial(
            front_kernel,
            tile=rows // 3,
            scale=scale,
            side=side,
            prep_width=index.shape[1] // 4,
        ),
        out_shape=(
            jax.ShapeDtypeStruct((rows, width), bf16),
            jax.ShapeDtypeStruct((count, heads), bf16),
            jax.ShapeDtypeStruct((count, heads), bf16),
            jax.ShapeDtypeStruct((2 * PLANES, side, samples), bf16),
            jax.ShapeDtypeStruct((PLANES, 16, samples), bf16),
        ),
        in_specs=[pl.BlockSpec(memory_space=pltpu.HBM)] * 5 + in_vmem(2),
        out_specs=tuple(in_vmem(5)),
        scratch_shapes=[
            pltpu.VMEM(tokens.shape, bf16),
            pltpu.VMEM(images.shape, bf16),
            pltpu.VMEM((count, depth), bf16),
            pltpu.VMEM(w_query.shape, bf16),
            pltpu.VMEM(w_key.shape, bf16),
            pltpu.VMEM(w_value.shape, bf16),
            pltpu.SemaphoreType.DMA((5,)),
            *exchange_sems(),
        ],
        compiler_params=pltpu.CompilerParams(
            collective_id=collective_id,
            has_side_effects=True,
            vmem_limit_bytes=24 * 1024 * 1024,
        ),
        name="front",
    )(
        *(
            pltpu.with_memory_space_constraint(array, pltpu.HBM)
            for array in (tokens, images, w_query, w_key, w_value)
        ),
        index,
        weight,
    )


def table_rows(col_ref, row_ref, plane, first_row, row_count, start, width, side):
    span = pl.ds(start, width)
    pieces = side // 16
    upper = col_ref[2 * plane, :, span].reshape(pieces, 16, width)
    lower = col_ref[2 * plane + 1, :, span].reshape(pieces, 16, width)
    cell_row = row_ref[plane, :, span]
    zero = jnp.zeros((16, width), bf16)
    row_id = jnp.asarray(first_row, jnp.int32)
    before = cell_row == (row_id - 1).astype(bf16)
    blocks = []
    for step in range(row_count):
        here = cell_row == (row_id + step).astype(bf16)
        for piece in range(pieces):
            blocks.append(
                jnp.where(here, upper[piece], jnp.where(before, lower[piece], zero))
            )
        before = here
    return jnp.concatenate(blocks, axis=0)


def ray_scan(values, lane, reverse):
    width = values.shape[1]
    shift = 1
    while shift < STEPS:
        if reverse:
            moved = pltpu.roll(values, width - shift, 1)
            values = values + jnp.where(lane < STEPS - shift, moved, 0.0)
        else:
            moved = pltpu.roll(values, shift, 1)
            values = values + jnp.where(lane >= shift, moved, 0.0)
        shift *= 2
    return values


def parts_of(values):
    first = values.astype(bf16)
    rest = values - first.astype(f32)
    second = rest.astype(bf16)
    third = (rest - second.astype(f32)).astype(bf16)
    return jnp.concatenate([first, second, third], axis=0)


def join(product):
    count = product.shape[0] // 3
    return product[:count] + product[count : 2 * count] + product[2 * count :]


def column_of(row_ref):
    count = row_ref.shape[1]
    diagonal = lax.broadcasted_iota(jnp.int32, (count, count), 0) == lax.broadcasted_iota(
        jnp.int32, (count, count), 1
    )
    return jnp.sum(jnp.where(diagonal, row_ref[...], 0.0), axis=1, keepdims=True)


def token_rows(col_ref, row_ref, chip, start, width, side, grid_rows):
    blocks = []
    for group in range(grid_rows // 4):
        number = chip * (grid_rows // 4) + group
        plane = number // (side // 4)
        first = (number - plane * (side // 4)) * 4
        blocks.append(table_rows(col_ref, row_ref, plane, first, 4, start, width, side))
    return jnp.concatenate(blocks, axis=0)


def scene_kernel(
    block_ref,
    plane_in_ref,
    col_ref,
    row_ref,
    target_ref,
    w_plane_ref,
    w1_ref,
    b1_ref,
    w2_ref,
    b2_ref,
    w3_ref,
    b3_ref,
    colors_ref,
    token_grad_ref,
    total_ref,
    planes_ref,
    features_ref,
    fgrad_ref,
    z1_ref,
    z2_ref,
    decoded_ref,
    give_ref,
    keep_ref,
    pair_ref,
    stage_ref,
    half_ref,
    side_ref,
    over_ref,
    part_ref,
    chunk_land_ref,
    chunk_ref,
    scene_ref,
    last_ref,
    pair_send,
    pair_recv,
    half_send,
    half_recv,
    side_send,
    side_recv,
    over_send,
    over_recv,
    chunk_send,
    chunk_recv,
    scene_send,
    scene_recv,
    last_send,
    last_recv,
    *ring_sems,
    side,
    size,
    scenes,
    prep_width,
    width,
    tile,
):
    samples = row_ref.shape[2]
    channels, tokens = planes_ref.shape
    extent = block_ref.shape[1]
    half_extent = extent // 2
    plane_size = side * side
    chip_tokens = 2 * extent
    grid_rows = chip_tokens // side
    chips = size // 2
    turned = (((1,), (1,)), ((), ()))
    flip = (((0,), (0,)), ((), ()))

    ring = Exchange(block_ref, planes_ref, 1, ring_sems)
    me, core = ring.me, ring.core
    scene = lax.axis_index("dp")
    others = [(me + step) % size for step in range(1, size)]
    other_scenes = [(scene + step) % scenes for step in range(1, scenes)]
    greet([{"seq": owner} for owner in others] + [{"dp": owner} for owner in other_scenes])
    ring.begin()

    def chip_at(dx, dy):
        return 2 * ((ring.x + dx) % RING) + (ring.y + dy) % 2

    w1, w2, w3 = w1_ref[...], w2_ref[...], w3_ref[...]
    b1, b2, b3 = column_of(b1_ref), column_of(b2_ref), column_of(b3_ref)
    features_ref[...] = jnp.zeros_like(features_ref)

    arrivals = (
        ((), ((12, 0, 0, None),)),
        ((ring.beside, ring.crossed), ((1, 1, 0, None),)),
        ((), ((0, -1, 0, None),)),
        ((ring.opposite, ring.crossed_beside), ((8, 2, 0, 0), (9, 2, 0, 1))),
        ((), ((2, 0, 1, 0), (3, 0, 1, 1))),
        ((ring.opposite_across,), ((6, 1, 1, 0), (7, 1, 1, 1))),
        ((), ((4, -1, 1, 0), (5, -1, 1, 1))),
        ((), ((10, 2, 1, 0), (11, 2, 1, 1))),
    )

    def interpolate(step, carry):
        for number, (receive, handed) in enumerate(arrivals):

            @pl.when(step == number)
            def _(number=number, receive=receive, handed=handed):
                for take in receive:
                    take()
                if number == 0:
                    ring.own.wait()
                for item in handed:
                    ring.handed(*item)

        place = step % 4
        chip = chip_at(place + place // 2 - 2 * (place // 3), step // 4)
        block = pl.ds(pl.multiple_of(chip * chip_tokens, chip_tokens), chip_tokens)

        def add(part, inner):
            start = pl.multiple_of(part * width, width)
            span = pl.ds(start, width)
            table = token_rows(col_ref, row_ref, chip, start, width, side, grid_rows)
            features_ref[:, span] = features_ref[:, span] + jnp.dot(
                planes_ref[:, block], table, preferred_element_type=f32
            )
            return inner

        lax.fori_loop(0, samples // width, add, 0)
        return carry

    lax.fori_loop(0, chips, interpolate, 0)

    def decode(step, carry):
        span = pl.ds(pl.multiple_of(step * prep_width, prep_width), prep_width)
        z1 = jnp.dot(w1, features_ref[:, span].astype(bf16), preferred_element_type=f32) + b1
        z1_ref[:, span] = z1
        h1 = (z1 * jax.nn.sigmoid(z1)).astype(bf16)
        z2 = jnp.dot(w2, h1, preferred_element_type=f32) + b2
        z2_ref[:, span] = z2
        h2 = (z2 * jax.nn.sigmoid(z2)).astype(bf16)
        decoded_ref[:, span] = jnp.dot(w3, h2, preferred_element_type=f32) + b3
        return carry

    lax.fori_loop(0, samples // prep_width, decode, 0)

    rays = samples // STEPS
    lane = lax.broadcasted_iota(jnp.int32, (1, samples), 1) % STEPS
    density = decoded_ref[0:1]
    optical = (jnp.maximum(density, 0.0) + jnp.log1p(jnp.exp(-jnp.abs(density)))) * DEPTH_STEP
    albedo = jax.nn.sigmoid(decoded_ref[1:4])
    reach = jnp.exp(optical - ray_scan(optical, lane, False))
    passed = jnp.exp(-optical)
    weight = reach * (1.0 - passed)
    spread = (
        lax.broadcasted_iota(jnp.int32, (rays, samples), 0)
        == lax.broadcasted_iota(jnp.int32, (rays, samples), 1) // STEPS
    ).astype(bf16)
    colors = join(
        lax.dot_general(
            parts_of(weight * albedo), spread, turned, preferred_element_type=f32
        )
    )
    colors_ref[...] = colors
    miss = join(
        jnp.dot(parts_of(colors - target_ref[...]), spread, preferred_element_type=f32)
    )
    weight_grad = jnp.sum(miss * albedo, axis=0, keepdims=True)
    term = weight_grad * weight
    later = ray_scan(term, lane, True) - term
    optical_grad = weight_grad * reach * passed - later
    decoded_ref[0:1] = optical_grad * (DEPTH_STEP * jax.nn.sigmoid(density))
    decoded_ref[1:4] = miss * weight * albedo * (1.0 - albedo)

    def silu_grad(pre):
        gate = jax.nn.sigmoid(pre)
        return gate * (1.0 + pre * (1.0 - gate))

    def decode_back(step, carry):
        span = pl.ds(pl.multiple_of(step * prep_width, prep_width), prep_width)
        g2 = lax.dot_general(
            w3, decoded_ref[:, span].astype(bf16), flip, preferred_element_type=f32
        )
        g2 = g2.astype(bf16).astype(f32) * silu_grad(z2_ref[:, span])
        g1 = lax.dot_general(w2, g2.astype(bf16), flip, preferred_element_type=f32)
        g1 = g1.astype(bf16).astype(f32) * silu_grad(z1_ref[:, span])
        fgrad_ref[:, span] = lax.dot_general(
            w1, g1.astype(bf16), flip, preferred_element_type=f32
        ).astype(bf16)
        return carry

    lax.fori_loop(0, samples // prep_width, decode_back, 0)

    def swap(number):
        return remote(
            give_ref.at[number],
            pair_ref.at[number],
            pair_send.at[number],
            pair_recv.at[number],
            ring.partner,
        )

    def push_half(way, row, number):
        part = pl.ds(way * half_extent, half_extent)
        return remote(
            stage_ref.at[number, :, part],
            half_ref.at[way, row],
            half_send.at[way, row],
            half_recv.at[way, row],
            ring.right if way == 0 else ring.left,
        )

    def push_side(way, row, number):
        return remote(
            stage_ref.at[number],
            side_ref.at[way, row],
            side_send.at[way, row],
            side_recv.at[way, row],
            ring.right if way == 0 else ring.left,
        )

    def push_over(number):
        return remote(stage_ref.at[number], over_ref, over_send, over_recv, ring.over)

    def stage(number):
        swap(number).wait_recv()
        row = 1 - number // 4
        kind = number % 4
        both = keep_ref[...] + pair_ref[number].astype(f32)
        if kind == 0:
            stage_ref[number] = both.astype(bf16)
            push_half(0, row, number).start()
            push_half(1, row, number).start()
        elif kind < 3:
            way = kind - 1
            push_half(way, row, number).wait_recv()
            part = pl.ds(way * half_extent, half_extent)
            stage_ref[number] = both.astype(bf16)
            first = way * half_extent
            stage_ref[number, :, part] = (
                both[:, first : first + half_extent] + half_ref[way, row].astype(f32)
            ).astype(bf16)
            push_side(way, row, number).start()
        else:
            for way in range(2):
                push_side(way, row, number).wait_recv()
                both = both + side_ref[way, row].astype(f32)
            if row == 1:
                stage_ref[number] = both.astype(bf16)
                push_over(number).start()
        return both

    def spread_back(step, carry):
        place = step % 4
        across = 2 + 3 * place + 3 * (place // 2) + 2 * (place // 3)
        chip = chip_at(across, 1 - step // 4)

        def product(owner):
            table = token_rows(col_ref, row_ref, owner, 0, samples, side, extent // side)
            return lax.dot_general(fgrad_ref[...], table, turned, preferred_element_type=f32)

        give_ref[step] = product(2 * chip + 1 - core).astype(bf16)
        swap(step).start()
        keep_ref[...] = product(2 * chip + core)
        for number in range(chips - 1):

            @pl.when(step == number)
            def _(number=number):
                stage(number)

        return carry

    lax.fori_loop(0, chips, spread_back, 0)
    both = stage(chips - 1)
    push_over(3).wait_recv()
    own_grad = (both + over_ref[...].astype(f32)).astype(bf16)

    rows, lanes = chunk_ref.shape

    def chunk_of(owner):
        return (
            pl.ds(pl.multiple_of((owner % 2) * rows, rows), rows),
            pl.ds(pl.multiple_of((owner // 2) * lanes, lanes), lanes),
        )

    part_ref[0:channels] = jnp.dot(
        own_grad, plane_in_ref[...], preferred_element_type=f32
    ).astype(bf16)
    part_ref[channels:] = jnp.zeros((2 * rows - channels, part_ref.shape[1]), bf16)
    waiting = []
    for owner in others:
        copy = remote(
            part_ref.at[chunk_of(owner)],
            chunk_land_ref.at[me],
            chunk_send.at[owner],
            chunk_recv.at[me],
            {"seq": owner},
        )
        copy.start()
        waiting.append(copy)
    for first in range(0, extent, tile):
        token_grad_ref[first : first + tile, :] = lax.dot_general(
            own_grad[:, first : first + tile],
            w_plane_ref[...],
            flip,
            preferred_element_type=f32,
        ).astype(bf16)
    chunk = part_ref[chunk_of(me)].astype(f32)
    for owner in others:
        remote(
            last_ref.at[chunk_of(me)],
            chunk_land_ref.at[owner],
            chunk_send.at[owner],
            chunk_recv.at[owner],
            ring.partner,
        ).wait_recv()
        chunk = chunk + chunk_land_ref[owner].astype(f32)
    chunk_ref[...] = chunk
    scene_ref[scene] = chunk
    for other in other_scenes:
        copy = remote(
            chunk_ref,
            scene_ref.at[scene],
            scene_send.at[other],
            scene_recv.at[scene],
            {"dp": other},
        )
        copy.start()
        waiting.append(copy)
    for other in other_scenes:
        remote(
            chunk_ref,
            scene_ref.at[other],
            scene_send.at[other],
            scene_recv.at[other],
            ring.partner,
        ).wait_recv()
    final = scene_ref[0]
    for other in range(1, scenes):
        final = final + scene_ref[other]
    spot = chunk_of(me)
    last_ref[spot] = final.astype(bf16)
    for owner in others:
        copy = remote(
            last_ref.at[spot],
            last_ref.at[spot],
            last_send.at[owner],
            last_recv.at[me],
            {"seq": owner},
        )
        copy.start()
        waiting.append(copy)
    for owner in others:
        there = chunk_of(owner)
        remote(
            last_ref.at[there],
            last_ref.at[there],
            last_send.at[owner],
            last_recv.at[owner],
            ring.partner,
        ).wait_recv()
    total_ref[...] = last_ref[0:channels].astype(f32)
    for copy in waiting:
        copy.wait_send()
    for number in range(chips):
        swap(number).wait_send()
    for row in range(2):
        base = 4 * (1 - row)
        for way in range(2):
            push_half(way, row, base).wait_send()
            push_side(way, row, base + 1 + way).wait_send()
    push_over(3).wait_send()
    ring.finish()


def render_scene(
    block,
    plane_in,
    columns,
    cell_rows,
    target,
    w_plane,
    w1,
    b1,
    w2,
    b2,
    w3,
    b3,
    size,
    scenes,
    collective_id,
):
    channels, extent = block.shape
    width = plane_in.shape[1]
    samples = cell_rows.shape[2]
    tokens = extent * size
    side = math.isqrt(tokens // PLANES)
    chips = size // 2
    rows, lanes = -(-channels // 32) * 16, width // chips
    sems = pltpu.SemaphoreType.DMA
    return pl.pallas_call(
        functools.partial(
            scene_kernel,
            side=side,
            size=size,
            scenes=scenes,
            prep_width=1024,
            width=2048,
            tile=256,
        ),
        out_shape=(
            jax.ShapeDtypeStruct(target.shape, f32),
            jax.ShapeDtypeStruct((extent, width), bf16),
            jax.ShapeDtypeStruct((channels, width), f32),
        ),
        in_specs=in_vmem(12),
        out_specs=tuple(in_vmem(3)),
        scratch_shapes=[
            pltpu.VMEM((channels, tokens), bf16),
            pltpu.VMEM((channels, samples), f32),
            pltpu.VMEM((channels, samples), bf16),
            pltpu.VMEM((w1.shape[0], samples), f32),
            pltpu.VMEM((w2.shape[0], samples), f32),
            pltpu.VMEM((w3.shape[0], samples), f32),
            pltpu.VMEM((chips, channels, extent), bf16),
            pltpu.VMEM((channels, extent), f32),
            pltpu.VMEM((chips, channels, extent), bf16),
            pltpu.VMEM((chips, channels, extent), bf16),
            pltpu.VMEM((2, 2, channels, extent // 2), bf16),
            pltpu.VMEM((2, 2, channels, extent), bf16),
            pltpu.VMEM((channels, extent), bf16),
            pltpu.VMEM((2 * rows, width), bf16),
            pltpu.VMEM((size, rows, lanes), bf16),
            pltpu.VMEM((rows, lanes), f32),
            pltpu.VMEM((scenes, rows, lanes), f32),
            pltpu.VMEM((2 * rows, width), bf16),
            sems((chips,)),
            sems((chips,)),
            sems((2, 2)),
            sems((2, 2)),
            sems((2, 2)),
            sems((2, 2)),
            sems,
            sems,
            sems((size,)),
            sems((size,)),
            sems((scenes,)),
            sems((scenes,)),
            sems((size,)),
            sems((size,)),
            *exchange_sems(),
        ],
        compiler_params=pltpu.CompilerParams(
            collective_id=collective_id,
            has_side_effects=True,
            vmem_limit_bytes=40 * 1024 * 1024,
        ),
        name="scene",
    )(
        block,
        plane_in,
        columns,
        cell_rows,
        target,
        w_plane.T,
        w1,
        b1[None, :],
        w2,
        b2[None, :],
        w3,
        b3[None, :],
    )


def body(
    tokens,
    image_tokens,
    norm_gain,
    w_query,
    w_key,
    w_value,
    w_out,
    w_plane,
    dec_w1,
    dec_b1,
    dec_w2,
    dec_b2,
    dec_w3,
    dec_b3,
    corner_idx,
    corner_wts,
    target_color,
):
    own_tokens = tokens[0]
    model_width = own_tokens.shape[1]
    head_dim = model_width // HEADS
    size = lax.axis_size("seq")
    score_scale = math.log2(math.e) / math.sqrt(head_dim)
    queries, keys, values, columns, cell_rows = front(
        own_tokens,
        image_tokens[0],
        w_query,
        w_key,
        w_value,
        corner_idx[0],
        corner_wts[0],
        size,
        score_scale,
        0,
    )
    plane_in, planes = attention(
        queries, keys, values, own_tokens, w_out, norm_gain, w_plane
    )
    colors, token_grad, weight_grad = render_scene(
        planes,
        plane_in,
        columns,
        cell_rows,
        target_color[0],
        w_plane,
        dec_w1,
        dec_b1,
        dec_w2,
        dec_b2,
        dec_w3,
        dec_b3,
        size,
        lax.axis_size("dp"),
        1,
    )
    return (colors[None], token_grad[None], weight_grad.T)


def solution(mesh):
    in_specs = (
        P("dp", "seq", None),
        P("dp", "seq", None),
        *(P() for _ in range(12)),
        P("dp", None, "seq"),
        P("dp", None, "seq"),
        P("dp", None, "seq"),
    )
    out_specs = (P("dp", None, "seq"), P("dp", "seq", None), P())
    return jax.shard_map(body, mesh=mesh, in_specs=in_specs, out_specs=out_specs, check_vma=False)
```
